32 devices in a mesh: gx: 4 (over x, core), gy: 4 (over z), gz: 2 (over y).
Axes of the slice: x: 2, y: 2, z: 4, core: 2. Of those that a mesh axis runs over, the one named last changes fastest.
Arguments:
- wave: float32 [64, 128, 256], P('gx', 'gy', 'gz'), may hold values from -7 to 7
- external: float32 [64, 128, 256], P('gx', 'gy', 'gz'), may hold values from 0 to 2
- weights: float32 [3, 17], replicated, may hold values from 0.02 to 0.1
Outputs:
- wave_next: float32 [64, 128, 256], P('gx', 'gy', 'gz')
- correlation: float32 [64, 128, 256], P('gx', 'gy', 'gz')
The draws below stay inside these ranges and needn't reach their ends.
All inputs are finite; a program needn't handle non-finite values.
Results may differ from the reference program's by a relative error of at most 0.00029.
Values sent between devices are 32-bit elements; how exact they have to be, the bound alone decides.
A program may use at most 64 MiB of HBM per device.

```python
import math
import jax
import jax.numpy as jnp
from jax import lax

CX = 16
CY = 32
CZ = 128
SUBSTEPS = 3
NX = 64
NY = 128
NZ = 256


def tile_levels(key, low, high):
    level_key, shift_key = jax.random.split(key)
    counts = (NX // CX, NY // CY, NZ // CZ)
    logs = jax.random.uniform(level_key, counts, jnp.float32, jnp.log(low), jnp.log(high))
    levels = jnp.exp(logs)
    levels = jnp.repeat(levels, CX, axis=0)
    levels = jnp.repeat(levels, CY, axis=1)
    levels = jnp.repeat(levels, CZ, axis=2)
    shifts = jax.random.randint(shift_key, (3,), 0, 4)
    levels = jnp.roll(levels, shifts[0], axis=0)
    levels = jnp.roll(levels, shifts[1], axis=1)
    levels = jnp.roll(levels, shifts[2], axis=2)
    return levels


def draw_wave(key, part):
    first = jax.random.fold_in(key, 0)
    rise = 1.0 + 0.732 * jnp.arange(NX, dtype=jnp.float32) / max(NX - 1, 1)
    amplitude = tile_levels(jax.random.fold_in(key, 11), 0.45, 1.1)
    rough = jnp.clip(jax.random.normal(first, (NX, NY, NZ), jnp.float32), -4.0, 4.0)
    values = rough * rise[:, None, None] * amplitude
    return jnp.clip(values, -7.0, 7.0).astype(jnp.float32)


def draw_external(key, part):
    first, second = jax.random.split(jax.random.fold_in(key, 23))
    levels = tile_levels(first, 0.15, 1.0)
    rough = jnp.exp(jax.random.uniform(second, (NX, NY, NZ), jnp.float32, jnp.log(0.5), jnp.log(2.0)))
    return jnp.clip(levels * rough, 0.0, 2.0).astype(jnp.float32)


def setup_inputs(seed: int = 0) -> dict:
    key_of = jax.random.split(jax.random.key(seed), 4)
    return {
        "wave": draw_wave(jax.random.fold_in(key_of[3], 71), 0),
        "external": draw_external(jax.random.fold_in(key_of[3], 71), 0),
        "weights": jnp.clip(jnp.exp(jax.random.uniform(key_of[2], (3, 17), jnp.float32, math.log(0.02), math.log(0.1))), 0.02, 0.1),
    }


LAP_COEF = (-205.0 / 72.0, 8.0 / 5.0, -1.0 / 5.0, 8.0 / 315.0, -1.0 / 560.0)

def smear(field, weights, flip):
    for dim in range(3):
        length = field.shape[dim]
        widths = [(0, 0), (0, 0), (0, 0)]
        widths[dim] = (8, 8)
        padded = jnp.pad(field, widths)
        total = jnp.zeros_like(field)
        for tap in range(17):
            coef = weights[dim, 16 - tap] if flip else weights[dim, tap]
            total = total + coef * lax.slice_in_dim(padded, tap, tap + length, axis=dim)
        field = total
    return field

def laplace(field):
    padded = jnp.pad(field, 4)
    total = 3.0 * LAP_COEF[0] * field
    for dim in range(3):
        length = field.shape[dim]
        inner = [slice(4, -4), slice(4, -4), slice(4, -4)]
        for step in range(1, 5):
            upper = list(inner)
            lower = list(inner)
            upper[dim] = slice(4 + step, 4 + step + length)
            lower[dim] = slice(4 - step, 4 - step + length)
            total = total + LAP_COEF[step] * (padded[tuple(upper)] + padded[tuple(lower)])
    return total

def reference(wave, external, weights):
    density = wave * wave
    coarse = smear(density, weights, False)
    source = -1.0 * density * coarse + 0.5 * density * coarse * coarse
    correlation = -0.5 * coarse * coarse + 0.5 / 3.0 * coarse * coarse * coarse + smear(source, weights, True)
    potential = correlation + external
    psi = wave
    for step in range(SUBSTEPS):
        psi = psi - 0.08 * (-0.5 * laplace(psi) + potential * psi)
    total = jnp.sum(psi * psi)
    wave_next = psi * lax.rsqrt(total / (NX * NY * NZ) + 1e-06)
    return (wave_next, correlation)
```

```python
import functools

import jax
import jax.numpy as jnp
from jax import lax
from jax.experimental import pallas as pl
from jax.experimental.pallas import tpu as pltpu
from jax.sharding import PartitionSpec as P

SUBSTEPS = 3
LAP_COEF = (-205.0 / 72.0, 8.0 / 5.0, -1.0 / 5.0, 8.0 / 315.0, -1.0 / 560.0)
STEP = 0.08
AXES = ("gx", "gy", "gz")
MESH = pl.DeviceIdType.MESH
R = 8
H = 4


def lanes(shape):
    return lax.broadcasted_iota(jnp.int32, shape, len(shape) - 1)


def lane_taps(mid, low, high, step, taps):
    at = lanes(mid.shape)
    width = mid.shape[-1]
    total = None
    for k, tap in taps:
        if k == 0:
            part = mid
        elif k > 0:
            s = k * step
            part = pltpu.roll(jnp.where(at < s, high, mid), width - s, mid.ndim - 1)
        else:
            s = -k * step
            part = pltpu.roll(jnp.where(at >= width - s, low, mid), s, mid.ndim - 1)
        part = part * tap
        total = part if total is None else total + part
    return total


FACES = [(1, 0, 0), (-1, 0, 0), (0, 1, 0), (0, -1, 0), (0, 0, 1), (0, 0, -1)]
UNROLL = {"stage": 16, "source": 16, "corr": 16}
ZW = 4


def loop(name, n, body, init):
    width = min(UNROLL[name], n)
    if n % width:
        width = 1
    if width == n:
        for i in range(n):
            init = body(i, init)
        return init

    def step(j, carry):
        for k in range(width):
            carry = body(j * width + k, carry)
        return carry

    return lax.fori_loop(0, n // width, step, init)


def turn(value, shift):
    return value if isinstance(shift, int) and shift == 0 else pltpu.roll(value, shift, 1)


def modulo(a, n):
    return a % n if isinstance(a, int) else lax.rem(a, n)


def kernel(sizes, w_hbm, wave_hbm, ext_hbm, out_ref, corr_ref, scale_ref,
           wb, sb, yb, psi, va, pack, zin, ypack, yin, bands, ext_ref, w_ref, sums, sums2,
           send, recv, send2, recv2, local, known):
    nx, ny, nz = sizes
    cx, cy, cz = wave_hbm.shape
    wave_ref = wb.at[pl.ds(R, cx), pl.ds(R, cy)]
    get_wave = pltpu.make_async_copy(wave_hbm, wave_ref, local.at[0])
    get_ext = pltpu.make_async_copy(ext_hbm, ext_ref, local.at[1])
    get_weights = pltpu.make_async_copy(w_hbm, w_ref, local.at[2])
    get_wave.start()
    get_weights.start()
    ix, iy, iz = (lax.axis_index(a) for a in AXES)
    plane = nx * nz
    per = cz // cx
    here = ix * nz + iz

    def plane_id(d):
        t = lax.rem(here + d, plane)
        return t, {"gx": lax.div(t, nz), "gz": lax.rem(t, nz)}

    def line_id(d):
        t = lax.rem(iy + d, ny)
        return t, {"gy": t}

    barrier = pltpu.get_barrier_semaphore()

    def greet(ids):
        def body(d, c):
            pl.semaphore_signal(barrier, inc=1, device_id=ids(d)[1], device_id_type=MESH)
            return c
        return body

    near = nx <= 4 and ny <= 4 and nz <= 2

    def greet_faces(sem):
        count = 0
        for d3 in FACES:
            for name, d, i, n in zip(AXES, d3, (ix, iy, iz), sizes):
                if d:
                    there = i < n - 1 if d > 0 else i > 0
                    target = {name: jnp.clip(i + d, 0, n - 1)}
            count += there.astype(jnp.int32)

            @pl.when(there)
            def _(target=target):
                pl.semaphore_signal(sem, inc=1, device_id=target, device_id_type=MESH)
        return count

    if near:
        guests = greet_faces(barrier)
    else:
        guests = plane - 1 + ny - 1
        lax.fori_loop(1, plane, greet(plane_id), 0)
        lax.fori_loop(1, ny, greet(line_id), 0)

    counter = [0]

    def message(src, dst, dx, dy, dz):
        k = counter[0]
        counter[0] += 1
        to, back = None, None
        for d, i, n in ((dx, ix, nx), (dy, iy, ny), (dz, iz, nz)):
            if d > 0:
                a, b = i < n - 1, i > 0
            elif d < 0:
                a, b = i > 0, i < n - 1
            else:
                continue
            to = a if to is None else to & a
            back = b if back is None else back & b
        target = {}
        for name, d, i, n in zip(AXES, (dx, dy, dz), (ix, iy, iz), sizes):
            if d:
                target[name] = jnp.clip(i + d, 0, n - 1)
        copy = pltpu.make_async_remote_copy(
            src_ref=src, dst_ref=dst, send_sem=send.at[k], recv_sem=recv.at[k],
            device_id=target, device_id_type=MESH)
        return copy, to, back, dst

    sent = []

    def start(messages):
        for copy, to, _, _ in messages:
            pl.when(to)(copy.start)
            sent.append((copy, to))

    def blank(messages):
        for _, _, back, dst in messages:
            @pl.when(jnp.logical_not(back))
            def _(dst=dst):
                dst[...] = jnp.zeros(dst.shape, dst.dtype)

    def arrive(messages):
        for copy, _, back, _ in messages:
            pl.when(back)(copy.wait_recv)

    at = lanes((cy, cz))
    zero = jnp.zeros((cy, cz), jnp.float32)

    def pack_one(i, value, packs):
        mine = (at >= per * i) & (at < per * i + per)
        low = turn(value, per * i)
        high = turn(value, modulo(per * i + per, cz))
        return jnp.where(mine, low, packs[0]), jnp.where(mine, high, packs[1])

    def unpack(i, from_low, from_high):
        a = turn(from_high, modulo(cz - per * i, cz))
        b = turn(from_low, cz - per - per * i)
        return jnp.where(lanes(a.shape) < per, a, b)

    def pack_out(slot, packs):
        pack[slot, 0] = packs[0]
        pack[slot, 1] = packs[1]

    def z_messages(slot, dxs, dys):
        out = []
        for dx in dxs:
            for dy in dys:
                if dy > 0:
                    rows, into = pl.ds(cy - R, R), pl.ds(0, R)
                elif dy < 0:
                    rows, into = pl.ds(0, R), pl.ds(R + cy, R)
                else:
                    rows, into = pl.ds(0, cy), pl.ds(R, cy)
                out.append(message(pack.at[slot, 1, rows], zin.at[slot, 0, 1 - dx, into], dx, dy, 1))
                out.append(message(pack.at[slot, 0, rows], zin.at[slot, 1, 1 - dx, into], dx, dy, -1))
        return out

    def stage(i, packs):
        return pack_one(i, wave_ref[i], packs)

    half = cy // 2
    halves = [(0, half), (half, half)] if half % 8 == 0 else [(0, cy)]

    def side_messages(src, dst, moves):
        out = []
        for dx, dy, first, rows in moves:
            if dx > 0:
                sx, tx = pl.ds(cx - R, R), pl.ds(0, R)
            elif dx < 0:
                sx, tx = pl.ds(0, R), pl.ds(R + cx, R)
            else:
                sx, tx = pl.ds(0, cx), pl.ds(R, cx)
            if dy > 0:
                sy, ty = pl.ds(cy - R, R), pl.ds(0, R)
            elif dy < 0:
                sy, ty = pl.ds(0, R), pl.ds(R + cy, R)
            else:
                sy, ty = pl.ds(first, rows), pl.ds(R + first, rows)
            out.append(message(src.at[sx, sy], dst.at[tx, ty], dx, dy, 0))
        return out

    face_x = [(dx, 0, first, rows) for first, rows in halves for dx in (1, -1)]
    face_y = [(0, dy, 0, 0) for dy in (1, -1)]
    edge_xy = [(dx, dy, 0, 0) for dx in (1, -1) for dy in (1, -1)]
    src_ref = sb.at[pl.ds(R, cx), pl.ds(R, cy)]
    wave_x, wave_y, wave_xy = (side_messages(wave_hbm, wb, m) for m in (face_x, face_y, edge_xy))
    wave_z, wave_xz = z_messages(0, (0,), (0,)), z_messages(0, (-1, 1), (0,))
    wave_yz, wave_xyz = z_messages(0, (0,), (-1, 1)), z_messages(0, (-1, 1), (-1, 1))
    src_x, src_y, src_xy = (side_messages(src_ref, sb, m) for m in (face_x, face_y, edge_xy))
    src_z, src_e = z_messages(1, (-1, 0, 1), (0,)), z_messages(1, (-1, 0, 1), (-1, 1))

    pl.semaphore_wait(barrier, guests)
    start(wave_x + wave_y)
    mates = greet_faces(known.at[0])
    get_wave.wait()

    pack_out(0, loop("stage", cx, stage, (zero, zero)))

    start(wave_z)
    pl.semaphore_wait(known.at[0], mates)
    greet_faces(known.at[1])
    start(wave_xz + wave_xy + wave_yz)
    get_ext.start()
    get_weights.wait()

    psi_moves = []
    for s in range(SUBSTEPS - 1):
        buf = psi.at[s]
        moves = [
            message(buf.at[pl.ds(cx, H), pl.ds(R, cy)], buf.at[pl.ds(0, H), pl.ds(R, cy)], 1, 0, 0),
            message(buf.at[pl.ds(H, H), pl.ds(R, cy)], buf.at[pl.ds(H + cx, H), pl.ds(R, cy)], -1, 0, 0),
        ]
        moves += [
            message(ypack.at[s, 1], yin.at[s, 0], 0, 1, 0),
            message(ypack.at[s, 0], yin.at[s, 1], 0, -1, 0),
        ]
        moves += z_messages(2 + s, (0,), (0,))
        psi_moves.append(moves)

    for group in [wave_x, wave_y, wave_xy, wave_z, wave_xz, wave_yz, wave_xyz,
                  src_x, src_y, src_xy, src_z, src_e] + psi_moves:
        blank(group)

    def taps_of(dim, flip):
        return [(k, w_ref[dim, R - k if flip else R + k]) for k in range(-R, R + 1)]

    row = lax.broadcasted_iota(jnp.int32, (cz, cz), 0)
    gap = row - lanes((cz, cz))

    def band(slot, taps):
        inner = jnp.zeros((cz, cz), jnp.float32)
        outer = inner
        for k, tap in taps:
            inner = jnp.where(gap == k, tap, inner)
            if k:
                outer = jnp.where(gap == (k - cz if k > 0 else k + cz), tap, outer)
        bands[slot, pl.ds(0, cz)] = inner
        bands[slot, pl.ds(cz, cz)] = outer

    def along_z(values, nears, slot):
        both = jnp.concatenate([jnp.concatenate(values, 0), jnp.concatenate(nears, 0)], 1)
        return jnp.dot(both, bands[slot], precision=lax.Precision.HIGHEST,
                       preferred_element_type=jnp.float32)

    band(0, taps_of(2, False))
    band(1, taps_of(2, True))
    gains = [STEP * 0.5 * c for c in LAP_COEF]
    band(2, [(k, gains[abs(k)]) for k in range(-H, H + 1) if k])

    def smear_xz(src, slot, square, flip, buf, first_wait, late_wait):
        taps = taps_of(0, flip)

        def tile(first):
            sides = []
            for side in range(2):
                near = [zin[slot, side, place, pl.ds(R + first, 8)] for place in range(3)]
                if square:
                    near = [v * v for v in near]
                sides.append(lane_taps(near[1], near[0], near[2], per, taps))
            ins = [src[k, pl.ds(R + first, 8)] for k in range(cx + 2 * R)]
            if square:
                ins = [v * v for v in ins]
            outs = []
            for i in range(cx):
                total = None
                for k, tap in taps:
                    part = ins[i + R + k] * tap
                    total = part if total is None else total + part
                outs.append(total)
            made = along_z(outs, [unpack(i, *sides) for i in range(cx)], int(flip))
            for i in range(cx):
                buf[i, pl.ds(R + first, 8)] = made[8 * i:8 * i + 8]

        for (first, rows), wait in zip(halves, first_wait):
            arrive(wait)
            for f in range(first, first + rows, 8):
                tile(f)
        arrive(late_wait)
        tile(-8)
        tile(cy)

    def smear_y(buf, i, taps):
        total = None
        for k, tap in taps:
            part = buf[i, pl.ds(R + k, cy)] * tap
            total = part if total is None else total + part
        return total

    pl.semaphore_wait(known.at[1], mates)
    start(wave_xyz)

    def in_turn(faces, packs):
        each = [faces[2 * n:2 * n + 2] for n in range(len(halves))]
        each[0] = packs + each[0]
        return each

    smear_xz(wb, 0, True, False, yb.at[0], in_turn(wave_x, wave_z + wave_xz), wave_y + wave_xy + wave_yz + wave_xyz)
    taps_y = taps_of(1, False)

    def source_pass(i, packs):
        coarse = smear_y(yb.at[0], i, taps_y)
        value = wave_ref[i]
        dens = value * value
        both = coarse * coarse
        source = 0.5 * dens * both - dens * coarse
        corr_ref[i] = (0.5 / 3.0) * both * coarse - 0.5 * both
        sb[R + i, pl.ds(R, cy)] = source
        return pack_one(i, source, packs)

    pack_out(1, loop("source", cx, source_pass, (zero, zero)))

    start(src_x + src_z + src_e + src_xy + src_y)
    smear_xz(sb, 1, False, True, yb.at[1], in_turn(src_x, src_z), src_y + src_xy + src_e)
    taps_yt = taps_of(1, True)

    get_ext.wait()

    def corr_pass(i, c):
        corr = corr_ref[i] + smear_y(yb.at[1], i, taps_yt)
        corr_ref[i] = corr
        va[i] = (1.0 + STEP * 0.5 * 3.0 * LAP_COEF[0]) - STEP * (corr + ext_ref[i])
        return c

    loop("corr", cx, corr_pass, 0)


    def advance(buf, reach, these, below, above):
        centers = [buf[reach + i, pl.ds(R, cy)] for i in these]
        along = along_z(centers, [unpack(i, below, above) for i in these], 2)
        made = []
        for at_, i in enumerate(these):
            total = centers[at_] * va[i] + along[at_ * cy:(at_ + 1) * cy]
            for k in range(1, H + 1):
                pair = buf[reach + i + k, pl.ds(R, cy)] + buf[reach + i - k, pl.ds(R, cy)]
                pair += buf[reach + i, pl.ds(R + k, cy)] + buf[reach + i, pl.ds(R - k, cy)]
                total += gains[k] * pair
            made.append(total)
        return made

    groups = [list(range(g, g + ZW)) for g in range(0, cx, ZW)]
    groups = groups[:1] + groups[-1:] + groups[1:-1]
    buf, reach, slot = wb, R, 0
    for s in range(SUBSTEPS):
        if s:
            arrive(psi_moves[s - 1])
            for i in range(cx):
                half = pl.ds(H * (i % 2), H)
                buf[H + i, pl.ds(R - H, H)] = yin[s - 1, 0, i // 2, half]
                buf[H + i, pl.ds(R + cy, H)] = yin[s - 1, 1, i // 2, half]
        below, above = (zin[slot, side, 1, pl.ds(R, cy)] for side in range(2))
        if s < SUBSTEPS - 1:
            after = psi.at[s]
            packs = (zero, zero)
            for n_, these in enumerate(groups):
                for i, value in zip(these, advance(buf, reach, these, below, above)):
                    after[H + i, pl.ds(R, cy)] = value
                    packs = pack_one(i, value, packs)
                    half = pl.ds(H * (i % 2), H)
                    ypack[s, 0, i // 2, half] = value[:H]
                    ypack[s, 1, i // 2, half] = value[cy - H:]
                if n_ == 1:
                    start(psi_moves[s][:2])
            pack_out(2 + s, packs)
            start(psi_moves[s][2:])
            buf, reach, slot = after, H, 2 + s
        else:
            total = zero
            for these in groups:
                for i, value in zip(these, advance(buf, reach, these, below, above)):
                    out_ref[i] = value
                    total = total + value * value

    part = jnp.sum(total, axis=0, keepdims=True)
    everyone = plane * ny
    me = iy * plane + here

    def any_id(d):
        t = lax.rem(me + d, everyone)
        p = lax.rem(t, plane)
        return t, {"gx": lax.div(p, nz), "gy": lax.div(t, plane), "gz": lax.rem(p, nz)}

    def all_sum(part, slots, ssem, rsem, me, n, ids):
        if n == 1:
            return part
        slots[me] = part

        def copy_of(d, slot):
            return pltpu.make_async_remote_copy(
                src_ref=slots.at[me], dst_ref=slots.at[slot], send_sem=ssem.at[d], recv_sem=rsem.at[slot],
                device_id=ids(d)[1], device_id_type=MESH)

        def go(d, c):
            copy_of(d, me).start()
            return c

        def come(d, c):
            copy_of(d, ids(d)[0]).wait_recv()
            return c

        def left(d, c):
            copy_of(d, me).wait_send()
            return c

        lax.fori_loop(1, n, go, 0)
        lax.fori_loop(1, n, come, 0)
        total = jnp.sum(slots[...], axis=0)
        lax.fori_loop(1, n, left, 0)
        return total

    if near:
        sums[0] = part
        for d in range(1, everyone):
            pltpu.make_async_remote_copy(
                src_ref=sums.at[0], dst_ref=sums.at[d], send_sem=send2.at[0, 0], recv_sem=recv2.at[0, 0],
                device_id=any_id(d)[1], device_id_type=MESH).start()
        rest = sums.at[pl.ds(1, everyone - 1)]
        whole = pltpu.make_async_remote_copy(
            src_ref=rest, dst_ref=rest, send_sem=send2.at[0, 0], recv_sem=recv2.at[0, 0],
            device_id=any_id(1)[1], device_id_type=MESH)
        whole.wait_recv()
        part = jnp.sum(sums[...], axis=0)
    else:
        part = all_sum(part, sums, send2.at[0], recv2.at[0], here, plane, plane_id)
        part = all_sum(part, sums2, send2.at[1], recv2.at[1], iy, ny, line_id)
    cells = float(cx * cy * cz * nx * ny * nz)
    scale_ref[...] = lax.rsqrt(jnp.full(scale_ref.shape, jnp.sum(part), jnp.float32) / cells + 1e-06)
    for copy, to in sent:
        pl.when(to)(copy.wait_send)
    if near:
        whole.wait_send()


def finish(psi_ref, corr_ref, scale_ref, out_hbm, corr_hbm, scaled, sems):
    copies = [pltpu.make_async_copy(corr_ref, corr_hbm, sems.at[0])]
    copies[0].start()
    cx, cy, cz = psi_ref.shape
    scale = scale_ref[0:1]
    steps = 2 if cx % 2 == 0 else 1
    for n in range(steps):
        some = pl.ds(n * (cx // steps), cx // steps)
        scaled[some] = psi_ref[some] * scale.reshape(1, 1, cz)
        copies.append(pltpu.make_async_copy(scaled.at[some], out_hbm.at[some], sems.at[1 + n]))
        copies[-1].start()
    for copy in copies:
        copy.wait()


def shards(sizes, wave, external, weights):
    cx, cy, cz = wave.shape
    nx, ny, nz = sizes
    f32 = jnp.float32
    n_messages = 72
    summed = nx * ny * nz if nx <= 4 and ny <= 4 and nz <= 2 else nx * nz
    most = max(summed, ny)
    vmem = pl.BlockSpec(memory_space=pltpu.VMEM)
    stay = pl.BlockSpec(memory_space=pltpu.HBM)
    psi, corr, scale = pl.pallas_call(
        functools.partial(kernel, sizes),
        out_shape=(jax.ShapeDtypeStruct(wave.shape, f32), jax.ShapeDtypeStruct(wave.shape, f32),
                   jax.ShapeDtypeStruct((8, cz), f32)),
        in_specs=[stay, stay, stay],
        out_specs=(vmem, vmem, vmem),
        scratch_shapes=[
            pltpu.VMEM((cx + 2 * R, cy + 2 * R, cz), f32),
            pltpu.VMEM((cx + 2 * R, cy + 2 * R, cz), f32),
            pltpu.VMEM((2, cx, cy + 2 * R, cz), f32),
            pltpu.VMEM((SUBSTEPS - 1, cx + 2 * H, cy + 2 * R, cz), f32),
            pltpu.VMEM((cx, cy, cz), f32),
            pltpu.VMEM((SUBSTEPS + 1, 2, cy, cz), f32),
            pltpu.VMEM((SUBSTEPS + 1, 2, 3, cy + 2 * R, cz), f32),
            pltpu.VMEM((SUBSTEPS - 1, 2, cx // 2, 2 * H, cz), f32),
            pltpu.VMEM((SUBSTEPS - 1, 2, cx // 2, 2 * H, cz), f32),
            pltpu.VMEM((3, 2 * cz, cz), f32),
            pltpu.VMEM((cx, cy, cz), f32),
            pltpu.SMEM(weights.shape, f32),
            pltpu.VMEM((summed, 1, cz), f32),
            pltpu.VMEM((ny, 1, cz), f32),
            pltpu.SemaphoreType.DMA((n_messages,)),
            pltpu.SemaphoreType.DMA((n_messages,)),
            pltpu.SemaphoreType.DMA((2, most)),
            pltpu.SemaphoreType.DMA((2, most)),
            pltpu.SemaphoreType.DMA((3,)),
            pltpu.SemaphoreType.REGULAR((2,)),
        ],
        compiler_params=pltpu.CompilerParams(collective_id=0, has_side_effects=True,
                                             vmem_limit_bytes=48 * 1024 * 1024),
    )(*[pltpu.with_memory_space_constraint(x, pltpu.HBM) for x in (weights, wave, external)])
    return pl.pallas_call(
        finish,
        out_shape=(jax.ShapeDtypeStruct(wave.shape, f32), jax.ShapeDtypeStruct(wave.shape, f32)),
        in_specs=[vmem, vmem, vmem],
        out_specs=(stay, stay),
        scratch_shapes=[pltpu.VMEM((cx, cy, cz), f32), pltpu.SemaphoreType.DMA((3,))],
    )(psi, corr, scale)


def solution(mesh):
    sizes = tuple(mesh.shape[a] for a in AXES)
    spec = P(*AXES)
    return jax.shard_map(
        functools.partial(shards, sizes),
        mesh=mesh,
        in_specs=(spec, spec, P()),
        out_specs=(spec, spec),
        check_vma=False,
    )
```

```python
import functools

import jax
import jax.numpy as jnp
from jax import lax
from jax.experimental import pallas as pl
from jax.experimental.pallas import tpu as pltpu
from jax.sharding import PartitionSpec as P

SUBSTEPS = 3
LAP_COEF = (-205.0 / 72.0, 8.0 / 5.0, -1.0 / 5.0, 8.0 / 315.0, -1.0 / 560.0)
STEP = 0.08
AXES = ("gx", "gy", "gz")
MESH = pl.DeviceIdType.MESH
R = 8
H = 4


def lanes(shape):
    return lax.broadcasted_iota(jnp.int32, shape, len(shape) - 1)


PARTNERS = [(dx, dy, dz) for dx in (-1, 0, 1) for dy in (-1, 0, 1) for dz in (-1, 0, 1) if dx or dy or dz]
GROUP = 4


def turn(value, shift):
    return value if isinstance(shift, int) and shift == 0 else pltpu.roll(value, shift, 1)


def modulo(a, n):
    return a % n if isinstance(a, int) else lax.rem(a, n)


def kernel(sizes, w_hbm, wave_hbm, ext_hbm, out_ref, corr_ref, scale_ref,
           wb, sb, yb, co, psi, va, part, pack, zin, zb, ypack, yin, bands, edges, rims, ext_ref, w_ref,
           sums, sums2, send, recv, send2, recv2, local):
    nx, ny, nz = sizes
    cx, cy, cz = wave_hbm.shape
    wave_ref = wb.at[pl.ds(R, cx), pl.ds(R, cy)]
    get_wave = pltpu.make_async_copy(wave_hbm, wave_ref, local.at[0])
    get_ext = pltpu.make_async_copy(ext_hbm, ext_ref, local.at[1])
    get_weights = pltpu.make_async_copy(w_hbm, w_ref, local.at[2])
    get_wave.start()
    get_weights.start()
    ix, iy, iz = (lax.axis_index(a) for a in AXES)
    plane = nx * nz
    per = cz // cx
    here = ix * nz + iz

    def plane_id(d):
        t = lax.rem(here + d, plane)
        return t, {"gx": lax.div(t, nz), "gz": lax.rem(t, nz)}

    def line_id(d):
        t = lax.rem(iy + d, ny)
        return t, {"gy": t}

    barrier = pltpu.get_barrier_semaphore()

    def greet(ids):
        def body(d, c):
            pl.semaphore_signal(barrier, inc=1, device_id=ids(d)[1], device_id_type=MESH)
            return c
        return body

    near = nx <= 4 and ny <= 4 and nz <= 2

    def greet_partners(partners):
        count = 0
        for d3 in partners:
            there = None
            target = {}
            for name, d, i, n in zip(AXES, d3, (ix, iy, iz), sizes):
                if d:
                    ok = i < n - 1 if d > 0 else i > 0
                    there = ok if there is None else there & ok
                    target[name] = jnp.clip(i + d, 0, n - 1)
            count += there.astype(jnp.int32)

            @pl.when(there)
            def _(target=target):
                pl.semaphore_signal(barrier, inc=1, device_id=target, device_id_type=MESH)
        return count

    if near:
        guests = greet_partners(PARTNERS)
    else:
        guests = plane - 1 + ny - 1 + greet_partners([d for d in PARTNERS if d[1] and (d[0] or d[2])])
        lax.fori_loop(1, plane, greet(plane_id), 0)
        lax.fori_loop(1, ny, greet(line_id), 0)

    counter = [0]

    def message(src, dst, dx, dy, dz):
        k = counter[0]
        counter[0] += 1
        to, back = None, None
        for d, i, n in ((dx, ix, nx), (dy, iy, ny), (dz, iz, nz)):
            if d > 0:
                a, b = i < n - 1, i > 0
            elif d < 0:
                a, b = i > 0, i < n - 1
            else:
                continue
            to = a if to is None else to & a
            back = b if back is None else back & b
        target = {}
        for name, d, i, n in zip(AXES, (dx, dy, dz), (ix, iy, iz), sizes):
            if d:
                target[name] = jnp.clip(i + d, 0, n - 1)
        copy = pltpu.make_async_remote_copy(
            src_ref=src, dst_ref=dst, send_sem=send.at[k], recv_sem=recv.at[k],
            device_id=target, device_id_type=MESH)
        return copy, to, back, dst

    sent = []

    def start(messages):
        for copy, to, _, _ in messages:
            pl.when(to)(copy.start)
            sent.append((copy, to))

    def blank(messages):
        for _, _, back, dst in messages:
            @pl.when(jnp.logical_not(back))
            def _(dst=dst):
                dst[...] = jnp.zeros(dst.shape, dst.dtype)

    def arrive(messages):
        for copy, _, back, _ in messages:
            pl.when(back)(copy.wait_recv)

    at = lanes((cy, cz))
    zero = jnp.zeros((cy, cz), jnp.float32)

    def pack_one(i, value, packs):
        mine = (at >= per * i) & (at < per * i + per)
        low = turn(value, per * i)
        high = turn(value, modulo(per * i + per, cz))
        return jnp.where(mine, low, packs[0]), jnp.where(mine, high, packs[1])

    def pack_out(slot, packs):
        pack[slot, 0] = packs[0]
        pack[slot, 1] = packs[1]

    def z_messages(slot, dxs, dys):
        out = []
        for dx in dxs:
            for dy in dys:
                if dy > 0:
                    rows, into = pl.ds(cy - R, R), pl.ds(0, R)
                elif dy < 0:
                    rows, into = pl.ds(0, R), pl.ds(R + cy, R)
                else:
                    rows, into = pl.ds(0, cy), pl.ds(R, cy)
                out.append(message(pack.at[slot, 1, rows], zin.at[slot, 0, 1 - dx, into], dx, dy, 1))
                out.append(message(pack.at[slot, 0, rows], zin.at[slot, 1, 1 - dx, into], dx, dy, -1))
        return out

    def side_messages(src, dst, moves):
        out = []
        for dx, dy in moves:
            if dx > 0:
                sx, tx = pl.ds(cx - R, R), pl.ds(0, R)
            elif dx < 0:
                sx, tx = pl.ds(0, R), pl.ds(R + cx, R)
            else:
                sx, tx = pl.ds(0, cx), pl.ds(R, cx)
            if dy > 0:
                sy, ty = pl.ds(cy - R, R), pl.ds(0, R)
            elif dy < 0:
                sy, ty = pl.ds(0, R), pl.ds(R + cy, R)
            else:
                sy, ty = pl.ds(0, cy), pl.ds(R, cy)
            out.append(message(src.at[sx, sy], dst.at[tx, ty], dx, dy, 0))
        return out

    face_x = [(dx, 0) for dx in (1, -1)]
    face_y = [(0, dy) for dy in (1, -1)]
    edge_xy = [(dx, dy) for dx in (1, -1) for dy in (1, -1)]
    src_ref = sb.at[pl.ds(R, cx), pl.ds(R, cy)]
    wave_x, wave_y, wave_xy = (side_messages(wave_hbm, wb, m) for m in (face_x, face_y, edge_xy))
    wave_z, wave_e = z_messages(0, (-1, 0, 1), (0,)), z_messages(0, (-1, 0, 1), (-1, 1))
    src_x, src_y, src_xy = (side_messages(src_ref, sb, m) for m in (face_x, face_y, edge_xy))
    src_z, src_e = z_messages(1, (-1, 0, 1), (0,)), z_messages(1, (-1, 0, 1), (-1, 1))

    psi_moves = []
    for s in range(SUBSTEPS - 1):
        buf = psi.at[s]
        moves = [
            message(buf.at[pl.ds(cx, H), pl.ds(R, cy)], buf.at[pl.ds(0, H), pl.ds(R, cy)], 1, 0, 0),
            message(buf.at[pl.ds(H, H), pl.ds(R, cy)], buf.at[pl.ds(H + cx, H), pl.ds(R, cy)], -1, 0, 0),
        ]
        moves += [
            message(ypack.at[s, 1], yin.at[s, 0], 0, 1, 0),
            message(ypack.at[s, 0], yin.at[s, 1], 0, -1, 0),
        ]
        moves += z_messages(2 + s, (0,), (0,))
        psi_moves.append(moves)

    get_wave.wait()
    packs = (zero, zero)
    for i in range(cx):
        packs = pack_one(i, wave_ref[i], packs)
    pack_out(0, packs)
    pl.semaphore_wait(barrier, guests)
    start(wave_e + wave_x + wave_z + wave_y + wave_xy)
    get_ext.start()
    for group in [wave_x, wave_y, wave_xy, wave_z, wave_e, src_x, src_y, src_xy, src_z, src_e] + psi_moves:
        blank(group)
    get_weights.wait()

    def taps_of(dim, flip):
        return [(k, w_ref[dim, R - k if flip else R + k]) for k in range(-R, R + 1)]

    row = lax.broadcasted_iota(jnp.int32, (cz, cz), 0)
    gap = row - lanes((cz, cz))
    gains = [STEP * 0.5 * c for c in LAP_COEF]
    z_taps = [taps_of(2, False), taps_of(2, True), [(k, gains[abs(k)]) for k in range(-H, H + 1) if k]]

    def dot(a, b):
        return jnp.dot(a, b, precision=lax.Precision.HIGHEST, preferred_element_type=jnp.float32)

    for slot, taps in enumerate(z_taps):
        inner = jnp.zeros((cz, cz), jnp.float32)
        for k, tap in taps:
            inner = jnp.where(gap == k, tap, inner)
        bands[slot] = inner

    tile = (per, cz)
    lane = lanes(tile)
    cell = lax.rem(lane, per)
    apart = lax.broadcasted_iota(jnp.int32, tile, 0) - cell
    group_of = lax.div(lane, per)
    owner = [group_of, lax.rem(group_of + 1, cx)]
    none = jnp.zeros(tile, jnp.float32)

    def corner(side, taps):
        shift = per if side == 0 else -per
        made = none
        for k, tap in taps:
            made = jnp.where(apart == k + shift, tap, made)
        return made

    for flip in range(2):
        taps = dict(taps_of(0, bool(flip)))
        for side in range(2):
            by_z = corner(side, [(k, tap) for k, tap in z_taps[flip] if (k < 0) == (side == 0) and k])
            is_owner = [owner[side] == q for q in range(cx)]
            for t in range(2 * cx):
                at_plane = t if t < cx else (t if t - cx < cx // 2 else t - 2 * cx)
                by_x = none
                for q in range(cx):
                    if at_plane - q in taps:
                        by_x = jnp.where(is_owner[q], taps[at_plane - q], by_x)
                edges[flip, side, pl.ds(per * t, per)] = by_x * by_z
    for side in range(2):
        by_z = corner(side, [(k, tap) for k, tap in z_taps[2] if (k < 0) == (side == 0)])
        for t in range(cx):
            rims[side, pl.ds(per * t, per)] = jnp.where(owner[side] == t, by_z, none)

    even = lax.rem(lax.div(at, per), 2) == 0

    def rim_pair(sides):
        return jnp.where(even, sides[0], sides[1]), jnp.where(even, sides[1], sides[0])

    def from_rim(pair, i, width):
        return jnp.where((at < width) | (at >= cz - width), turn(pair[i % 2], modulo(cz - per * i, cz)), zero)

    def planes(buf, first, count, rows):
        return buf[pl.ds(first, count), rows].reshape(count * rows.size, cz)

    def smear(src, slot, square, flip, faces, packs_in, late):
        taps_x, taps_y = taps_of(0, flip), taps_of(1, flip)

        def along_x(first):
            ins = [src[k, pl.ds(R + first, 8)] for k in range(cx + 2 * R)]
            if square:
                ins = [v * v for v in ins]
            for i in range(cx):
                total = None
                for k, tap in taps_x:
                    part_ = ins[i + R + k] * tap
                    total = part_ if total is None else total + part_
                yb[i, pl.ds(R + first, 8)] = total

        arrive(faces)
        for first in range(0, cy, 8):
            along_x(first)
        own = pl.ds(R, cy)
        for g in range(0, cx, cx // 2):
            yb[pl.ds(g, cx // 2), own] = dot(planes(yb, g, cx // 2, own), bands[int(flip)]).reshape(cx // 2, cy, cz)
        arrive(packs_in)
        wide = lanes((cy + 2 * R, cz)) < cz // 2
        for side in range(2):
            mine = zin[slot, side, 1]
            other = jnp.where(wide, zin[slot, side, 2], zin[slot, side, 0])
            if square:
                mine, other = mine * mine, other * other
            zb[side] = dot(jnp.concatenate([mine, other], 1), edges[int(flip), side])
        pair = []
        for side in range(2):
            total = zero
            for k, tap in taps_y:
                total = total + zb[side, pl.ds(R + k, cy)] * tap
            pair.append(total)
        pair = rim_pair(pair)
        for i in range(cx):
            total = from_rim(pair, i, R)
            low, mid, high = total[:8], total[8:cy - 8], total[cy - 8:]
            for k, tap in taps_y:
                if k >= 0:
                    low = low + yb[i, pl.ds(R + k, 8)] * tap
                mid = mid + yb[i, pl.ds(R + 8 + k, cy - 16)] * tap
                if k <= 0:
                    high = high + yb[i, pl.ds(R + cy - 8 + k, 8)] * tap
            co[i] = jnp.concatenate([low, mid, high], 0)
        arrive(late)
        for first in (-8, cy):
            along_x(first)
            rows = pl.ds(R + first, 8)
            yb[:, rows] = dot(planes(yb, 0, cx, rows), bands[int(flip)]).reshape(cx, 8, cz)

        def result(i):
            low, high = co[i, pl.ds(0, 8)], co[i, pl.ds(cy - 8, 8)]
            for k, tap in taps_y:
                if k < 0:
                    low = low + yb[i, pl.ds(R + k, 8)] * tap
                if k > 0:
                    high = high + yb[i, pl.ds(R + cy - 8 + k, 8)] * tap
            return jnp.concatenate([low, co[i, pl.ds(8, cy - 16)], high], 0)

        return result

    smeared = smear(wb, 0, True, False, wave_x, wave_z + wave_e, wave_y + wave_xy)
    packs = (zero, zero)
    for i in range(cx):
        coarse = smeared(i)
        value = wave_ref[i]
        dens = value * value
        both = coarse * coarse
        source = 0.5 * dens * both - dens * coarse
        corr_ref[i] = (0.5 / 3.0) * both * coarse - 0.5 * both
        sb[R + i, pl.ds(R, cy)] = source
        packs = pack_one(i, source, packs)
    pack_out(1, packs)
    start(src_e + src_x + src_z + src_y + src_xy)

    def z_rim(slot):
        return rim_pair([dot(zin[slot, side, 1, pl.ds(R, cy)], rims[side]) for side in range(2)])

    def own_part(buf, reach, weight, first_step):
        pair = z_rim(0) if first_step else None
        own = pl.ds(R, cy)
        for g in range(0, cx, GROUP):
            along = dot(planes(buf, reach + g, GROUP, own), bands[2])
            for i in range(g, g + GROUP):
                total = buf[reach + i, own] * weight(i) + along[(i - g) * cy:(i - g + 1) * cy]
                if first_step:
                    total = total + from_rim(pair, i, H)
                for k in range(1, H + 1):
                    pairs = [buf[reach + j, own] for j in (i - k, i + k) if first_step or 0 <= j < cx]
                    if first_step:
                        pairs += [buf[reach + i, pl.ds(R + j, cy)] for j in (-k, k)]
                    both = pairs[0]
                    for p in pairs[1:]:
                        both = both + p
                    total = total + gains[k] * both
                if not first_step:
                    up = down = None
                    for k in range(1, H + 1):
                        a = gains[k] * buf[reach + i, pl.ds(R + k, cy - 8)]
                        b = gains[k] * buf[reach + i, pl.ds(R + 8 - k, cy - 8)]
                        up, down = (a, b) if up is None else (up + a, down + b)
                    total = total + jnp.concatenate([up[:8], up[8:] + down[:cy - 16], down[cy - 16:]], 0)
                part[i] = total

    def halo_part(buf, pair, i):
        total = part[i] + from_rim(pair, i, H)
        for k in range(1, H + 1):
            for j in (i - k, i + k):
                if not 0 <= j < cx:
                    total = total + gains[k] * buf[H + j, pl.ds(R, cy)]
        low, high = total[:8], total[cy - 8:]
        for k in range(1, H + 1):
            low = low + gains[k] * buf[H + i, pl.ds(R - k, 8)]
            high = high + gains[k] * buf[H + i, pl.ds(R + cy - 8 + k, 8)]
        return jnp.concatenate([low, total[8:cy - 8], high], 0)

    middle = 1.0 + STEP * 0.5 * 3.0 * LAP_COEF[0]
    own_part(wb, R, lambda i: middle, True)
    smeared = smear(sb, 1, False, True, src_x, src_z + src_e, src_y + src_xy)
    get_ext.wait()
    groups = [list(range(g, g + GROUP)) for g in range(0, cx, GROUP)]
    groups = groups[:1] + groups[-1:] + groups[1:-1]

    def first_step(i):
        corr = corr_ref[i] + smeared(i)
        corr_ref[i] = corr
        felt = STEP * (corr + ext_ref[i])
        va[i] = middle - felt
        return part[i] - felt * wave_ref[i]

    def send_out(s, step):
        after = psi.at[s]
        packs = (zero, zero)
        for n_, these in enumerate(groups):
            for i in these:
                value = step(i)
                after[H + i, pl.ds(R, cy)] = value
                packs = pack_one(i, value, packs)
                half = pl.ds(H * (i % 2), H)
                ypack[s, 0, i // 2, half] = value[:H]
                ypack[s, 1, i // 2, half] = value[cy - H:]
            if n_ == 1:
                start(psi_moves[s][:2])
        pack_out(2 + s, packs)
        start(psi_moves[s][2:])

    send_out(0, first_step)
    total = zero
    for s in range(SUBSTEPS - 1):
        buf = psi.at[s]
        own_part(buf, H, lambda i: va[i], False)
        arrive(psi_moves[s])
        for i in range(cx):
            half = pl.ds(H * (i % 2), H)
            buf[H + i, pl.ds(R - H, H)] = yin[s, 0, i // 2, half]
            buf[H + i, pl.ds(R + cy, H)] = yin[s, 1, i // 2, half]
        pair = z_rim(2 + s)
        if s < SUBSTEPS - 2:
            send_out(s + 1, lambda i: halo_part(buf, pair, i))
        else:
            for i in range(cx):
                value = halo_part(buf, pair, i)
                out_ref[i] = value
                total = total + value * value

    partial = jnp.sum(total, axis=0, keepdims=True)
    everyone = plane * ny
    me = iy * plane + here

    def any_id(d):
        t = lax.rem(me + d, everyone)
        p = lax.rem(t, plane)
        return t, {"gx": lax.div(p, nz), "gy": lax.div(t, plane), "gz": lax.rem(p, nz)}

    def all_sum(value, slots, ssem, rsem, me, n, ids):
        if n == 1:
            return value
        slots[me] = value

        def copy_of(d, slot):
            return pltpu.make_async_remote_copy(
                src_ref=slots.at[me], dst_ref=slots.at[slot], send_sem=ssem.at[d], recv_sem=rsem.at[slot],
                device_id=ids(d)[1], device_id_type=MESH)

        def go(d, c):
            copy_of(d, me).start()
            return c

        def come(d, c):
            copy_of(d, ids(d)[0]).wait_recv()
            return c

        def left(d, c):
            copy_of(d, me).wait_send()
            return c

        lax.fori_loop(1, n, go, 0)
        lax.fori_loop(1, n, come, 0)
        total = jnp.sum(slots[...], axis=0)
        lax.fori_loop(1, n, left, 0)
        return total

    if near:
        sums[0] = partial
        for d in range(1, everyone):
            pltpu.make_async_remote_copy(
                src_ref=sums.at[0], dst_ref=sums.at[d], send_sem=send2.at[0, 0], recv_sem=recv2.at[0, 0],
                device_id=any_id(d)[1], device_id_type=MESH).start()
        rest = sums.at[pl.ds(1, everyone - 1)]
        whole = pltpu.make_async_remote_copy(
            src_ref=rest, dst_ref=rest, send_sem=send2.at[0, 0], recv_sem=recv2.at[0, 0],
            device_id=any_id(1)[1], device_id_type=MESH)
        whole.wait_recv()
        partial = jnp.sum(sums[...], axis=0)
    else:
        partial = all_sum(partial, sums, send2.at[0], recv2.at[0], here, plane, plane_id)
        partial = all_sum(partial, sums2, send2.at[1], recv2.at[1], iy, ny, line_id)
    cells = float(cx * cy * cz * nx * ny * nz)
    scale_ref[...] = lax.rsqrt(jnp.full(scale_ref.shape, jnp.sum(partial), jnp.float32) / cells + 1e-06)
    for copy, to in sent:
        pl.when(to)(copy.wait_send)
    if near:
        whole.wait_send()


def finish(psi_ref, corr_ref, scale_ref, out_hbm, corr_hbm, scaled, sems):
    copies = [pltpu.make_async_copy(corr_ref, corr_hbm, sems.at[0])]
    copies[0].start()
    cx, cy, cz = psi_ref.shape
    scale = scale_ref[0:1]
    steps = 2 if cx % 2 == 0 else 1
    for n in range(steps):
        some = pl.ds(n * (cx // steps), cx // steps)
        scaled[some] = psi_ref[some] * scale.reshape(1, 1, cz)
        copies.append(pltpu.make_async_copy(scaled.at[some], out_hbm.at[some], sems.at[1 + n]))
        copies[-1].start()
    for copy in copies:
        copy.wait()


def shards(sizes, wave, external, weights):
    cx, cy, cz = wave.shape
    nx, ny, nz = sizes
    f32 = jnp.float32
    n_messages = 72
    summed = nx * ny * nz if nx <= 4 and ny <= 4 and nz <= 2 else nx * nz
    most = max(summed, ny)
    vmem = pl.BlockSpec(memory_space=pltpu.VMEM)
    stay = pl.BlockSpec(memory_space=pltpu.HBM)
    psi, corr, scale = pl.pallas_call(
        functools.partial(kernel, sizes),
        out_shape=(jax.ShapeDtypeStruct(wave.shape, f32), jax.ShapeDtypeStruct(wave.shape, f32),
                   jax.ShapeDtypeStruct((8, cz), f32)),
        in_specs=[stay, stay, stay],
        out_specs=(vmem, vmem, vmem),
        scratch_shapes=[
            pltpu.VMEM((cx + 2 * R, cy + 2 * R, cz), f32),
            pltpu.VMEM((cx + 2 * R, cy + 2 * R, cz), f32),
            pltpu.VMEM((cx, cy + 2 * R, cz), f32),
            pltpu.VMEM((cx, cy, cz), f32),
            pltpu.VMEM((SUBSTEPS - 1, cx + 2 * H, cy + 2 * R, cz), f32),
            pltpu.VMEM((cx, cy, cz), f32),
            pltpu.VMEM((cx, cy, cz), f32),
            pltpu.VMEM((SUBSTEPS + 1, 2, cy, cz), f32),
            pltpu.VMEM((SUBSTEPS + 1, 2, 3, cy + 2 * R, cz), f32),
            pltpu.VMEM((2, cy + 2 * R, cz), f32),
            pltpu.VMEM((SUBSTEPS - 1, 2, cx // 2, 2 * H, cz), f32),
            pltpu.VMEM((SUBSTEPS - 1, 2, cx // 2, 2 * H, cz), f32),
            pltpu.VMEM((3, cz, cz), f32),
            pltpu.VMEM((2, 2, 2 * cz, cz), f32),
            pltpu.VMEM((2, cz, cz), f32),
            pltpu.VMEM((cx, cy, cz), f32),
            pltpu.SMEM(weights.shape, f32),
            pltpu.VMEM((summed, 1, cz), f32),
            pltpu.VMEM((ny, 1, cz), f32),
            pltpu.SemaphoreType.DMA((n_messages,)),
            pltpu.SemaphoreType.DMA((n_messages,)),
            pltpu.SemaphoreType.DMA((2, most)),
            pltpu.SemaphoreType.DMA((2, most)),
            pltpu.SemaphoreType.DMA((3,)),
        ],
        compiler_params=pltpu.CompilerParams(collective_id=0, has_side_effects=True,
                                             vmem_limit_bytes=48 * 1024 * 1024),
    )(*[pltpu.with_memory_space_constraint(x, pltpu.HBM) for x in (weights, wave, external)])
    return pl.pallas_call(
        finish,
        out_shape=(jax.ShapeDtypeStruct(wave.shape, f32), jax.ShapeDtypeStruct(wave.shape, f32)),
        in_specs=[vmem, vmem, vmem],
        out_specs=(stay, stay),
        scratch_shapes=[pltpu.VMEM((cx, cy, cz), f32), pltpu.SemaphoreType.DMA((3,))],
    )(*[pltpu.with_memory_space_constraint(x, pltpu.VMEM) for x in (psi, corr, scale)])


def solution(mesh):
    sizes = tuple(mesh.shape[a] for a in AXES)
    spec = P(*AXES)
    return jax.shard_map(
        functools.partial(shards, sizes),
        mesh=mesh,
        in_specs=(spec, spec, P()),
        out_specs=(spec, spec),
        check_vma=False,
    )
```

```python
import functools

import jax
import jax.numpy as jnp
from jax import lax
from jax.experimental import pallas as pl
from jax.experimental.pallas import tpu as pltpu
from jax.sharding import PartitionSpec as P

SUBSTEPS = 3
LAP_COEF = (-205.0 / 72.0, 8.0 / 5.0, -1.0 / 5.0, 8.0 / 315.0, -1.0 / 560.0)
STEP = 0.08
AXES = ("gx", "gy", "gz")
MESH = pl.DeviceIdType.MESH
R = 8
H = 4


def lanes(shape):
    return lax.broadcasted_iota(jnp.int32, shape, len(shape) - 1)


PARTNERS = [(dx, dy, dz) for dx in (-1, 0, 1) for dy in (-1, 0, 1) for dz in (-1, 0, 1) if dx or dy or dz]
GROUP = 4


def turn(value, shift):
    return value if isinstance(shift, int) and shift == 0 else pltpu.roll(value, shift, 1)


def modulo(a, n):
    return a % n if isinstance(a, int) else lax.rem(a, n)


def kernel(sizes, w_hbm, wave_hbm, ext_hbm, out_ref, corr_ref, scale_ref,
           wb, sb, yb, co, psi, va, part, pack, zin, zb, ypack, yin, bands, edges, rims, blanks, spare, ext_ref, w_ref,
           sums, sums2, send, recv, send2, recv2, local):
    nx, ny, nz = sizes
    cx, cy, cz = wave_hbm.shape
    wave_ref = wb.at[pl.ds(R, cx), pl.ds(R, cy)]
    get_wave = pltpu.make_async_copy(wave_hbm, wave_ref, local.at[0])
    get_ext = pltpu.make_async_copy(ext_hbm, ext_ref, local.at[1])
    get_weights = pltpu.make_async_copy(w_hbm, w_ref, local.at[2])
    get_wave.start()
    get_weights.start()
    ix, iy, iz = (lax.axis_index(a) for a in AXES)
    plane = nx * nz
    per = cz // cx
    here = ix * nz + iz

    def plane_id(d):
        t = lax.rem(here + d, plane)
        return t, {"gx": lax.div(t, nz), "gz": lax.rem(t, nz)}

    def line_id(d):
        t = lax.rem(iy + d, ny)
        return t, {"gy": t}

    barrier = pltpu.get_barrier_semaphore()

    def greet(ids):
        def body(d, c):
            pl.semaphore_signal(barrier, inc=1, device_id=ids(d)[1], device_id_type=MESH)
            return c
        return body

    near = nx <= 4 and ny <= 4 and nz <= 2

    def greet_partners(partners):
        count = 0
        for d3 in partners:
            there = None
            target = {}
            for name, d, i, n in zip(AXES, d3, (ix, iy, iz), sizes):
                if d:
                    ok = i < n - 1 if d > 0 else i > 0
                    there = ok if there is None else there & ok
                    target[name] = jnp.clip(i + d, 0, n - 1)
            count += there.astype(jnp.int32)

            @pl.when(there)
            def _(target=target):
                pl.semaphore_signal(barrier, inc=1, device_id=target, device_id_type=MESH)
        return count

    if near:
        guests = greet_partners(PARTNERS)
    else:
        guests = plane - 1 + ny - 1 + greet_partners([d for d in PARTNERS if d[1] and (d[0] or d[2])])
        lax.fori_loop(1, plane, greet(plane_id), 0)
        lax.fori_loop(1, ny, greet(line_id), 0)

    blanks[...] = jnp.zeros(blanks.shape, jnp.float32)
    sent_rows = {}

    def rows_of(ref):
        count = 1
        for n in ref.shape[:-1]:
            count *= n
        return count

    def message(src, dst, dx, dy, dz, group):
        to, back = None, None
        for d, i, n in ((dx, ix, nx), (dy, iy, ny), (dz, iz, nz)):
            if d > 0:
                a, b = i < n - 1, i > 0
            elif d < 0:
                a, b = i > 0, i < n - 1
            else:
                continue
            to = a if to is None else to & a
            back = b if back is None else back & b
        target = {}
        for name, d, i, n in zip(AXES, (dx, dy, dz), (ix, iy, iz), sizes):
            if d:
                target[name] = jnp.clip(i + d, 0, n - 1)
        way = PARTNERS.index((dx, dy, dz))
        rows, _ = sent_rows.get(way, (0, to))
        sent_rows[way] = rows + rows_of(dst), to
        copy = pltpu.make_async_remote_copy(
            src_ref=src, dst_ref=dst, send_sem=send.at[way], recv_sem=recv.at[group],
            device_id=target, device_id_type=MESH)
        return copy, to, back, dst, group

    def start(messages):
        for copy, to, *_ in messages:
            pl.when(to)(copy.start)

    def blank(messages):
        for _, _, back, dst, group in messages:
            first = [pl.ds(0, n) for n in dst.shape[:-1]]
            src = blanks.at[tuple(first) if len(first) == 2 else (0, *first)]
            pl.when(jnp.logical_not(back))(pltpu.make_async_copy(src, dst, recv.at[group]).start)

    def bytes_of(rows, send_sem, recv_sem):
        some = spare.at[pl.ds(0, rows)]
        return pltpu.make_async_remote_copy(
            src_ref=some, dst_ref=some, send_sem=send_sem, recv_sem=recv_sem,
            device_id={"gx": ix}, device_id_type=MESH)

    def arrive(messages):
        group = messages[0][-1]
        bytes_of(sum(rows_of(m[3]) for m in messages), send.at[0], recv.at[group]).wait_recv()

    at = lanes((cy, cz))
    zero = jnp.zeros((cy, cz), jnp.float32)

    def pack_one(i, value, packs):
        mine = (at >= per * i) & (at < per * i + per)
        low = turn(value, per * i)
        high = turn(value, modulo(per * i + per, cz))
        return jnp.where(mine, low, packs[0]), jnp.where(mine, high, packs[1])

    def pack_out(slot, packs):
        pack[slot, 0] = packs[0]
        pack[slot, 1] = packs[1]

    def z_messages(slot, dxs, dys, group):
        out = []
        for dx in dxs:
            for dy in dys:
                if dy > 0:
                    rows, into = pl.ds(cy - R, R), pl.ds(0, R)
                elif dy < 0:
                    rows, into = pl.ds(0, R), pl.ds(R + cy, R)
                else:
                    rows, into = pl.ds(0, cy), pl.ds(R, cy)
                out.append(message(pack.at[slot, 1, rows], zin.at[slot, 0, 1 - dx, into], dx, dy, 1, group))
                out.append(message(pack.at[slot, 0, rows], zin.at[slot, 1, 1 - dx, into], dx, dy, -1, group))
        return out

    def side_messages(src, dst, moves, group):
        out = []
        for dx, dy in moves:
            if dx > 0:
                sx, tx = pl.ds(cx - R, R), pl.ds(0, R)
            elif dx < 0:
                sx, tx = pl.ds(0, R), pl.ds(R + cx, R)
            else:
                sx, tx = pl.ds(0, cx), pl.ds(R, cx)
            if dy > 0:
                sy, ty = pl.ds(cy - R, R), pl.ds(0, R)
            elif dy < 0:
                sy, ty = pl.ds(0, R), pl.ds(R + cy, R)
            else:
                sy, ty = pl.ds(0, cy), pl.ds(R, cy)
            out.append(message(src.at[sx, sy], dst.at[tx, ty], dx, dy, 0, group))
        return out

    face_x = [(dx, 0) for dx in (1, -1)]
    face_y = [(0, dy) for dy in (1, -1)]
    edge_xy = [(dx, dy) for dx in (1, -1) for dy in (1, -1)]
    src_ref = sb.at[pl.ds(R, cx), pl.ds(R, cy)]
    wave_x, src_x = side_messages(wave_hbm, wb, face_x, 0), side_messages(src_ref, sb, face_x, 3)
    wave_y, src_y = side_messages(wave_hbm, wb, face_y, 2), side_messages(src_ref, sb, face_y, 5)
    wave_xy, src_xy = side_messages(wave_hbm, wb, edge_xy, 2), side_messages(src_ref, sb, edge_xy, 5)
    wave_z, src_z = z_messages(0, (-1, 0, 1), (0,), 1), z_messages(1, (-1, 0, 1), (0,), 4)
    wave_e, src_e = z_messages(0, (-1, 0, 1), (-1, 1), 1), z_messages(1, (-1, 0, 1), (-1, 1), 4)

    psi_moves = []
    for s in range(SUBSTEPS - 1):
        buf = psi.at[s]
        moves = [
            message(buf.at[pl.ds(cx, H), pl.ds(R, cy)], buf.at[pl.ds(0, H), pl.ds(R, cy)], 1, 0, 0, 6 + s),
            message(buf.at[pl.ds(H, H), pl.ds(R, cy)], buf.at[pl.ds(H + cx, H), pl.ds(R, cy)], -1, 0, 0, 6 + s),
        ]
        moves += [
            message(ypack.at[s, 1], yin.at[s, 0], 0, 1, 0, 6 + s),
            message(ypack.at[s, 0], yin.at[s, 1], 0, -1, 0, 6 + s),
        ]
        moves += z_messages(2 + s, (0,), (0,), 6 + s)
        psi_moves.append(moves)

    pl.semaphore_wait(barrier, guests)
    start(wave_x + wave_y + wave_xy)
    get_wave.wait()
    packs = (zero, zero)
    for i in range(cx):
        packs = pack_one(i, wave_ref[i], packs)
    pack_out(0, packs)
    start(wave_e + wave_z)
    get_ext.start()
    for group in [wave_x, wave_y, wave_xy, wave_z, wave_e, src_x, src_y, src_xy, src_z, src_e] + psi_moves:
        blank(group)
    get_weights.wait()

    def taps_of(dim, flip):
        return [(k, w_ref[dim, R - k if flip else R + k]) for k in range(-R, R + 1)]

    row = lax.broadcasted_iota(jnp.int32, (cz, cz), 0)
    gap = row - lanes((cz, cz))
    gains = [STEP * 0.5 * c for c in LAP_COEF]
    z_taps = [taps_of(2, False), taps_of(2, True), [(k, gains[abs(k)]) for k in range(-H, H + 1) if k]]

    def halves(a):
        high = a.astype(jnp.bfloat16)
        return high, (a - high.astype(jnp.float32)).astype(jnp.bfloat16)

    def keep(ref, index, a):
        high, low = halves(a)
        k = a.shape[0]
        ref[(*index, pl.ds(0, k), pl.ds(0, cz))] = high
        ref[(*index, pl.ds(0, k), pl.ds(cz, cz))] = low
        ref[(*index, pl.ds(k, k), pl.ds(0, cz))] = high
        ref[(*index, pl.ds(k, k), pl.ds(cz, cz))] = jnp.zeros_like(low)

    def dot(a, b):
        both = jnp.dot(jnp.concatenate(halves(a), 1), b, preferred_element_type=jnp.float32)
        return both[:, :cz] + both[:, cz:]

    for slot, taps in enumerate(z_taps):
        inner = jnp.zeros((cz, cz), jnp.float32)
        for k, tap in taps:
            inner = jnp.where(gap == k, tap, inner)
        keep(bands, (slot,), inner)

    tile = (per, cz)
    lane = lanes(tile)
    cell = lax.rem(lane, per)
    apart = lax.broadcasted_iota(jnp.int32, tile, 0) - cell
    group_of = lax.div(lane, per)
    owner = [group_of, lax.rem(group_of + 1, cx)]
    none = jnp.zeros(tile, jnp.float32)

    def corner(side, taps):
        shift = per if side == 0 else -per
        made = none
        for k, tap in taps:
            made = jnp.where(apart == k + shift, tap, made)
        return made

    for flip in range(2):
        taps = dict(taps_of(0, bool(flip)))
        for side in range(2):
            by_z = corner(side, [(k, tap) for k, tap in z_taps[flip] if (k < 0) == (side == 0) and k])
            is_owner = [owner[side] == q for q in range(cx)]
            rows = []
            for t in range(2 * cx):
                at_plane = t if t < cx else (t if t - cx < cx // 2 else t - 2 * cx)
                by_x = none
                for q in range(cx):
                    if at_plane - q in taps:
                        by_x = jnp.where(is_owner[q], taps[at_plane - q], by_x)
                rows.append(by_x * by_z)
            keep(edges, (flip, side), jnp.concatenate(rows, 0))
    for side in range(2):
        by_z = corner(side, [(k, tap) for k, tap in z_taps[2] if (k < 0) == (side == 0)])
        keep(rims, (side,), jnp.concatenate([jnp.where(owner[side] == t, by_z, none) for t in range(cx)], 0))

    even = lax.rem(lax.div(at, per), 2) == 0

    def rim_pair(sides):
        return jnp.where(even, sides[0], sides[1]), jnp.where(even, sides[1], sides[0])

    def from_rim(pair, i, width):
        return jnp.where((at < width) | (at >= cz - width), turn(pair[i % 2], modulo(cz - per * i, cz)), zero)

    def planes(buf, first, count, rows):
        return buf[pl.ds(first, count), rows].reshape(count * rows.size, cz)

    def smear(src, slot, square, flip, faces, packs_in, late):
        taps_x, taps_y = taps_of(0, flip), taps_of(1, flip)

        def load(k, first):
            v = src[k, pl.ds(R + first, 8)]
            return v * v if square else v

        def along_x(first, own, other, init):
            ins = {k: load(k, first) for k in range(cx + 2 * R) if (own if R <= k < R + cx else other)}
            for i in range(cx):
                total = yb[i, pl.ds(R + first, 8)] if init else None
                for k, tap in taps_x:
                    if i + R + k in ins:
                        part_ = ins[i + R + k] * tap
                        total = part_ if total is None else total + part_
                if total is not None:
                    yb[i, pl.ds(R + first, 8)] = total

        for first in range(0, cy, 8):
            along_x(first, True, False, False)
        arrive(faces)
        for first in range(0, cy, 8):
            along_x(first, False, True, True)
        own = pl.ds(R, cy)
        for g in range(0, cx, cx // 2):
            yb[pl.ds(g, cx // 2), own] = dot(planes(yb, g, cx // 2, own), bands[int(flip)]).reshape(cx // 2, cy, cz)
        for i in range(cx):
            low = mid = high = None
            for k, tap in taps_y:
                a = yb[i, pl.ds(R + 8 + k, cy - 16)] * tap
                mid = a if mid is None else mid + a
                if k >= 0:
                    a = yb[i, pl.ds(R + k, 8)] * tap
                    low = a if low is None else low + a
                if k <= 0:
                    a = yb[i, pl.ds(R + cy - 8 + k, 8)] * tap
                    high = a if high is None else high + a
            co[i] = jnp.concatenate([low, mid, high], 0)
        arrive(packs_in)
        wide = lanes((cy + 2 * R, cz)) < cz // 2
        for side in range(2):
            mine = zin[slot, side, 1]
            other = jnp.where(wide, zin[slot, side, 2], zin[slot, side, 0])
            if square:
                mine, other = mine * mine, other * other
            zb[side] = dot(jnp.concatenate([mine, other], 1), edges[int(flip), side])
        pair = []
        for side in range(2):
            total = zero
            for k, tap in taps_y:
                total = total + zb[side, pl.ds(R + k, cy)] * tap
            pair.append(total)
        pair = rim_pair(pair)
        arrive(late)
        for first in (-8, cy):
            along_x(first, True, True, False)
            rows = pl.ds(R + first, 8)
            yb[:, rows] = dot(planes(yb, 0, cx, rows), bands[int(flip)]).reshape(cx, 8, cz)

        def result(i):
            total = co[i] + from_rim(pair, i, R)
            low, high = total[:8], total[cy - 8:]
            for k, tap in taps_y:
                if k < 0:
                    low = low + yb[i, pl.ds(R + k, 8)] * tap
                if k > 0:
                    high = high + yb[i, pl.ds(R + cy - 8 + k, 8)] * tap
            return jnp.concatenate([low, total[8:cy - 8], high], 0)

        return result

    smeared = smear(wb, 0, True, False, wave_x, wave_z + wave_e, wave_y + wave_xy)
    packs = (zero, zero)
    for i in range(cx):
        coarse = smeared(i)
        value = wave_ref[i]
        dens = value * value
        both = coarse * coarse
        source = 0.5 * dens * both - dens * coarse
        corr_ref[i] = (0.5 / 3.0) * both * coarse - 0.5 * both
        sb[R + i, pl.ds(R, cy)] = source
        packs = pack_one(i, source, packs)
    pack_out(1, packs)
    start(src_x + src_z + src_y + src_xy + src_e)

    def z_rim(slot):
        return rim_pair([dot(zin[slot, side, 1, pl.ds(R, cy)], rims[side]) for side in range(2)])

    def own_part(buf, reach, weight, first_step):
        pair = z_rim(0) if first_step else None
        own = pl.ds(R, cy)
        step = 2 * GROUP
        for g in range(0, cx, step):
            along = dot(planes(buf, reach + g, step, own), bands[2])
            for i in range(g, g + step):
                total = buf[reach + i, own] * weight(i) + along[(i - g) * cy:(i - g + 1) * cy]
                if first_step:
                    total = total + from_rim(pair, i, H)
                for k in range(1, H + 1):
                    pairs = [buf[reach + j, own] for j in (i - k, i + k) if first_step or 0 <= j < cx]
                    if first_step:
                        pairs += [buf[reach + i, pl.ds(R + j, cy)] for j in (-k, k)]
                    both = pairs[0]
                    for p in pairs[1:]:
                        both = both + p
                    total = total + gains[k] * both
                if not first_step:
                    up = down = None
                    for k in range(1, H + 1):
                        a = gains[k] * buf[reach + i, pl.ds(R + k, cy - 8)]
                        b = gains[k] * buf[reach + i, pl.ds(R + 8 - k, cy - 8)]
                        up, down = (a, b) if up is None else (up + a, down + b)
                    total = total + jnp.concatenate([up[:8], up[8:] + down[:cy - 16], down[cy - 16:]], 0)
                part[i] = total

    def halo_part(buf, pair, i):
        total = part[i] + from_rim(pair, i, H)
        for k in range(1, H + 1):
            for j in (i - k, i + k):
                if not 0 <= j < cx:
                    total = total + gains[k] * buf[H + j, pl.ds(R, cy)]
        low, high = total[:8], total[cy - 8:]
        for k in range(1, H + 1):
            low = low + gains[k] * buf[H + i, pl.ds(R - k, 8)]
            high = high + gains[k] * buf[H + i, pl.ds(R + cy - 8 + k, 8)]
        return jnp.concatenate([low, total[8:cy - 8], high], 0)

    middle = 1.0 + STEP * 0.5 * 3.0 * LAP_COEF[0]
    own_part(wb, R, lambda i: middle, True)
    smeared = smear(sb, 1, False, True, src_x, src_z + src_e, src_y + src_xy)
    get_ext.wait()
    groups = [list(range(g, g + GROUP)) for g in range(0, cx, GROUP)]
    groups = groups[:1] + groups[-1:] + groups[1:-1]

    def first_step(i):
        corr = corr_ref[i] + smeared(i)
        corr_ref[i] = corr
        felt = STEP * (corr + ext_ref[i])
        va[i] = middle - felt
        return part[i] - felt * wave_ref[i]

    def send_out(s, step):
        after = psi.at[s]
        packs = (zero, zero)
        for n_, these in enumerate(groups):
            for i in these:
                value = step(i)
                after[H + i, pl.ds(R, cy)] = value
                packs = pack_one(i, value, packs)
                half = pl.ds(H * (i % 2), H)
                ypack[s, 0, i // 2, half] = value[:H]
                ypack[s, 1, i // 2, half] = value[cy - H:]
            if n_ == 1:
                start(psi_moves[s][:2])
        pack_out(2 + s, packs)
        start(psi_moves[s][2:])

    send_out(0, first_step)
    total = zero
    for s in range(SUBSTEPS - 1):
        buf = psi.at[s]
        own_part(buf, H, lambda i: va[i], False)
        arrive(psi_moves[s])
        for i in range(cx):
            half = pl.ds(H * (i % 2), H)
            buf[H + i, pl.ds(R - H, H)] = yin[s, 0, i // 2, half]
            buf[H + i, pl.ds(R + cy, H)] = yin[s, 1, i // 2, half]
        pair = z_rim(2 + s)
        if s < SUBSTEPS - 2:
            send_out(s + 1, lambda i: halo_part(buf, pair, i))
        else:
            for i in range(cx):
                value = halo_part(buf, pair, i)
                out_ref[i] = value
                total = total + value * value

    partial = jnp.sum(total, axis=0, keepdims=True)
    everyone = plane * ny
    me = iy * plane + here

    def any_id(d):
        t = lax.rem(me + d, everyone)
        p = lax.rem(t, plane)
        return t, {"gx": lax.div(p, nz), "gy": lax.div(t, plane), "gz": lax.rem(p, nz)}

    def all_sum(value, slots, ssem, rsem, me, n, ids):
        if n == 1:
            return value
        slots[me] = value

        def copy_of(d, slot):
            return pltpu.make_async_remote_copy(
                src_ref=slots.at[me], dst_ref=slots.at[slot], send_sem=ssem.at[d], recv_sem=rsem.at[slot],
                device_id=ids(d)[1], device_id_type=MESH)

        def go(d, c):
            copy_of(d, me).start()
            return c

        def come(d, c):
            copy_of(d, ids(d)[0]).wait_recv()
            return c

        def left(d, c):
            copy_of(d, me).wait_send()
            return c

        lax.fori_loop(1, n, go, 0)
        lax.fori_loop(1, n, come, 0)
        total = jnp.sum(slots[...], axis=0)
        lax.fori_loop(1, n, left, 0)
        return total

    if near:
        sums[0] = partial
        for d in range(1, everyone):
            pltpu.make_async_remote_copy(
                src_ref=sums.at[0], dst_ref=sums.at[d], send_sem=send2.at[0, 0], recv_sem=recv2.at[0, 0],
                device_id=any_id(d)[1], device_id_type=MESH).start()
        rest = sums.at[pl.ds(1, everyone - 1)]
        whole = pltpu.make_async_remote_copy(
            src_ref=rest, dst_ref=rest, send_sem=send2.at[0, 0], recv_sem=recv2.at[0, 0],
            device_id=any_id(1)[1], device_id_type=MESH)
        whole.wait_recv()
        partial = jnp.sum(sums[...], axis=0)
    else:
        partial = all_sum(partial, sums, send2.at[0], recv2.at[0], here, plane, plane_id)
        partial = all_sum(partial, sums2, send2.at[1], recv2.at[1], iy, ny, line_id)
    cells = float(cx * cy * cz * nx * ny * nz)
    scale_ref[...] = lax.rsqrt(jnp.full(scale_ref.shape, jnp.sum(partial), jnp.float32) / cells + 1e-06)
    for way, (rows, to) in sent_rows.items():
        pl.when(to)(bytes_of(rows, send.at[way], recv.at[0]).wait_send)
    if near:
        whole.wait_send()


def finish(psi_ref, corr_ref, scale_ref, out_hbm, corr_hbm, scaled, sems):
    copies = [pltpu.make_async_copy(corr_ref, corr_hbm, sems.at[0])]
    copies[0].start()
    cx, cy, cz = psi_ref.shape
    scale = scale_ref[0:1]
    steps = 2 if cx % 2 == 0 else 1
    for n in range(steps):
        some = pl.ds(n * (cx // steps), cx // steps)
        scaled[some] = psi_ref[some] * scale.reshape(1, 1, cz)
        copies.append(pltpu.make_async_copy(scaled.at[some], out_hbm.at[some], sems.at[1 + n]))
        copies[-1].start()
    for copy in copies:
        copy.wait()


def shards(sizes, wave, external, weights):
    cx, cy, cz = wave.shape
    nx, ny, nz = sizes
    f32 = jnp.float32
    near = nx <= 4 and ny <= 4 and nz <= 2
    spare_rows = max(2 * (R + H) * cy, 2 * cx * (R + H), 2 * cx * R + 4 * R * R, 6 * cy + 12 * R)
    summed = nx * ny * nz if near else nx * nz
    stages, most = (1, 1) if near else (2, max(summed, ny))
    vmem = pl.BlockSpec(memory_space=pltpu.VMEM)
    stay = pl.BlockSpec(memory_space=pltpu.HBM)
    psi, corr, scale = pl.pallas_call(
        functools.partial(kernel, sizes),
        out_shape=(jax.ShapeDtypeStruct(wave.shape, f32), jax.ShapeDtypeStruct(wave.shape, f32),
                   jax.ShapeDtypeStruct((8, cz), f32)),
        in_specs=[stay, stay, stay],
        out_specs=(vmem, vmem, vmem),
        scratch_shapes=[
            pltpu.VMEM((cx + 2 * R, cy + 2 * R, cz), f32),
            pltpu.VMEM((cx + 2 * R, cy + 2 * R, cz), f32),
            pltpu.VMEM((cx, cy + 2 * R, cz), f32),
            pltpu.VMEM((cx, cy, cz), f32),
            pltpu.VMEM((SUBSTEPS - 1, cx + 2 * H, cy + 2 * R, cz), f32),
            pltpu.VMEM((cx, cy, cz), f32),
            pltpu.VMEM((cx, cy, cz), f32),
            pltpu.VMEM((SUBSTEPS + 1, 2, cy, cz), f32),
            pltpu.VMEM((SUBSTEPS + 1, 2, 3, cy + 2 * R, cz), f32),
            pltpu.VMEM((2, cy + 2 * R, cz), f32),
            pltpu.VMEM((SUBSTEPS - 1, 2, cx // 2, 2 * H, cz), f32),
            pltpu.VMEM((SUBSTEPS - 1, 2, cx // 2, 2 * H, cz), f32),
            pltpu.VMEM((3, 2 * cz, 2 * cz), jnp.bfloat16),
            pltpu.VMEM((2, 2, 4 * cz, 2 * cz), jnp.bfloat16),
            pltpu.VMEM((2, 2 * cz, 2 * cz), jnp.bfloat16),
            pltpu.VMEM((cx, cy, cz), f32),
            pltpu.VMEM((spare_rows, cz), f32),
            pltpu.VMEM((cx, cy, cz), f32),
            pltpu.SMEM(weights.shape, f32),
            pltpu.VMEM((summed, 1, cz), f32),
            pltpu.VMEM((ny, 1, cz), f32),
            pltpu.SemaphoreType.DMA((len(PARTNERS),)),
            pltpu.SemaphoreType.DMA((6 + SUBSTEPS - 1,)),
            pltpu.SemaphoreType.DMA((stages, most)),
            pltpu.SemaphoreType.DMA((stages, most)),
            pltpu.SemaphoreType.DMA((3,)),
        ],
        compiler_params=pltpu.CompilerParams(collective_id=0, has_side_effects=True,
                                             vmem_limit_bytes=48 * 1024 * 1024),
    )(*[pltpu.with_memory_space_constraint(x, pltpu.HBM) for x in (weights, wave, external)])
    return pl.pallas_call(
        finish,
        out_shape=(jax.ShapeDtypeStruct(wave.shape, f32), jax.ShapeDtypeStruct(wave.shape, f32)),
        in_specs=[vmem, vmem, vmem],
        out_specs=(stay, stay),
        scratch_shapes=[pltpu.VMEM((cx, cy, cz), f32), pltpu.SemaphoreType.DMA((3,))],
    )(*[pltpu.with_memory_space_constraint(x, pltpu.VMEM) for x in (psi, corr, scale)])


def solution(mesh):
    sizes = tuple(mesh.shape[a] for a in AXES)
    spec = P(*AXES)
    return jax.shard_map(
        functools.partial(shards, sizes),
        mesh=mesh,
        in_specs=(spec, spec, P()),
        out_specs=(spec, spec),
        check_vma=False,
    )
```

```python
import functools

import jax
import jax.numpy as jnp
from jax import lax
from jax.experimental import pallas as pl
from jax.experimental.pallas import tpu as pltpu
from jax.sharding import PartitionSpec as P

SUBSTEPS = 3
LAP_COEF = (-205.0 / 72.0, 8.0 / 5.0, -1.0 / 5.0, 8.0 / 315.0, -1.0 / 560.0)
STEP = 0.08
AXES = ("gx", "gy", "gz")
MESH = pl.DeviceIdType.MESH
R = 8
H = 4


def lanes(shape):
    return lax.broadcasted_iota(jnp.int32, shape, len(shape) - 1)


PARTNERS = [(dx, dy, dz) for dx in (-1, 0, 1) for dy in (-1, 0, 1) for dz in (-1, 0, 1) if dx or dy or dz]
FLAT = [(dx, dy) for dx in (-1, 0, 1) for dy in (-1, 0, 1) if dx or dy]
GROUP = 4


def turn(value, shift):
    return value if isinstance(shift, int) and shift == 0 else pltpu.roll(value, shift, 1)


def modulo(a, n):
    return a % n if isinstance(a, int) else lax.rem(a, n)


def kernel(sizes, w_hbm, wave_hbm, ext_hbm, out_ref, corr_ref, scale_ref,
           wb, sb, yb, co, psi, va, part, pack, zin, zb, ypack, yin, bands, edges, rims, blanks, spare, ext_ref, w_ref,
           sums, sums2, send, recv, send2, recv2, local):
    nx, ny, nz = sizes
    cx, cy, cz = wave_hbm.shape
    wave_ref = wb.at[pl.ds(R, cx), pl.ds(R, cy)]
    get_wave = pltpu.make_async_copy(wave_hbm, wave_ref, local.at[0])
    get_ext = pltpu.make_async_copy(ext_hbm, ext_ref, local.at[1])
    get_weights = pltpu.make_async_copy(w_hbm, w_ref, local.at[2])
    get_wave.start()
    get_weights.start()
    ix, iy, iz = (lax.axis_index(a) for a in AXES)
    plane = nx * nz
    per = cz // cx
    here = ix * nz + iz

    def plane_id(d):
        t = lax.rem(here + d, plane)
        return t, {"gx": lax.div(t, nz), "gz": lax.rem(t, nz)}

    def line_id(d):
        t = lax.rem(iy + d, ny)
        return t, {"gy": t}

    barrier = pltpu.get_barrier_semaphore()

    def greet(ids):
        def body(d, c):
            pl.semaphore_signal(barrier, inc=1, device_id=ids(d)[1], device_id_type=MESH)
            return c
        return body

    near = nx <= 4 and ny <= 4 and nz <= 2

    def greet_partners(partners):
        count = 0
        for d3 in partners:
            there = None
            target = {}
            for name, d, i, n in zip(AXES, d3, (ix, iy, iz), sizes):
                if d:
                    ok = i < n - 1 if d > 0 else i > 0
                    there = ok if there is None else there & ok
                    target[name] = jnp.clip(i + d, 0, n - 1)
            count += there.astype(jnp.int32)

            @pl.when(there)
            def _(target=target):
                pl.semaphore_signal(barrier, inc=1, device_id=target, device_id_type=MESH)
        return count

    if near:
        guests = greet_partners(PARTNERS)
    else:
        guests = plane - 1 + ny - 1 + greet_partners([d for d in PARTNERS if d[1] and (d[0] or d[2])])
        lax.fori_loop(1, plane, greet(plane_id), 0)
        lax.fori_loop(1, ny, greet(line_id), 0)

    blanks[...] = jnp.zeros(blanks.shape, jnp.float32)
    pool = len(FLAT)
    sent_rows = {}

    def rows_of(ref):
        count = 1
        for n in ref.shape[:-1]:
            count *= n
        return count

    def message(src, dst, dx, dy, dz, group):
        to, back = None, None
        for d, i, n in ((dx, ix, nx), (dy, iy, ny), (dz, iz, nz)):
            if d > 0:
                a, b = i < n - 1, i > 0
            elif d < 0:
                a, b = i > 0, i < n - 1
            else:
                continue
            to = a if to is None else to & a
            back = b if back is None else back & b
        target = {}
        for name, d, i, n in zip(AXES, (dx, dy, dz), (ix, iy, iz), sizes):
            if d:
                target[name] = jnp.clip(i + d, 0, n - 1)
        way = PARTNERS.index((dx, dy, dz))
        rows, _ = sent_rows.get(way, (0, to))
        sent_rows[way] = rows + rows_of(dst), to
        copy = pltpu.make_async_remote_copy(
            src_ref=src, dst_ref=dst, send_sem=send.at[way],
            recv_sem=recv.at[group % 2, pool + group // 2 if dz else FLAT.index((dx, dy))],
            device_id=target, device_id_type=MESH)
        return copy, to, back, dst, dz, group

    def start(messages):
        for copy, to, *_ in messages:
            pl.when(to)(copy.start)

    def blank(messages):
        for _, _, back, dst, dz, group in messages:
            @pl.when(jnp.logical_not(back))
            def _(dst=dst, dz=dz, group=group):
                if dz:
                    pltpu.make_async_copy(blanks.at[pl.ds(0, dst.shape[0])], dst, recv.at[group % 2, pool + group // 2]).start()
                else:
                    dst[...] = jnp.zeros(dst.shape, dst.dtype)

    def bytes_of(rows, send_sem, recv_sem):
        some = spare.at[pl.ds(0, rows)]
        return pltpu.make_async_remote_copy(
            src_ref=some, dst_ref=some, send_sem=send_sem, recv_sem=recv_sem,
            device_id={"gx": ix}, device_id_type=MESH)

    def arrive(messages):
        rows = 0
        for copy, _, back, dst, dz, group in messages:
            if dz:
                rows += rows_of(dst)
            else:
                pl.when(back)(copy.wait_recv)
        if rows:
            bytes_of(rows, send.at[0], recv.at[group % 2, pool + group // 2]).wait_recv()

    at = lanes((cy, cz))
    zero = jnp.zeros((cy, cz), jnp.float32)

    def pack_one(i, value, packs):
        mine = (at >= per * i) & (at < per * i + per)
        low = turn(value, per * i)
        high = turn(value, modulo(per * i + per, cz))
        return jnp.where(mine, low, packs[0]), jnp.where(mine, high, packs[1])

    def pack_out(slot, packs):
        pack[slot, 0] = packs[0]
        pack[slot, 1] = packs[1]

    def z_messages(slot, dxs, dys, group):
        out = []
        for dx in dxs:
            for dy in dys:
                if dy > 0:
                    rows, into = pl.ds(cy - R, R), pl.ds(0, R)
                elif dy < 0:
                    rows, into = pl.ds(0, R), pl.ds(R + cy, R)
                else:
                    rows, into = pl.ds(0, cy), pl.ds(R, cy)
                out.append(message(pack.at[slot, 1, rows], zin.at[slot, 0, 1 - dx, into], dx, dy, 1, group))
                out.append(message(pack.at[slot, 0, rows], zin.at[slot, 1, 1 - dx, into], dx, dy, -1, group))
        return out

    def side_messages(src, dst, moves, group):
        out = []
        for dx, dy in moves:
            if dx > 0:
                sx, tx = pl.ds(cx - R, R), pl.ds(0, R)
            elif dx < 0:
                sx, tx = pl.ds(0, R), pl.ds(R + cx, R)
            else:
                sx, tx = pl.ds(0, cx), pl.ds(R, cx)
            if dy > 0:
                sy, ty = pl.ds(cy - R, R), pl.ds(0, R)
            elif dy < 0:
                sy, ty = pl.ds(0, R), pl.ds(R + cy, R)
            else:
                sy, ty = pl.ds(0, cy), pl.ds(R, cy)
            out.append(message(src.at[sx, sy], dst.at[tx, ty], dx, dy, 0, group))
        return out

    face_x = [(dx, 0) for dx in (1, -1)]
    face_y = [(0, dy) for dy in (1, -1)]
    edge_xy = [(dx, dy) for dx in (1, -1) for dy in (1, -1)]
    src_ref = sb.at[pl.ds(R, cx), pl.ds(R, cy)]
    wave_x, src_x = side_messages(wave_hbm, wb, face_x, 0), side_messages(src_ref, sb, face_x, 1)
    wave_y, src_y = side_messages(wave_hbm, wb, face_y, 0), side_messages(src_ref, sb, face_y, 1)
    wave_xy, src_xy = side_messages(wave_hbm, wb, edge_xy, 0), side_messages(src_ref, sb, edge_xy, 1)
    wave_z, src_z = z_messages(0, (-1, 0, 1), (0,), 0), z_messages(1, (-1, 0, 1), (0,), 1)
    wave_e, src_e = z_messages(0, (-1, 0, 1), (-1, 1), 0), z_messages(1, (-1, 0, 1), (-1, 1), 1)

    psi_moves = []
    for s in range(SUBSTEPS - 1):
        buf = psi.at[s]
        moves = [
            message(buf.at[pl.ds(cx, H), pl.ds(R, cy)], buf.at[pl.ds(0, H), pl.ds(R, cy)], 1, 0, 0, 2 + s),
            message(buf.at[pl.ds(H, H), pl.ds(R, cy)], buf.at[pl.ds(H + cx, H), pl.ds(R, cy)], -1, 0, 0, 2 + s),
        ]
        moves += [
            message(ypack.at[s, 1], yin.at[s, 0], 0, 1, 0, 2 + s),
            message(ypack.at[s, 0], yin.at[s, 1], 0, -1, 0, 2 + s),
        ]
        moves += z_messages(2 + s, (0,), (0,), 2 + s)
        psi_moves.append(moves)

    pl.semaphore_wait(barrier, guests)
    start(wave_x + wave_y)
    get_wave.wait()
    packs = (zero, zero)
    for i in range(cx):
        packs = pack_one(i, wave_ref[i], packs)
    pack_out(0, packs)
    start(wave_e + wave_z + wave_xy)
    get_ext.start()
    for group in [wave_x, wave_y, wave_xy, wave_z, wave_e, src_x, src_y, src_xy, src_z, src_e] + psi_moves:
        blank(group)
    get_weights.wait()

    def taps_of(dim, flip):
        return [(k, w_ref[dim, R - k if flip else R + k]) for k in range(-R, R + 1)]

    row = lax.broadcasted_iota(jnp.int32, (cz, cz), 0)
    gap = row - lanes((cz, cz))
    gains = [STEP * 0.5 * c for c in LAP_COEF]
    z_taps = [taps_of(2, False), taps_of(2, True), [(k, gains[abs(k)]) for k in range(-H, H + 1) if k]]

    def halves(a):
        high = a.astype(jnp.bfloat16)
        return high, (a - high.astype(jnp.float32)).astype(jnp.bfloat16)

    def keep(ref, index, a):
        high, low = halves(a)
        k = a.shape[0]
        ref[(*index, pl.ds(0, k), pl.ds(0, cz))] = high
        ref[(*index, pl.ds(0, k), pl.ds(cz, cz))] = low
        ref[(*index, pl.ds(k, k), pl.ds(0, cz))] = high
        ref[(*index, pl.ds(k, k), pl.ds(cz, cz))] = jnp.zeros_like(low)

    def dot(a, b):
        both = jnp.dot(jnp.concatenate(halves(a), 1), b, preferred_element_type=jnp.float32)
        return both[:, :cz] + both[:, cz:]

    for slot, taps in enumerate(z_taps):
        inner = jnp.zeros((cz, cz), jnp.float32)
        for k, tap in taps:
            inner = jnp.where(gap == k, tap, inner)
        keep(bands, (slot,), inner)

    tile = (per, cz)
    lane = lanes(tile)
    cell = lax.rem(lane, per)
    apart = lax.broadcasted_iota(jnp.int32, tile, 0) - cell
    group_of = lax.div(lane, per)
    owner = [group_of, lax.rem(group_of + 1, cx)]
    none = jnp.zeros(tile, jnp.float32)

    def corner(side, taps):
        shift = per if side == 0 else -per
        made = none
        for k, tap in taps:
            made = jnp.where(apart == k + shift, tap, made)
        return made

    for flip in range(2):
        taps = dict(taps_of(0, bool(flip)))
        for side in range(2):
            by_z = corner(side, [(k, tap) for k, tap in z_taps[flip] if (k < 0) == (side == 0) and k])
            is_owner = [owner[side] == q for q in range(cx)]
            rows = []
            for t in range(2 * cx):
                at_plane = t if t < cx else (t if t - cx < cx // 2 else t - 2 * cx)
                by_x = none
                for q in range(cx):
                    if at_plane - q in taps:
                        by_x = jnp.where(is_owner[q], taps[at_plane - q], by_x)
                rows.append(by_x * by_z)
            keep(edges, (flip, side), jnp.concatenate(rows, 0))
    for side in range(2):
        by_z = corner(side, [(k, tap) for k, tap in z_taps[2] if (k < 0) == (side == 0)])
        keep(rims, (side,), jnp.concatenate([jnp.where(owner[side] == t, by_z, none) for t in range(cx)], 0))

    even = lax.rem(lax.div(at, per), 2) == 0

    def rim_pair(sides):
        return jnp.where(even, sides[0], sides[1]), jnp.where(even, sides[1], sides[0])

    def from_rim(pair, i, width):
        return jnp.where((at < width) | (at >= cz - width), turn(pair[i % 2], modulo(cz - per * i, cz)), zero)

    def planes(buf, first, count, rows):
        return buf[pl.ds(first, count), rows].reshape(count * rows.size, cz)

    def smear(src, slot, square, flip, faces, packs_in, late):
        taps_x, taps_y = taps_of(0, flip), taps_of(1, flip)

        def load(k, first):
            v = src[k, pl.ds(R + first, 8)]
            return v * v if square else v

        def along_x(first, own, other, init):
            ins = {k: load(k, first) for k in range(cx + 2 * R) if (own if R <= k < R + cx else other)}
            for i in range(cx):
                total = yb[i, pl.ds(R + first, 8)] if init else None
                for k, tap in taps_x:
                    if i + R + k in ins:
                        part_ = ins[i + R + k] * tap
                        total = part_ if total is None else total + part_
                if total is not None:
                    yb[i, pl.ds(R + first, 8)] = total

        for first in range(0, cy, 8):
            along_x(first, True, False, False)
        arrive(faces)
        for first in range(0, cy, 8):
            along_x(first, False, True, True)
        own = pl.ds(R, cy)
        for g in range(0, cx, cx // 2):
            yb[pl.ds(g, cx // 2), own] = dot(planes(yb, g, cx // 2, own), bands[int(flip)]).reshape(cx // 2, cy, cz)
        for i in range(cx):
            low = mid = high = None
            for k, tap in taps_y:
                a = yb[i, pl.ds(R + 8 + k, cy - 16)] * tap
                mid = a if mid is None else mid + a
                if k >= 0:
                    a = yb[i, pl.ds(R + k, 8)] * tap
                    low = a if low is None else low + a
                if k <= 0:
                    a = yb[i, pl.ds(R + cy - 8 + k, 8)] * tap
                    high = a if high is None else high + a
            co[i] = jnp.concatenate([low, mid, high], 0)
        arrive(packs_in)
        wide = lanes((cy + 2 * R, cz)) < cz // 2
        for side in range(2):
            mine = zin[slot, side, 1]
            other = jnp.where(wide, zin[slot, side, 2], zin[slot, side, 0])
            if square:
                mine, other = mine * mine, other * other
            zb[side] = dot(jnp.concatenate([mine, other], 1), edges[int(flip), side])
        pair = []
        for side in range(2):
            total = zero
            for k, tap in taps_y:
                total = total + zb[side, pl.ds(R + k, cy)] * tap
            pair.append(total)
        pair = rim_pair(pair)
        arrive(late)
        for first in (-8, cy):
            along_x(first, True, True, False)
            rows = pl.ds(R + first, 8)
            yb[:, rows] = dot(planes(yb, 0, cx, rows), bands[int(flip)]).reshape(cx, 8, cz)

        def result(i):
            total = co[i] + from_rim(pair, i, R)
            low, high = total[:8], total[cy - 8:]
            for k, tap in taps_y:
                if k < 0:
                    low = low + yb[i, pl.ds(R + k, 8)] * tap
                if k > 0:
                    high = high + yb[i, pl.ds(R + cy - 8 + k, 8)] * tap
            return jnp.concatenate([low, total[8:cy - 8], high], 0)

        return result

    smeared = smear(wb, 0, True, False, wave_x, wave_z + wave_e, wave_y + wave_xy)
    packs = (zero, zero)
    for i in range(cx):
        coarse = smeared(i)
        value = wave_ref[i]
        dens = value * value
        both = coarse * coarse
        source = 0.5 * dens * both - dens * coarse
        corr_ref[i] = (0.5 / 3.0) * both * coarse - 0.5 * both
        sb[R + i, pl.ds(R, cy)] = source
        packs = pack_one(i, source, packs)
    pack_out(1, packs)
    start(src_e + src_z + src_x + src_y + src_xy)

    def z_rim(slot):
        return rim_pair([dot(zin[slot, side, 1, pl.ds(R, cy)], rims[side]) for side in range(2)])

    def own_part(buf, reach, weight, first_step):
        pair = z_rim(0) if first_step else None
        own = pl.ds(R, cy)
        step = 2 * GROUP
        for g in range(0, cx, step):
            along = dot(planes(buf, reach + g, step, own), bands[2])
            for i in range(g, g + step):
                total = buf[reach + i, own] * weight(i) + along[(i - g) * cy:(i - g + 1) * cy]
                if first_step:
                    total = total + from_rim(pair, i, H)
                for k in range(1, H + 1):
                    pairs = [buf[reach + j, own] for j in (i - k, i + k) if first_step or 0 <= j < cx]
                    if first_step:
                        pairs += [buf[reach + i, pl.ds(R + j, cy)] for j in (-k, k)]
                    both = pairs[0]
                    for p in pairs[1:]:
                        both = both + p
                    total = total + gains[k] * both
                if not first_step:
                    up = down = None
                    for k in range(1, H + 1):
                        a = gains[k] * buf[reach + i, pl.ds(R + k, cy - 8)]
                        b = gains[k] * buf[reach + i, pl.ds(R + 8 - k, cy - 8)]
                        up, down = (a, b) if up is None else (up + a, down + b)
                    total = total + jnp.concatenate([up[:8], up[8:] + down[:cy - 16], down[cy - 16:]], 0)
                part[i] = total

    def halo_part(buf, pair, i):
        total = part[i] + from_rim(pair, i, H)
        for k in range(1, H + 1):
            for j in (i - k, i + k):
                if not 0 <= j < cx:
                    total = total + gains[k] * buf[H + j, pl.ds(R, cy)]
        low, high = total[:8], total[cy - 8:]
        for k in range(1, H + 1):
            low = low + gains[k] * buf[H + i, pl.ds(R - k, 8)]
            high = high + gains[k] * buf[H + i, pl.ds(R + cy - 8 + k, 8)]
        return jnp.concatenate([low, total[8:cy - 8], high], 0)

    middle = 1.0 + STEP * 0.5 * 3.0 * LAP_COEF[0]
    own_part(wb, R, lambda i: middle, True)
    smeared = smear(sb, 1, False, True, src_x, src_z + src_e, src_y + src_xy)
    get_ext.wait()
    groups = [list(range(g, g + GROUP)) for g in range(0, cx, GROUP)]
    groups = groups[:1] + groups[-1:] + groups[1:-1]

    def first_step(i):
        corr = corr_ref[i] + smeared(i)
        corr_ref[i] = corr
        felt = STEP * (corr + ext_ref[i])
        va[i] = middle - felt
        return part[i] - felt * wave_ref[i]

    def send_out(s, step):
        after = psi.at[s]
        packs = (zero, zero)
        for n_, these in enumerate(groups):
            for i in these:
                value = step(i)
                after[H + i, pl.ds(R, cy)] = value
                packs = pack_one(i, value, packs)
                half = pl.ds(H * (i % 2), H)
                ypack[s, 0, i // 2, half] = value[:H]
                ypack[s, 1, i // 2, half] = value[cy - H:]
            if n_ == 1:
                start(psi_moves[s][:2])
        pack_out(2 + s, packs)
        start(psi_moves[s][2:])

    send_out(0, first_step)
    total = zero
    for s in range(SUBSTEPS - 1):
        buf = psi.at[s]
        own_part(buf, H, lambda i: va[i], False)
        arrive(psi_moves[s])
        for i in range(cx):
            half = pl.ds(H * (i % 2), H)
            buf[H + i, pl.ds(R - H, H)] = yin[s, 0, i // 2, half]
            buf[H + i, pl.ds(R + cy, H)] = yin[s, 1, i // 2, half]
        pair = z_rim(2 + s)
        if s < SUBSTEPS - 2:
            send_out(s + 1, lambda i: halo_part(buf, pair, i))
        else:
            for i in range(cx):
                value = halo_part(buf, pair, i)
                out_ref[i] = value
                total = total + value * value

    partial = jnp.sum(total, axis=0, keepdims=True)
    everyone = plane * ny
    me = iy * plane + here

    def any_id(d):
        t = lax.rem(me + d, everyone)
        p = lax.rem(t, plane)
        return t, {"gx": lax.div(p, nz), "gy": lax.div(t, plane), "gz": lax.rem(p, nz)}

    def all_sum(value, slots, ssem, rsem, me, n, ids):
        if n == 1:
            return value
        slots[me] = value

        def copy_of(d, slot):
            return pltpu.make_async_remote_copy(
                src_ref=slots.at[me], dst_ref=slots.at[slot], send_sem=ssem.at[d], recv_sem=rsem.at[slot],
                device_id=ids(d)[1], device_id_type=MESH)

        def go(d, c):
            copy_of(d, me).start()
            return c

        def come(d, c):
            copy_of(d, ids(d)[0]).wait_recv()
            return c

        def left(d, c):
            copy_of(d, me).wait_send()
            return c

        lax.fori_loop(1, n, go, 0)
        lax.fori_loop(1, n, come, 0)
        total = jnp.sum(slots[...], axis=0)
        lax.fori_loop(1, n, left, 0)
        return total

    if near:
        sums[0] = partial
        for d in range(1, everyone):
            pltpu.make_async_remote_copy(
                src_ref=sums.at[0], dst_ref=sums.at[d], send_sem=send2.at[0, 0], recv_sem=recv2.at[0, 0],
                device_id=any_id(d)[1], device_id_type=MESH).start()
        rest = sums.at[pl.ds(1, everyone - 1)]
        whole = pltpu.make_async_remote_copy(
            src_ref=rest, dst_ref=rest, send_sem=send2.at[0, 0], recv_sem=recv2.at[0, 0],
            device_id=any_id(1)[1], device_id_type=MESH)
        whole.wait_recv()
        partial = jnp.sum(sums[...], axis=0)
    else:
        partial = all_sum(partial, sums, send2.at[0], recv2.at[0], here, plane, plane_id)
        partial = all_sum(partial, sums2, send2.at[1], recv2.at[1], iy, ny, line_id)
    cells = float(cx * cy * cz * nx * ny * nz)
    scale_ref[...] = lax.rsqrt(jnp.full(scale_ref.shape, jnp.sum(partial), jnp.float32) / cells + 1e-06)
    for way, (rows, to) in sent_rows.items():
        pl.when(to)(bytes_of(rows, send.at[way], recv.at[0, 0]).wait_send)
    if near:
        whole.wait_send()


def finish(psi_ref, corr_ref, scale_ref, out_hbm, corr_hbm, scaled, sems):
    copies = [pltpu.make_async_copy(corr_ref, corr_hbm, sems.at[0])]
    copies[0].start()
    cx, cy, cz = psi_ref.shape
    scale = scale_ref[0:1]
    steps = 2 if cx % 2 == 0 else 1
    for n in range(steps):
        some = pl.ds(n * (cx // steps), cx // steps)
        scaled[some] = psi_ref[some] * scale.reshape(1, 1, cz)
        copies.append(pltpu.make_async_copy(scaled.at[some], out_hbm.at[some], sems.at[1 + n]))
        copies[-1].start()
    for copy in copies:
        copy.wait()


def shards(sizes, wave, external, weights):
    cx, cy, cz = wave.shape
    nx, ny, nz = sizes
    f32 = jnp.float32
    near = nx <= 4 and ny <= 4 and nz <= 2
    spare_rows = max(2 * (R + H) * cy, 2 * cx * (R + H), 2 * cx * R + 4 * R * R, 6 * cy + 12 * R)
    summed = nx * ny * nz if near else nx * nz
    stages, most = (1, 1) if near else (2, max(summed, ny))
    vmem = pl.BlockSpec(memory_space=pltpu.VMEM)
    stay = pl.BlockSpec(memory_space=pltpu.HBM)
    psi, corr, scale = pl.pallas_call(
        functools.partial(kernel, sizes),
        out_shape=(jax.ShapeDtypeStruct(wave.shape, f32), jax.ShapeDtypeStruct(wave.shape, f32),
                   jax.ShapeDtypeStruct((8, cz), f32)),
        in_specs=[stay, stay, stay],
        out_specs=(vmem, vmem, vmem),
        scratch_shapes=[
            pltpu.VMEM((cx + 2 * R, cy + 2 * R, cz), f32),
            pltpu.VMEM((cx + 2 * R, cy + 2 * R, cz), f32),
            pltpu.VMEM((cx, cy + 2 * R, cz), f32),
            pltpu.VMEM((cx, cy, cz), f32),
            pltpu.VMEM((SUBSTEPS - 1, cx + 2 * H, cy + 2 * R, cz), f32),
            pltpu.VMEM((cx, cy, cz), f32),
            pltpu.VMEM((cx, cy, cz), f32),
            pltpu.VMEM((SUBSTEPS + 1, 2, cy, cz), f32),
            pltpu.VMEM((SUBSTEPS + 1, 2, 3, cy + 2 * R, cz), f32),
            pltpu.VMEM((2, cy + 2 * R, cz), f32),
            pltpu.VMEM((SUBSTEPS - 1, 2, cx // 2, 2 * H, cz), f32),
            pltpu.VMEM((SUBSTEPS - 1, 2, cx // 2, 2 * H, cz), f32),
            pltpu.VMEM((3, 2 * cz, 2 * cz), jnp.bfloat16),
            pltpu.VMEM((2, 2, 4 * cz, 2 * cz), jnp.bfloat16),
            pltpu.VMEM((2, 2 * cz, 2 * cz), jnp.bfloat16),
            pltpu.VMEM((cy, cz), f32),
            pltpu.VMEM((spare_rows, cz), f32),
            pltpu.VMEM((cx, cy, cz), f32),
            pltpu.SMEM(weights.shape, f32),
            pltpu.VMEM((summed, 1, cz), f32),
            pltpu.VMEM((ny, 1, cz), f32),
            pltpu.SemaphoreType.DMA((len(PARTNERS),)),
            pltpu.SemaphoreType.DMA((2, len(FLAT) + 1 + SUBSTEPS // 2)),
            pltpu.SemaphoreType.DMA((stages, most)),
            pltpu.SemaphoreType.DMA((stages, most)),
            pltpu.SemaphoreType.DMA((3,)),
        ],
        compiler_params=pltpu.CompilerParams(collective_id=0, has_side_effects=True,
                                             vmem_limit_bytes=48 * 1024 * 1024),
    )(*[pltpu.with_memory_space_constraint(x, pltpu.HBM) for x in (weights, wave, external)])
    return pl.pallas_call(
        finish,
        out_shape=(jax.ShapeDtypeStruct(wave.shape, f32), jax.ShapeDtypeStruct(wave.shape, f32)),
        in_specs=[vmem, vmem, vmem],
        out_specs=(stay, stay),
        scratch_shapes=[pltpu.VMEM((cx, cy, cz), f32), pltpu.SemaphoreType.DMA((3,))],
    )(*[pltpu.with_memory_space_constraint(x, pltpu.VMEM) for x in (psi, corr, scale)])


def solution(mesh):
    sizes = tuple(mesh.shape[a] for a in AXES)
    spec = P(*AXES)
    return jax.shard_map(
        functools.partial(shards, sizes),
        mesh=mesh,
        in_specs=(spec, spec, P()),
        out_specs=(spec, spec),
        check_vma=False,
    )
```

```python
import functools

import jax
import jax.numpy as jnp
from jax import lax
from jax.experimental import pallas as pl
from jax.experimental.pallas import tpu as pltpu
from jax.sharding import PartitionSpec as P

SUBSTEPS = 3
LAP_COEF = (-205.0 / 72.0, 8.0 / 5.0, -1.0 / 5.0, 8.0 / 315.0, -1.0 / 560.0)
STEP = 0.08
AXES = ("gx", "gy", "gz")
MESH = pl.DeviceIdType.MESH
R = 8
H = 4


def lanes(shape):
    return lax.broadcasted_iota(jnp.int32, shape, len(shape) - 1)


PARTNERS = [(dx, dy, dz) for dx in (-1, 0, 1) for dy in (-1, 0, 1) for dz in (-1, 0, 1) if dx or dy or dz]
PARTNERS.sort(key=lambda d: d.count(0))
FLAT = [(dx, dy) for dx in (-1, 0, 1) for dy in (-1, 0, 1) if dx or dy]
GROUP = 4


def turn(value, shift):
    return value if isinstance(shift, int) and shift == 0 else pltpu.roll(value, shift, 1)


def modulo(a, n):
    return a % n if isinstance(a, int) else lax.rem(a, n)


def kernel(sizes, w_hbm, wave_hbm, ext_hbm, out_ref, corr_ref, scale_ref,
           wb, sb, yb, co, psi, va, part, pack, zin, zb, ypack, yin, bands, edges, blanks, spill, spare, ext_ref, w_ref,
           sums, sums2, send, recv, send2, recv2, local):
    nx, ny, nz = sizes
    cx, cy, cz = wave_hbm.shape
    wave_ref = wb.at[pl.ds(R, cx), pl.ds(R, cy)]
    get_wave = pltpu.make_async_copy(wave_hbm, wave_ref, local.at[0])
    get_ext = pltpu.make_async_copy(ext_hbm, ext_ref, local.at[1])
    get_weights = pltpu.make_async_copy(w_hbm, w_ref, local.at[2])
    get_wave.start()
    get_weights.start()
    ix, iy, iz = (lax.axis_index(a) for a in AXES)
    plane = nx * nz
    per = cz // cx
    here = ix * nz + iz

    def plane_id(d):
        t = lax.rem(here + d, plane)
        return t, {"gx": lax.div(t, nz), "gz": lax.rem(t, nz)}

    def line_id(d):
        t = lax.rem(iy + d, ny)
        return t, {"gy": t}

    barrier = pltpu.get_barrier_semaphore()

    def greet(ids):
        def body(d, c):
            pl.semaphore_signal(barrier, inc=1, device_id=ids(d)[1], device_id_type=MESH)
            return c
        return body

    near = nx <= 4 and ny <= 4 and nz <= 2

    def greet_partners(partners):
        count = 0
        for d3 in partners:
            there = None
            target = {}
            for name, d, i, n in zip(AXES, d3, (ix, iy, iz), sizes):
                if d:
                    ok = i < n - 1 if d > 0 else i > 0
                    there = ok if there is None else there & ok
                    target[name] = jnp.clip(i + d, 0, n - 1)
            count += there.astype(jnp.int32)

            @pl.when(there)
            def _(target=target):
                pl.semaphore_signal(barrier, inc=1, device_id=target, device_id_type=MESH)
        return count

    if near:
        guests = greet_partners(PARTNERS)
    else:
        guests = plane - 1 + ny - 1 + greet_partners([d for d in PARTNERS if d[1] and (d[0] or d[2])])
        lax.fori_loop(1, plane, greet(plane_id), 0)
        lax.fori_loop(1, ny, greet(line_id), 0)

    everyone = plane * ny
    order = (ix * ny + iy) * nz + iz
    others = [jnp.where(order + d < everyone, order + d, order + d - everyone) for d in range(1, everyone)] if near else []
    blanks[...] = jnp.zeros(blanks.shape, jnp.float32)
    pool = len(FLAT)
    sent_rows = {}
    spilled = [0]

    def rows_of(ref):
        count = 1
        for n in ref.shape[:-1]:
            count *= n
        return count

    def message(src, dst, dx, dy, dz, group):
        to, back = None, None
        for d, i, n in ((dx, ix, nx), (dy, iy, ny), (dz, iz, nz)):
            if d > 0:
                a, b = i < n - 1, i > 0
            elif d < 0:
                a, b = i > 0, i < n - 1
            else:
                continue
            to = a if to is None else to & a
            back = b if back is None else back & b
        target = {}
        for name, d, i, n in zip(AXES, (dx, dy, dz), (ix, iy, iz), sizes):
            if d:
                target[name] = jnp.clip(i + d, 0, n - 1)
        way = pool if dz else FLAT.index((dx, dy))
        rows, _ = sent_rows.get(way, (0, None))
        sent_rows[way] = rows + rows_of(dst), None if dz else to
        copy = pltpu.make_async_remote_copy(
            src_ref=src, dst_ref=dst, send_sem=send.at[way],
            recv_sem=recv.at[group % 2, pool + group // 2 if dz else way],
            device_id=target, device_id_type=MESH)
        return copy, to, back, dst, dz, group, way

    def start(messages):
        for copy, to, *_ in messages:
            pl.when(to)(copy.start)

    def blank(messages):
        for _, to, back, dst, dz, group, _ in messages:
            if dz:
                some = pl.ds(0, dst.shape[0])
                waste = spill.at[pl.ds(spilled[0], dst.shape[0])]
                spilled[0] += dst.shape[0]
                pl.when(jnp.logical_not(to))(pltpu.make_async_copy(blanks.at[some], waste, send.at[pool]).start)

            @pl.when(jnp.logical_not(back))
            def _(dst=dst, dz=dz, group=group):
                if dz:
                    pltpu.make_async_copy(blanks.at[pl.ds(0, dst.shape[0])], dst, recv.at[group % 2, pool + group // 2]).start()
                else:
                    dst[...] = jnp.zeros(dst.shape, dst.dtype)

    def bytes_of(rows, send_sem, recv_sem):
        some = spare.at[pl.ds(0, rows)]
        return pltpu.make_async_remote_copy(
            src_ref=some, dst_ref=some, send_sem=send_sem, recv_sem=recv_sem,
            device_id={"gx": ix}, device_id_type=MESH)

    def arrive(messages):
        rows, waits = {}, {}
        for _, _, back, dst, dz, group, way in messages:
            rows[way] = rows.get(way, 0) + rows_of(dst)
            waits[way] = None if dz else back, recv.at[group % 2, way + group // 2 if dz else way]
        for way, (back, sem) in waits.items():
            wait = bytes_of(rows[way], send.at[0], sem).wait_recv
            if back is None:
                wait()
            else:
                pl.when(back)(wait)

    at = lanes((cy, cz))
    zero = jnp.zeros((cy, cz), jnp.float32)

    slot_of = lax.div(at, per)

    def pack_one(i, value, packs):
        moved = turn(value, modulo(per * i, cz))
        return jnp.where(slot_of == i, moved, packs[0]), jnp.where(slot_of == (i - 1) % cx, moved, packs[1])

    def pack_out(slot, packs):
        pack[slot, 0] = packs[0]
        pack[slot, 1] = packs[1]

    def z_messages(slot, dxs, dys, group):
        out = []
        for dx in dxs:
            for dy in dys:
                if dy > 0:
                    rows, into = pl.ds(cy - R, R), pl.ds(0, R)
                elif dy < 0:
                    rows, into = pl.ds(0, R), pl.ds(R + cy, R)
                else:
                    rows, into = pl.ds(0, cy), pl.ds(R, cy)
                out.append(message(pack.at[slot, 1, rows], zin.at[slot, 0, 1 - dx, into], dx, dy, 1, group))
                out.append(message(pack.at[slot, 0, rows], zin.at[slot, 1, 1 - dx, into], dx, dy, -1, group))
        return out

    def side_messages(src, dst, moves, group, part=0, parts=1):
        out = []
        for dx, dy in moves:
            if dx > 0:
                sx, tx = pl.ds(cx - R, R), pl.ds(0, R)
            elif dx < 0:
                sx, tx = pl.ds(0, R), pl.ds(R + cx, R)
            else:
                some = cx // parts
                sx, tx = pl.ds(part * some, some), pl.ds(R + part * some, some)
            if dy > 0:
                sy, ty = pl.ds(cy - R, R), pl.ds(0, R)
            elif dy < 0:
                sy, ty = pl.ds(0, R), pl.ds(R + cy, R)
            else:
                some = cy // parts
                sy, ty = pl.ds(part * some, some), pl.ds(R + part * some, some)
            out.append(message(src.at[sx, sy], dst.at[tx, ty], dx, dy, 0, group))
        return out

    face_x = [(dx, 0) for dx in (1, -1)]
    face_y = [(0, dy) for dy in (1, -1)]
    edge_xy = [(dx, dy) for dx in (1, -1) for dy in (1, -1)]
    src_ref = sb.at[pl.ds(R, cx), pl.ds(R, cy)]
    wave_x1, wave_x2 = (side_messages(wave_hbm, wb, face_x, 0, n, 2) for n in range(2))
    wave_y1, wave_y2 = (side_messages(wave_hbm, wb, face_y, 0, n, 2) for n in range(2))
    src_x, src_y = side_messages(src_ref, sb, face_x, 1), side_messages(src_ref, sb, face_y, 1)
    wave_xy, src_xy = side_messages(wave_hbm, wb, edge_xy, 0), side_messages(src_ref, sb, edge_xy, 1)
    wave_z, src_z = z_messages(0, (-1, 0, 1), (0,), 0), z_messages(1, (-1, 0, 1), (0,), 1)
    wave_e, src_e = z_messages(0, (-1, 0, 1), (-1, 1), 0), z_messages(1, (-1, 0, 1), (-1, 1), 1)

    psi_moves = []
    for s in range(SUBSTEPS - 1):
        buf = psi.at[s]
        moves = [
            message(buf.at[pl.ds(cx, H), pl.ds(R, cy)], buf.at[pl.ds(0, H), pl.ds(R, cy)], 1, 0, 0, 2 + s),
            message(buf.at[pl.ds(H, H), pl.ds(R, cy)], buf.at[pl.ds(H + cx, H), pl.ds(R, cy)], -1, 0, 0, 2 + s),
        ]
        moves += [
            message(ypack.at[s, 1], yin.at[s, 0], 0, 1, 0, 2 + s),
            message(ypack.at[s, 0], yin.at[s, 1], 0, -1, 0, 2 + s),
        ]
        moves += z_messages(2 + s, (0,), (0,), 2 + s)
        psi_moves.append(moves)

    pl.semaphore_wait(barrier, guests)
    start(wave_x1 + wave_y1)
    get_wave.wait()
    packs = (zero, zero)
    for i in range(cx):
        packs = pack_one(i, wave_ref[i], packs)
    pack_out(0, packs)
    start(wave_e + wave_z + wave_x2 + wave_y2 + wave_xy)
    wave_x, wave_y = wave_x1 + wave_x2, wave_y1 + wave_y2
    get_ext.start()
    for group in [wave_x, wave_y, wave_xy, wave_z, wave_e, src_x, src_y, src_xy, src_z, src_e] + psi_moves:
        blank(group)
    get_weights.wait()

    def taps_of(dim, flip):
        return [(k, w_ref[dim, R - k if flip else R + k]) for k in range(-R, R + 1)]

    row = lax.broadcasted_iota(jnp.int32, (cz, cz), 0)
    gap = row - lanes((cz, cz))
    gains = [STEP * 0.5 * c for c in LAP_COEF]
    z_taps = [taps_of(2, False), taps_of(2, True), [(k, gains[abs(k)]) for k in range(-H, H + 1) if k]]

    def halves(a):
        high = a.astype(jnp.bfloat16)
        return high, (a - high.astype(jnp.float32)).astype(jnp.bfloat16)

    def keep(ref, index, a):
        high, low = halves(a)
        k = a.shape[0]
        ref[(*index, pl.ds(0, k), pl.ds(0, cz))] = high
        ref[(*index, pl.ds(0, k), pl.ds(cz, cz))] = low
        ref[(*index, pl.ds(k, k), pl.ds(0, cz))] = high
        ref[(*index, pl.ds(k, k), pl.ds(cz, cz))] = jnp.zeros_like(low)

    def dot(a, b):
        both = jnp.dot(jnp.concatenate(halves(a), 1), b, preferred_element_type=jnp.float32)
        return both[:, :cz] + both[:, cz:]

    for slot, taps in enumerate(z_taps):
        inner = jnp.zeros((cz, cz), jnp.float32)
        for k, tap in taps:
            inner = jnp.where(gap == k, tap, inner)
        keep(bands, (slot,), inner)

    tile = (per, cz)
    lane = lanes(tile)
    cell = lax.rem(lane, per)
    apart = lax.broadcasted_iota(jnp.int32, tile, 0) - cell
    group_of = lax.div(lane, per)
    owner = [group_of, lax.rem(group_of + 1, cx)]
    none = jnp.zeros(tile, jnp.float32)

    def corner(side, taps):
        shift = per if side == 0 else -per
        made = none
        for k, tap in taps:
            made = jnp.where(apart == k + shift, tap, made)
        return made

    for flip in range(2):
        taps = dict(taps_of(0, bool(flip)))
        for side in range(2):
            by_z = corner(side, [(k, tap) for k, tap in z_taps[flip] if (k < 0) == (side == 0) and k])
            is_owner = [owner[side] == q for q in range(cx)]
            rows = []
            for t in range(2 * cx):
                at_plane = (t + 1 - side) % cx
                if t >= cx:
                    at_plane += cx if at_plane < cx // 2 else -cx
                by_x = none
                for q in range(cx):
                    if at_plane - q in taps:
                        by_x = jnp.where(is_owner[q], taps[at_plane - q], by_x)
                rows.append(by_x * by_z)
            keep(edges, (flip, side), jnp.concatenate(rows, 0))
    even = lax.rem(lax.div(at, per), 2) == 0

    def rim_pair(sides):
        return jnp.where(even, sides[0], sides[1]), jnp.where(even, sides[1], sides[0])

    def from_rim(pair, i, width):
        return jnp.where((at < width) | (at >= cz - width), turn(pair[i % 2], modulo(cz - per * i, cz)), zero)

    def planes(buf, first, count, rows):
        return buf[pl.ds(first, count), rows].reshape(count * rows.size, cz)

    def smear(src, slot, square, flip, faces, packs_in, late):
        taps_x, taps_y = taps_of(0, flip), taps_of(1, flip)

        def load(k, first):
            v = src[k, pl.ds(R + first, 8)]
            return v * v if square else v

        def along_x(first, own, other, init):
            ins = {k: load(k, first) for k in range(cx + 2 * R) if (own if R <= k < R + cx else other)}
            for i in range(cx):
                total = yb[i, pl.ds(R + first, 8)] if init else None
                for k, tap in taps_x:
                    if i + R + k in ins:
                        part_ = ins[i + R + k] * tap
                        total = part_ if total is None else total + part_
                if total is not None:
                    yb[i, pl.ds(R + first, 8)] = total

        for first in range(0, cy, 8):
            along_x(first, True, False, False)
        arrive(faces)
        for first in range(0, cy, 8):
            along_x(first, False, True, True)
        own = pl.ds(R, cy)
        for g in range(0, cx, cx // 2):
            yb[pl.ds(g, cx // 2), own] = dot(planes(yb, g, cx // 2, own), bands[int(flip)]).reshape(cx // 2, cy, cz)
        for i in range(cx):
            low = mid = high = None
            for k, tap in taps_y:
                a = yb[i, pl.ds(R + 8 + k, cy - 16)] * tap
                mid = a if mid is None else mid + a
                if k >= 0:
                    a = yb[i, pl.ds(R + k, 8)] * tap
                    low = a if low is None else low + a
                if k <= 0:
                    a = yb[i, pl.ds(R + cy - 8 + k, 8)] * tap
                    high = a if high is None else high + a
            co[i] = jnp.concatenate([low, mid, high], 0)
        arrive(packs_in)
        wide_slot = lax.div(lanes((cy + 2 * R, cz)), per)
        for side in range(2):
            wide = lax.rem(wide_slot + 1 - side, cx) < cx // 2
            mine = zin[slot, side, 1]
            other = jnp.where(wide, zin[slot, side, 2], zin[slot, side, 0])
            if square:
                mine, other = mine * mine, other * other
            zb[side] = dot(jnp.concatenate([mine, other], 1), edges[int(flip), side])
        pair = []
        for side in range(2):
            total = zero
            for k, tap in taps_y:
                total = total + zb[side, pl.ds(R + k, cy)] * tap
            pair.append(total)
        pair = rim_pair(pair)
        arrive(late)
        for first in (-8, cy):
            along_x(first, True, True, False)
            rows = pl.ds(R + first, 8)
            yb[:, rows] = dot(planes(yb, 0, cx, rows), bands[int(flip)]).reshape(cx, 8, cz)

        def result(i):
            total = co[i] + from_rim(pair, i, R)
            low, high = total[:8], total[cy - 8:]
            for k, tap in taps_y:
                if k < 0:
                    low = low + yb[i, pl.ds(R + k, 8)] * tap
                if k > 0:
                    high = high + yb[i, pl.ds(R + cy - 8 + k, 8)] * tap
            return jnp.concatenate([low, total[8:cy - 8], high], 0)

        return result

    smeared = smear(wb, 0, True, False, wave_x, wave_z + wave_e, wave_y + wave_xy)
    packs = (zero, zero)
    for i in range(cx):
        coarse = smeared(i)
        value = wave_ref[i]
        dens = value * value
        both = coarse * coarse
        source = 0.5 * dens * both - dens * coarse
        corr_ref[i] = (0.5 / 3.0) * both * coarse - 0.5 * both
        sb[R + i, pl.ds(R, cy)] = source
        packs = pack_one(i, source, packs)
    pack_out(1, packs)
    start(src_e + src_z + src_x + src_y + src_xy)

    cell_of = lax.rem(at, per)

    def z_rim(slot):
        low, high = (zin[slot, side, 1, pl.ds(R, cy)] for side in range(2))
        made = [zero, zero]
        for k in range(1, H + 1):
            made[0] = made[0] + gains[k] * jnp.where(cell_of < k, turn(low, k), zero)
            made[1] = made[1] + gains[k] * jnp.where(cell_of >= per - k, turn(high, cz - k), zero)
        return rim_pair(made)

    def own_part(buf, reach, weight, first_step):
        pair = z_rim(0) if first_step else None
        own = pl.ds(R, cy)
        step = 2 * GROUP
        for g in range(0, cx, step):
            along = dot(planes(buf, reach + g, step, own), bands[2])
            for i in range(g, g + step):
                total = buf[reach + i, own] * weight(i) + along[(i - g) * cy:(i - g + 1) * cy]
                if first_step:
                    total = total + from_rim(pair, i, H)
                for k in range(1, H + 1):
                    pairs = [buf[reach + j, own] for j in (i - k, i + k) if first_step or 0 <= j < cx]
                    if first_step:
                        pairs += [buf[reach + i, pl.ds(R + j, cy)] for j in (-k, k)]
                    both = pairs[0]
                    for p in pairs[1:]:
                        both = both + p
                    total = total + gains[k] * both
                if not first_step:
                    up = down = None
                    for k in range(1, H + 1):
                        a = gains[k] * buf[reach + i, pl.ds(R + k, cy - 8)]
                        b = gains[k] * buf[reach + i, pl.ds(R + 8 - k, cy - 8)]
                        up, down = (a, b) if up is None else (up + a, down + b)
                    total = total + jnp.concatenate([up[:8], up[8:] + down[:cy - 16], down[cy - 16:]], 0)
                part[i] = total

    def halo_part(buf, pair, i):
        total = part[i]
        for k in range(1, H + 1):
            for j in (i - k, i + k):
                if not 0 <= j < cx:
                    total = total + gains[k] * buf[H + j, pl.ds(R, cy)]
        low, high = total[:8], total[cy - 8:]
        for k in range(1, H + 1):
            low = low + gains[k] * buf[H + i, pl.ds(R - k, 8)]
            high = high + gains[k] * buf[H + i, pl.ds(R + cy - 8 + k, 8)]
        return jnp.concatenate([low, total[8:cy - 8], high], 0) + from_rim(pair, i, H)

    middle = 1.0 + STEP * 0.5 * 3.0 * LAP_COEF[0]
    own_part(wb, R, lambda i: middle, True)
    smeared = smear(sb, 1, False, True, src_x, src_z + src_e, src_y + src_xy)
    get_ext.wait()
    groups = [list(range(g, g + GROUP)) for g in range(0, cx, GROUP)]
    groups = groups[:1] + groups[-1:] + groups[1:-1]

    def first_step(i):
        corr = corr_ref[i] + smeared(i)
        corr_ref[i] = corr
        felt = STEP * (corr + ext_ref[i])
        va[i] = middle - felt
        return part[i] - felt * wave_ref[i]

    def send_out(s, step):
        after = psi.at[s]
        packs = (zero, zero)
        for n_, these in enumerate(groups):
            for i in these:
                value = step(i)
                after[H + i, pl.ds(R, cy)] = value
                packs = pack_one(i, value, packs)
                half = pl.ds(H * (i % 2), H)
                ypack[s, 0, i // 2, half] = value[:H]
                ypack[s, 1, i // 2, half] = value[cy - H:]
            if n_ == 1:
                start(psi_moves[s][:2])
        pack_out(2 + s, packs)
        start(psi_moves[s][2:])

    send_out(0, first_step)
    total = zero
    for s in range(SUBSTEPS - 1):
        buf = psi.at[s]
        own_part(buf, H, lambda i: va[i], False)
        arrive(psi_moves[s])
        pair = z_rim(2 + s)
        for i in range(cx):
            half = pl.ds(H * (i % 2), H)
            buf[H + i, pl.ds(R - H, H)] = yin[s, 0, i // 2, half]
            buf[H + i, pl.ds(R + cy, H)] = yin[s, 1, i // 2, half]
        if s < SUBSTEPS - 2:
            send_out(s + 1, lambda i: halo_part(buf, pair, i))
        else:
            for i in range(cx):
                value = halo_part(buf, pair, i)
                out_ref[i] = value
                total = total + value * value

    partial = jnp.sum(total, axis=0, keepdims=True)
    def all_sum(value, slots, ssem, rsem, me, n, ids):
        if n == 1:
            return value
        slots[me] = value

        def copy_of(d, slot):
            return pltpu.make_async_remote_copy(
                src_ref=slots.at[me], dst_ref=slots.at[slot], send_sem=ssem.at[d], recv_sem=rsem.at[slot],
                device_id=ids(d)[1], device_id_type=MESH)

        def go(d, c):
            copy_of(d, me).start()
            return c

        def come(d, c):
            copy_of(d, ids(d)[0]).wait_recv()
            return c

        def left(d, c):
            copy_of(d, me).wait_send()
            return c

        lax.fori_loop(1, n, go, 0)
        lax.fori_loop(1, n, come, 0)
        total = jnp.sum(slots[...], axis=0)
        lax.fori_loop(1, n, left, 0)
        return total

    if near:
        sums[0] = partial
        for d in range(1, everyone):
            pltpu.make_async_remote_copy(
                src_ref=sums.at[0], dst_ref=sums.at[d], send_sem=send2.at[0, 0], recv_sem=recv2.at[0, 0],
                device_id=others[d - 1], device_id_type=pl.DeviceIdType.LOGICAL).start()
        rest = sums.at[pl.ds(1, everyone - 1)]
        whole = pltpu.make_async_remote_copy(
            src_ref=rest, dst_ref=rest, send_sem=send2.at[0, 0], recv_sem=recv2.at[0, 0],
            device_id=others[0], device_id_type=pl.DeviceIdType.LOGICAL)
        whole.wait_recv()
        partial = jnp.sum(sums[...], axis=0)
    else:
        partial = all_sum(partial, sums, send2.at[0], recv2.at[0], here, plane, plane_id)
        partial = all_sum(partial, sums2, send2.at[1], recv2.at[1], iy, ny, line_id)
    cells = float(cx * cy * cz * nx * ny * nz)
    scale_ref[...] = lax.rsqrt(jnp.broadcast_to(jnp.sum(partial, axis=1, keepdims=True), scale_ref.shape) / cells + 1e-06)
    for way, (rows, to) in sent_rows.items():
        left = bytes_of(rows, send.at[way], recv.at[0, 0]).wait_send
        if to is None:
            left()
        else:
            pl.when(to)(left)
    if near:
        whole.wait_send()


def finish(psi_ref, corr_ref, scale_ref, out_hbm, corr_hbm, scaled, sems):
    copies = [pltpu.make_async_copy(corr_ref, corr_hbm, sems.at[0])]
    copies[0].start()
    cx, cy, cz = psi_ref.shape
    scale = scale_ref[0:1]
    steps = 2 if cx % 2 == 0 else 1
    for n in range(steps):
        some = pl.ds(n * (cx // steps), cx // steps)
        scaled[some] = psi_ref[some] * scale.reshape(1, 1, cz)
        copies.append(pltpu.make_async_copy(scaled.at[some], out_hbm.at[some], sems.at[1 + n]))
        copies[-1].start()
    for copy in copies:
        copy.wait()


def shards(sizes, wave, external, weights):
    cx, cy, cz = wave.shape
    nx, ny, nz = sizes
    f32 = jnp.float32
    near = nx <= 4 and ny <= 4 and nz <= 2
    spare_rows = max(2 * (R + H) * cy, 2 * cx * (R + H), 2 * cx * R + 4 * R * R, 6 * cy + 12 * R, 2 * (6 * cy + 12 * R) + 4 * cy)
    summed = nx * ny * nz if near else nx * nz
    stages, most = (1, 1) if near else (2, max(summed, ny))
    vmem = pl.BlockSpec(memory_space=pltpu.VMEM)
    stay = pl.BlockSpec(memory_space=pltpu.HBM)
    psi, corr, scale = pl.pallas_call(
        functools.partial(kernel, sizes),
        out_shape=(jax.ShapeDtypeStruct(wave.shape, f32), jax.ShapeDtypeStruct(wave.shape, f32),
                   jax.ShapeDtypeStruct((8, cz), f32)),
        in_specs=[stay, stay, stay],
        out_specs=(vmem, vmem, vmem),
        scratch_shapes=[
            pltpu.VMEM((cx + 2 * R, cy + 2 * R, cz), f32),
            pltpu.VMEM((cx + 2 * R, cy + 2 * R, cz), f32),
            pltpu.VMEM((cx, cy + 2 * R, cz), f32),
            pltpu.VMEM((cx, cy, cz), f32),
            pltpu.VMEM((SUBSTEPS - 1, cx + 2 * H, cy + 2 * R, cz), f32),
            pltpu.VMEM((cx, cy, cz), f32),
            pltpu.VMEM((cx, cy, cz), f32),
            pltpu.VMEM((SUBSTEPS + 1, 2, cy, cz), f32),
            pltpu.VMEM((SUBSTEPS + 1, 2, 3, cy + 2 * R, cz), f32),
            pltpu.VMEM((2, cy + 2 * R, cz), f32),
            pltpu.VMEM((SUBSTEPS - 1, 2, cx // 2, 2 * H, cz), f32),
            pltpu.VMEM((SUBSTEPS - 1, 2, cx // 2, 2 * H, cz), f32),
            pltpu.VMEM((3, 2 * cz, 2 * cz), jnp.bfloat16),
            pltpu.VMEM((2, 2, 4 * cz, 2 * cz), jnp.bfloat16),
            pltpu.VMEM((cy, cz), f32),
            pltpu.VMEM((2 * (6 * cy + 12 * R) + 2 * (SUBSTEPS - 1) * cy, cz), f32),
            pltpu.VMEM((spare_rows, cz), f32),
            pltpu.VMEM((cx, cy, cz), f32),
            pltpu.SMEM(weights.shape, f32),
            pltpu.VMEM((summed, 1, cz), f32),
            pltpu.VMEM((ny, 1, cz), f32),
            pltpu.SemaphoreType.DMA((len(FLAT) + 1,)),
            pltpu.SemaphoreType.DMA((2, len(FLAT) + 1 + SUBSTEPS // 2)),
            pltpu.SemaphoreType.DMA((stages, most)),
            pltpu.SemaphoreType.DMA((stages, most)),
            pltpu.SemaphoreType.DMA((3,)),
        ],
        compiler_params=pltpu.CompilerParams(collective_id=0, has_side_effects=True,
                                             vmem_limit_bytes=48 * 1024 * 1024),
    )(*[pltpu.with_memory_space_constraint(x, pltpu.HBM) for x in (weights, wave, external)])
    return pl.pallas_call(
        finish,
        out_shape=(jax.ShapeDtypeStruct(wave.shape, f32), jax.ShapeDtypeStruct(wave.shape, f32)),
        in_specs=[vmem, vmem, vmem],
        out_specs=(stay, stay),
        scratch_shapes=[pltpu.VMEM((cx, cy, cz), f32), pltpu.SemaphoreType.DMA((3,))],
    )(*[pltpu.with_memory_space_constraint(x, pltpu.VMEM) for x in (psi, corr, scale)])


def solution(mesh):
    sizes = tuple(mesh.shape[a] for a in AXES)
    spec = P(*AXES)
    return jax.shard_map(
        functools.partial(shards, sizes),
        mesh=mesh,
        in_specs=(spec, spec, P()),
        out_specs=(spec, spec),
        check_vma=False,
    )
```

```python
import functools

import jax
import jax.numpy as jnp
from jax import lax
from jax.experimental import pallas as pl
from jax.experimental.pallas import tpu as pltpu
from jax.sharding import PartitionSpec as P

SUBSTEPS = 3
LAP_COEF = (-205.0 / 72.0, 8.0 / 5.0, -1.0 / 5.0, 8.0 / 315.0, -1.0 / 560.0)
STEP = 0.08
AXES = ("gx", "gy", "gz")
MESH = pl.DeviceIdType.MESH
R = 8
H = 4


def lanes(shape):
    return lax.broadcasted_iota(jnp.int32, shape, len(shape) - 1)


PARTNERS = [(dx, dy, dz) for dx in (-1, 0, 1) for dy in (-1, 0, 1) for dz in (-1, 0, 1) if dx or dy or dz]
PARTNERS.sort(key=lambda d: d.count(0))
FLAT = [(dx, dy) for dx in (-1, 0, 1) for dy in (-1, 0, 1) if dx or dy]
GROUP = 4


def turn(value, shift):
    return value if isinstance(shift, int) and shift == 0 else pltpu.roll(value, shift, 1)


def modulo(a, n):
    return a % n if isinstance(a, int) else lax.rem(a, n)


def kernel(sizes, w_hbm, wave_hbm, ext_hbm, out_ref, corr_ref, scale_ref,
           wb, sb, yb, co, pb, psi, va, part, pack, zin, zb, vx, ypack, yin, bands, edges, blanks, spill, spare, ext_ref, w_ref,
           sums, sums2, send, recv, send2, recv2, local):
    nx, ny, nz = sizes
    cx, cy, cz = wave_hbm.shape
    wave_ref = wb.at[pl.ds(R, cx), pl.ds(R, cy)]
    get_wave = pltpu.make_async_copy(wave_hbm, wave_ref, local.at[0])
    get_ext = pltpu.make_async_copy(ext_hbm, ext_ref, local.at[1])
    get_weights = pltpu.make_async_copy(w_hbm, w_ref, local.at[2])
    get_wave.start()
    get_weights.start()
    ix, iy, iz = (lax.axis_index(a) for a in AXES)
    plane = nx * nz
    per = cz // cx
    here = ix * nz + iz

    def plane_id(d):
        t = lax.rem(here + d, plane)
        return t, {"gx": lax.div(t, nz), "gz": lax.rem(t, nz)}

    def line_id(d):
        t = lax.rem(iy + d, ny)
        return t, {"gy": t}

    barrier = pltpu.get_barrier_semaphore()

    def greet(ids):
        def body(d, c):
            pl.semaphore_signal(barrier, inc=1, device_id=ids(d)[1], device_id_type=MESH)
            return c
        return body

    near = nx <= 4 and ny <= 4 and nz <= 2

    def greet_partners(partners):
        count = 0
        for d3 in partners:
            there = None
            target = {}
            for name, d, i, n in zip(AXES, d3, (ix, iy, iz), sizes):
                if d:
                    ok = i < n - 1 if d > 0 else i > 0
                    there = ok if there is None else there & ok
                    target[name] = jnp.clip(i + d, 0, n - 1)
            count += there.astype(jnp.int32)

            @pl.when(there)
            def _(target=target):
                pl.semaphore_signal(barrier, inc=1, device_id=target, device_id_type=MESH)
        return count

    if near:
        guests = greet_partners(PARTNERS)
    else:
        guests = plane - 1 + ny - 1 + greet_partners([d for d in PARTNERS if d[1] and (d[0] or d[2])])
        lax.fori_loop(1, plane, greet(plane_id), 0)
        lax.fori_loop(1, ny, greet(line_id), 0)

    everyone = plane * ny
    order = (ix * ny + iy) * nz + iz
    others = [jnp.where(order + d < everyone, order + d, order + d - everyone) for d in range(1, everyone)] if near else []
    blanks[...] = jnp.zeros(blanks.shape, jnp.float32)
    pool = len(FLAT)
    sent_rows = {}
    spilled = [0]

    def rows_of(ref):
        count = 1
        for n in ref.shape[:-1]:
            count *= n
        return count

    def message(src, dst, dx, dy, dz, group):
        to, back = None, None
        for d, i, n in ((dx, ix, nx), (dy, iy, ny), (dz, iz, nz)):
            if d > 0:
                a, b = i < n - 1, i > 0
            elif d < 0:
                a, b = i > 0, i < n - 1
            else:
                continue
            to = a if to is None else to & a
            back = b if back is None else back & b
        target = {}
        for name, d, i, n in zip(AXES, (dx, dy, dz), (ix, iy, iz), sizes):
            if d:
                target[name] = jnp.clip(i + d, 0, n - 1)
        way = pool if dz else FLAT.index((dx, dy))
        rows, _ = sent_rows.get(way, (0, None))
        sent_rows[way] = rows + rows_of(dst), None if dz else to
        copy = pltpu.make_async_remote_copy(
            src_ref=src, dst_ref=dst, send_sem=send.at[way],
            recv_sem=recv.at[group % 2, pool + group // 2 if dz else way],
            device_id=target, device_id_type=MESH)
        return copy, to, back, dst, dz, group, way

    def start(messages):
        for copy, to, *_ in messages:
            pl.when(to)(copy.start)

    def blank(messages):
        for _, to, back, dst, dz, group, _ in messages:
            if dz:
                some = pl.ds(0, dst.shape[0])
                waste = spill.at[pl.ds(spilled[0], dst.shape[0])]
                spilled[0] += dst.shape[0]
                pl.when(jnp.logical_not(to))(pltpu.make_async_copy(blanks.at[some], waste, send.at[pool]).start)

            @pl.when(jnp.logical_not(back))
            def _(dst=dst, dz=dz, group=group):
                if dz:
                    pltpu.make_async_copy(blanks.at[pl.ds(0, dst.shape[0])], dst, recv.at[group % 2, pool + group // 2]).start()
                else:
                    dst[...] = jnp.zeros(dst.shape, dst.dtype)

    def bytes_of(rows, send_sem, recv_sem):
        some = spare.at[pl.ds(0, rows)]
        return pltpu.make_async_remote_copy(
            src_ref=some, dst_ref=some, send_sem=send_sem, recv_sem=recv_sem,
            device_id={"gx": ix}, device_id_type=MESH)

    def arrive(messages):
        rows, waits = {}, {}
        for _, _, back, dst, dz, group, way in messages:
            rows[way] = rows.get(way, 0) + rows_of(dst)
            waits[way] = None if dz else back, recv.at[group % 2, way + group // 2 if dz else way]
        for way, (back, sem) in waits.items():
            wait = bytes_of(rows[way], send.at[0], sem).wait_recv
            if back is None:
                wait()
            else:
                pl.when(back)(wait)

    at = lanes((cy, cz))
    zero = jnp.zeros((cy, cz), jnp.float32)

    slot_of = lax.div(at, per)

    def pack_one(i, value, packs):
        moved = turn(value, modulo(per * i, cz))
        return jnp.where(slot_of == i, moved, packs[0]), jnp.where(slot_of == (i - 1) % cx, moved, packs[1])

    def pack_out(slot, packs):
        pack[slot, 0] = packs[0]
        pack[slot, 1] = packs[1]

    def z_messages(slot, dxs, dys, group):
        out = []
        for dx in dxs:
            for dy in dys:
                if dy > 0:
                    rows, into = pl.ds(cy - R, R), pl.ds(0, R)
                elif dy < 0:
                    rows, into = pl.ds(0, R), pl.ds(R + cy, R)
                else:
                    rows, into = pl.ds(0, cy), pl.ds(R, cy)
                out.append(message(pack.at[slot, 1, rows], zin.at[slot, 0, 1 - dx, into], dx, dy, 1, group))
                out.append(message(pack.at[slot, 0, rows], zin.at[slot, 1, 1 - dx, into], dx, dy, -1, group))
        return out

    def side_messages(src, dst, moves, group, part=0, parts=1, wide=R):
        out = []
        for dx, dy in moves:
            if dx > 0:
                sx, tx = pl.ds(cx - wide, wide), pl.ds(R - wide, wide)
            elif dx < 0:
                sx, tx = pl.ds(0, wide), pl.ds(R + cx, wide)
            else:
                some = cx // parts
                sx, tx = pl.ds(part * some, some), pl.ds(R + part * some, some)
            if dy > 0:
                sy, ty = pl.ds(cy - R, R), pl.ds(0, R)
            elif dy < 0:
                sy, ty = pl.ds(0, R), pl.ds(R + cy, R)
            else:
                some = cy // parts
                sy, ty = pl.ds(part * some, some), pl.ds(R + part * some, some)
            out.append(message(src.at[sx, sy], dst.at[tx, ty], dx, dy, 0, group))
        return out

    face_x = [(dx, 0) for dx in (1, -1)]
    face_y = [(0, dy) for dy in (1, -1)]
    edge_xy = [(dx, dy) for dx in (1, -1) for dy in (1, -1)]
    src_ref = sb.at[pl.ds(R, cx), pl.ds(R, cy)]
    wave_x1, wave_x2 = (side_messages(wave_hbm, wb, face_x, 0, n, 2) for n in range(2))
    wave_y1, wave_y2 = (side_messages(wave_hbm, wb, face_y, 0, n, 2) for n in range(2))
    src_x, src_y = side_messages(src_ref, sb, face_x, 1), side_messages(src_ref, sb, face_y, 1)
    wave_xy, src_xy = side_messages(wave_hbm, wb, edge_xy, 0), side_messages(src_ref, sb, edge_xy, 1)
    wave_z, src_z = z_messages(0, (-1, 0, 1), (0,), 0), z_messages(1, (-1, 0, 1), (0,), 1)
    wave_e, src_e = z_messages(0, (-1, 0, 1), (-1, 1), 0), z_messages(1, (-1, 0, 1), (-1, 1), 1)

    own_psi = pb.at[pl.ds(R, cx), pl.ds(R, cy)]
    psi_x = side_messages(own_psi, pb, face_x, 2) + [
        message(va.at[pl.ds(cx - H, H)], vx.at[0], 1, 0, 0, 2),
        message(va.at[pl.ds(0, H)], vx.at[1], -1, 0, 0, 2),
    ]
    psi_y = side_messages(own_psi, pb, face_y, 2) + [
        message(ypack.at[1], yin.at[0], 0, 1, 0, 2),
        message(ypack.at[0], yin.at[1], 0, -1, 0, 2),
    ] + side_messages(own_psi, pb, edge_xy, 2, wide=H)
    psi_z = z_messages(2, (-1, 0, 1), (0,), 2) + z_messages(2, (0,), (-1, 1), 2) + z_messages(3, (0,), (0,), 2)
    psi_moves = psi_z + psi_x + psi_y

    pl.semaphore_wait(barrier, guests)
    start(wave_x1 + wave_y1)
    get_wave.wait()
    packs = (zero, zero)
    for i in range(cx):
        packs = pack_one(i, wave_ref[i], packs)
    pack_out(0, packs)
    start(wave_e + wave_z + wave_x2 + wave_y2 + wave_xy)
    wave_x, wave_y = wave_x1 + wave_x2, wave_y1 + wave_y2
    get_ext.start()
    for group in [wave_x, wave_y, wave_xy, wave_z, wave_e, src_x, src_y, src_xy, src_z, src_e, psi_moves]:
        blank(group)
    get_weights.wait()

    def taps_of(dim, flip):
        return [(k, w_ref[dim, R - k if flip else R + k]) for k in range(-R, R + 1)]

    row = lax.broadcasted_iota(jnp.int32, (cz, cz), 0)
    gap = row - lanes((cz, cz))
    gains = [STEP * 0.5 * c for c in LAP_COEF]
    z_taps = [taps_of(2, False), taps_of(2, True), [(k, gains[abs(k)]) for k in range(-H, H + 1) if k]]

    def halves(a):
        high = a.astype(jnp.bfloat16)
        return high, (a - high.astype(jnp.float32)).astype(jnp.bfloat16)

    def keep(ref, index, a):
        high, low = halves(a)
        k = a.shape[0]
        ref[(*index, pl.ds(0, k), pl.ds(0, cz))] = high
        ref[(*index, pl.ds(0, k), pl.ds(cz, cz))] = low
        ref[(*index, pl.ds(k, k), pl.ds(0, cz))] = high
        ref[(*index, pl.ds(k, k), pl.ds(cz, cz))] = jnp.zeros_like(low)

    def dot(a, b):
        both = jnp.dot(jnp.concatenate(halves(a), 1), b, preferred_element_type=jnp.float32)
        return both[:, :cz] + both[:, cz:]

    for slot, taps in enumerate(z_taps):
        inner = jnp.zeros((cz, cz), jnp.float32)
        for k, tap in taps:
            inner = jnp.where(gap == k, tap, inner)
        keep(bands, (slot,), inner)

    tile = (per, cz)
    lane = lanes(tile)
    cell = lax.rem(lane, per)
    apart = lax.broadcasted_iota(jnp.int32, tile, 0) - cell
    group_of = lax.div(lane, per)
    owner = [group_of, lax.rem(group_of + 1, cx)]
    none = jnp.zeros(tile, jnp.float32)

    def corner(side, taps):
        shift = per if side == 0 else -per
        made = none
        for k, tap in taps:
            made = jnp.where(apart == k + shift, tap, made)
        return made

    for flip in range(2):
        taps = dict(taps_of(0, bool(flip)))
        for side in range(2):
            by_z = corner(side, [(k, tap) for k, tap in z_taps[flip] if (k < 0) == (side == 0) and k])
            is_owner = [owner[side] == q for q in range(cx)]
            rows = []
            for t in range(2 * cx):
                at_plane = (t + 1 - side) % cx
                if t >= cx:
                    at_plane += cx if at_plane < cx // 2 else -cx
                by_x = none
                for q in range(cx):
                    if at_plane - q in taps:
                        by_x = jnp.where(is_owner[q], taps[at_plane - q], by_x)
                rows.append(by_x * by_z)
            keep(edges, (flip, side), jnp.concatenate(rows, 0))
    def rim_pair(sides):
        even = lax.rem(lax.div(lanes(sides[0].shape), per), 2) == 0
        return jnp.where(even, sides[0], sides[1]), jnp.where(even, sides[1], sides[0])

    def from_rim(pair, i, width):
        spot = lanes(pair[0].shape)
        moved = turn(pair[i % 2], modulo(cz - per * i, cz))
        return jnp.where((spot < width) | (spot >= cz - width), moved, jnp.zeros_like(moved))

    def planes(buf, first, count, rows):
        return buf[pl.ds(first, count), rows].reshape(count * rows.size, cz)

    def smear(src, slot, square, flip, faces, packs_in, late):
        taps_x, taps_y = taps_of(0, flip), taps_of(1, flip)

        def load(k, first):
            v = src[k, pl.ds(R + first, 8)]
            return v * v if square else v

        def along_x(first, own, other, init):
            ins = {k: load(k, first) for k in range(cx + 2 * R) if (own if R <= k < R + cx else other)}
            for i in range(cx):
                total = yb[i, pl.ds(R + first, 8)] if init else None
                for k, tap in taps_x:
                    if i + R + k in ins:
                        part_ = ins[i + R + k] * tap
                        total = part_ if total is None else total + part_
                if total is not None:
                    yb[i, pl.ds(R + first, 8)] = total

        for first in range(0, cy, 8):
            along_x(first, True, False, False)
        arrive(faces)
        for first in range(0, cy, 8):
            along_x(first, False, True, True)
        own = pl.ds(R, cy)
        for g in range(0, cx, cx // 2):
            yb[pl.ds(g, cx // 2), own] = dot(planes(yb, g, cx // 2, own), bands[int(flip)]).reshape(cx // 2, cy, cz)
        for i in range(cx):
            low = mid = high = None
            for k, tap in taps_y:
                a = yb[i, pl.ds(R + 8 + k, cy - 16)] * tap
                mid = a if mid is None else mid + a
                if k >= 0:
                    a = yb[i, pl.ds(R + k, 8)] * tap
                    low = a if low is None else low + a
                if k <= 0:
                    a = yb[i, pl.ds(R + cy - 8 + k, 8)] * tap
                    high = a if high is None else high + a
            co[i] = jnp.concatenate([low, mid, high], 0)
        arrive(packs_in)
        wide_slot = lax.div(lanes((cy + 2 * R, cz)), per)
        for side in range(2):
            wide = lax.rem(wide_slot + 1 - side, cx) < cx // 2
            mine = zin[slot, side, 1]
            other = jnp.where(wide, zin[slot, side, 2], zin[slot, side, 0])
            if square:
                mine, other = mine * mine, other * other
            zb[side] = dot(jnp.concatenate([mine, other], 1), edges[int(flip), side])
        pair = []
        for side in range(2):
            total = zero
            for k, tap in taps_y:
                total = total + zb[side, pl.ds(R + k, cy)] * tap
            pair.append(total)
        pair = rim_pair(pair)
        arrive(late)
        for first in (-8, cy):
            along_x(first, True, True, False)
            rows = pl.ds(R + first, 8)
            yb[:, rows] = dot(planes(yb, 0, cx, rows), bands[int(flip)]).reshape(cx, 8, cz)

        def result(i):
            total = co[i] + from_rim(pair, i, R)
            low, high = total[:8], total[cy - 8:]
            for k, tap in taps_y:
                if k < 0:
                    low = low + yb[i, pl.ds(R + k, 8)] * tap
                if k > 0:
                    high = high + yb[i, pl.ds(R + cy - 8 + k, 8)] * tap
            return jnp.concatenate([low, total[8:cy - 8], high], 0)

        return result

    smeared = smear(wb, 0, True, False, wave_x, wave_z + wave_e, wave_y + wave_xy)
    packs = (zero, zero)
    for i in range(cx):
        coarse = smeared(i)
        value = wave_ref[i]
        dens = value * value
        both = coarse * coarse
        source = 0.5 * dens * both - dens * coarse
        corr_ref[i] = (0.5 / 3.0) * both * coarse - 0.5 * both
        sb[R + i, pl.ds(R, cy)] = source
        packs = pack_one(i, source, packs)
    pack_out(1, packs)
    start(src_e + src_z + src_x + src_y + src_xy)

    def z_rim_of(low, high):
        cell_of = lax.rem(lanes(low.shape), per)
        made = [jnp.zeros_like(low), jnp.zeros_like(low)]
        for k in range(1, H + 1):
            made[0] = made[0] + gains[k] * jnp.where(cell_of < k, turn(low, k), 0.0)
            made[1] = made[1] + gains[k] * jnp.where(cell_of >= per - k, turn(high, cz - k), 0.0)
        return rim_pair(made)

    def z_rim(slot, place=1, rows=pl.ds(R, cy)):
        return z_rim_of(*[zin[slot, side, place, rows] for side in range(2)])

    def own_part(buf, reach, weight, first_step):
        pair = z_rim(0) if first_step else None
        own = pl.ds(R, cy)
        step = 2 * GROUP
        for g in range(0, cx, step):
            along = dot(planes(buf, reach + g, step, own), bands[2])
            for i in range(g, g + step):
                total = buf[reach + i, own] * weight(i) + along[(i - g) * cy:(i - g + 1) * cy]
                if first_step:
                    total = total + from_rim(pair, i, H)
                for k in range(1, H + 1):
                    pairs = [buf[reach + j, own] for j in (i - k, i + k) if first_step or 0 <= j < cx]
                    if first_step:
                        pairs += [buf[reach + i, pl.ds(R + j, cy)] for j in (-k, k)]
                    both = pairs[0]
                    for p in pairs[1:]:
                        both = both + p
                    total = total + gains[k] * both
                if not first_step:
                    up = down = None
                    for k in range(1, H + 1):
                        a = gains[k] * buf[reach + i, pl.ds(R + k, cy - 8)]
                        b = gains[k] * buf[reach + i, pl.ds(R + 8 - k, cy - 8)]
                        up, down = (a, b) if up is None else (up + a, down + b)
                    total = total + jnp.concatenate([up[:8], up[8:] + down[:cy - 16], down[cy - 16:]], 0)
                part[i] = total

    def halo_part(buf, reach, pair, i):
        total = part[i]
        for k in range(1, H + 1):
            for j in (i - k, i + k):
                if not 0 <= j < cx:
                    total = total + gains[k] * buf[reach + j, pl.ds(R, cy)]
        low, high = total[:8], total[cy - 8:]
        for k in range(1, H + 1):
            low = low + gains[k] * buf[reach + i, pl.ds(R - k, 8)]
            high = high + gains[k] * buf[reach + i, pl.ds(R + cy - 8 + k, 8)]
        return jnp.concatenate([low, total[8:cy - 8], high], 0) + from_rim(pair, i, H)

    middle = 1.0 + STEP * 0.5 * 3.0 * LAP_COEF[0]
    own_part(wb, R, lambda i: middle, True)
    smeared = smear(sb, 1, False, True, src_x, src_z + src_e, src_y + src_xy)
    get_ext.wait()
    psi_packs = va_packs = (zero, zero)
    for i in range(cx):
        corr = corr_ref[i] + smeared(i)
        corr_ref[i] = corr
        felt = STEP * (corr + ext_ref[i])
        weight = middle - felt
        va[i] = weight
        value = part[i] - felt * wave_ref[i]
        pb[R + i, pl.ds(R, cy)] = value
        psi_packs = pack_one(i, value, psi_packs)
        va_packs = pack_one(i, weight, va_packs)
        half = pl.ds(H * (i % 2), H)
        ypack[0, i // 2, half] = weight[:H]
        ypack[1, i // 2, half] = weight[cy - H:]
    pack_out(2, psi_packs)
    pack_out(3, va_packs)
    start(psi_moves)
    own_part(pb, R, lambda i: va[i], False)
    arrive(psi_moves)
    own = pl.ds(R, cy)
    inside = {(0, 0): ix > 0, (0, 1): ix < nx - 1, (1, 0): iy > 0, (1, 1): iy < ny - 1, (2, 0): iz > 0, (2, 1): iz < nz - 1}

    def kept(dim, side, value):
        return jnp.where(inside[dim, side], value, 0.0)

    def star(p, first, rows):
        total = None
        for k in range(1, H + 1):
            pairs = pb[R + p - k, pl.ds(first, rows)] + pb[R + p + k, pl.ds(first, rows)]
            pairs += pb[R + p, pl.ds(first - k, rows)] + pb[R + p, pl.ds(first + k, rows)]
            total = gains[k] * pairs if total is None else total + gains[k] * pairs
        return total

    for side in range(2):
        pair = z_rim(2, 2 * side)
        begin = cx if side else -H
        along = dot(planes(pb, R + begin, H, own), bands[2])
        for n in range(H):
            p = begin + n
            total = pb[R + p, own] * vx[side, n] + along[n * cy:(n + 1) * cy] + star(p, R, cy)
            psi[H + p, own] = kept(0, side, total + from_rim(pair, p % cx, H))
    for side in range(2):
        first = R + cy - H if side else R - H
        pair = z_rim(2, 1, pl.ds(first, 2 * H))
        centers = [pb[R + i, pl.ds(first, 2 * H)] for i in range(cx)]
        along = dot(jnp.concatenate(centers, 0), bands[2])
        for i in range(cx):
            weight = yin[side, i // 2]
            if i % 2 != side:
                weight = pltpu.roll(weight, H, 0)
            total = centers[i] * weight + along[i * 2 * H:(i + 1) * 2 * H] + star(i, first, 2 * H)
            total = kept(1, side, total + from_rim(pair, i, H))
            if side:
                psi[H + i, pl.ds(R + cy, H)] = total[H:]
            else:
                psi[H + i, pl.ds(R - H, H)] = total[:H]
    rim = []
    cell = lax.rem(at, per)
    for side in range(2):
        far = zin[2, side, 1, own]
        plane_at = lax.rem(slot_of + 1 - side, cx)
        mine = turn(pack[2, side], per if side else cz - per)
        total = far * zin[3, side, 1, own]
        for k in range(1, H + 1):
            ahead = turn(jnp.where(plane_at < k, zin[2, side, 2, own], far), cz - per * k)
            behind = turn(jnp.where(plane_at >= cx - k, zin[2, side, 0, own], far), per * k)
            up, down = turn(far, cz - k), turn(far, k)
            if side:
                down = jnp.where(cell >= k, down, turn(mine, cz - per + k))
            else:
                up = jnp.where(cell < per - k, up, turn(mine, per - k))
            pairs = ahead + behind + up + down
            pairs += zin[2, side, 1, pl.ds(R - k, cy)] + zin[2, side, 1, pl.ds(R + k, cy)]
            total = total + gains[k] * pairs
        rim.append(kept(2, side, total))
    pair = z_rim(2)
    for i in range(cx):
        psi[H + i, own] = halo_part(pb, R, pair, i)
    own_part(psi, H, lambda i: va[i], False)
    pair = z_rim_of(*rim)
    total = zero
    for i in range(cx):
        value = halo_part(psi, H, pair, i)
        out_ref[i] = value
        total = total + value * value

    partial = jnp.sum(total, axis=0, keepdims=True)
    def all_sum(value, slots, ssem, rsem, me, n, ids):
        if n == 1:
            return value
        slots[me] = value

        def copy_of(d, slot):
            return pltpu.make_async_remote_copy(
                src_ref=slots.at[me], dst_ref=slots.at[slot], send_sem=ssem.at[d], recv_sem=rsem.at[slot],
                device_id=ids(d)[1], device_id_type=MESH)

        def go(d, c):
            copy_of(d, me).start()
            return c

        def come(d, c):
            copy_of(d, ids(d)[0]).wait_recv()
            return c

        def left(d, c):
            copy_of(d, me).wait_send()
            return c

        lax.fori_loop(1, n, go, 0)
        lax.fori_loop(1, n, come, 0)
        total = jnp.sum(slots[...], axis=0)
        lax.fori_loop(1, n, left, 0)
        return total

    if near:
        sums[0] = partial
        for d in range(1, everyone):
            pltpu.make_async_remote_copy(
                src_ref=sums.at[0], dst_ref=sums.at[d], send_sem=send2.at[0, 0], recv_sem=recv2.at[0, 0],
                device_id=others[d - 1], device_id_type=pl.DeviceIdType.LOGICAL).start()
        rest = sums.at[pl.ds(1, everyone - 1)]
        whole = pltpu.make_async_remote_copy(
            src_ref=rest, dst_ref=rest, send_sem=send2.at[0, 0], recv_sem=recv2.at[0, 0],
            device_id=others[0], device_id_type=pl.DeviceIdType.LOGICAL)
        whole.wait_recv()
        partial = jnp.sum(sums[...], axis=0)
    else:
        partial = all_sum(partial, sums, send2.at[0], recv2.at[0], here, plane, plane_id)
        partial = all_sum(partial, sums2, send2.at[1], recv2.at[1], iy, ny, line_id)
    cells = float(cx * cy * cz * nx * ny * nz)
    scale_ref[...] = lax.rsqrt(jnp.broadcast_to(jnp.sum(partial, axis=1, keepdims=True), scale_ref.shape) / cells + 1e-06)
    for way, (rows, to) in sent_rows.items():
        left = bytes_of(rows, send.at[way], recv.at[0, 0]).wait_send
        if to is None:
            left()
        else:
            pl.when(to)(left)
    if near:
        whole.wait_send()


def finish(psi_ref, corr_ref, scale_ref, out_hbm, corr_hbm, scaled, sems):
    copies = [pltpu.make_async_copy(corr_ref, corr_hbm, sems.at[0])]
    copies[0].start()
    cx, cy, cz = psi_ref.shape
    scale = scale_ref[0:1]
    steps = 2 if cx % 2 == 0 else 1
    for n in range(steps):
        some = pl.ds(n * (cx // steps), cx // steps)
        scaled[some] = psi_ref[some] * scale.reshape(1, 1, cz)
        copies.append(pltpu.make_async_copy(scaled.at[some], out_hbm.at[some], sems.at[1 + n]))
        copies[-1].start()
    for copy in copies:
        copy.wait()


def shards(sizes, wave, external, weights):
    cx, cy, cz = wave.shape
    nx, ny, nz = sizes
    f32 = jnp.float32
    near = nx <= 4 and ny <= 4 and nz <= 2
    spare_rows = max(2 * (R + H) * cy, 2 * cx * (R + H), 2 * cx * R + 4 * R * R, 6 * cy + 12 * R, 2 * (6 * cy + 12 * R) + 8 * cy + 4 * R, (3 * R + H) * cy, 3 * cx * R + cx * H)
    summed = nx * ny * nz if near else nx * nz
    stages, most = (1, 1) if near else (2, max(summed, ny))
    vmem = pl.BlockSpec(memory_space=pltpu.VMEM)
    stay = pl.BlockSpec(memory_space=pltpu.HBM)
    psi, corr, scale = pl.pallas_call(
        functools.partial(kernel, sizes),
        out_shape=(jax.ShapeDtypeStruct(wave.shape, f32), jax.ShapeDtypeStruct(wave.shape, f32),
                   jax.ShapeDtypeStruct((8, cz), f32)),
        in_specs=[stay, stay, stay],
        out_specs=(vmem, vmem, vmem),
        scratch_shapes=[
            pltpu.VMEM((cx + 2 * R, cy + 2 * R, cz), f32),
            pltpu.VMEM((cx + 2 * R, cy + 2 * R, cz), f32),
            pltpu.VMEM((cx, cy + 2 * R, cz), f32),
            pltpu.VMEM((cx, cy, cz), f32),
            pltpu.VMEM((cx + 2 * R, cy + 2 * R, cz), f32),
            pltpu.VMEM((cx + 2 * H, cy + 2 * R, cz), f32),
            pltpu.VMEM((cx, cy, cz), f32),
            pltpu.VMEM((cx, cy, cz), f32),
            pltpu.VMEM((4, 2, cy, cz), f32),
            pltpu.VMEM((4, 2, 3, cy + 2 * R, cz), f32),
            pltpu.VMEM((2, cy + 2 * R, cz), f32),
            pltpu.VMEM((2, H, cy, cz), f32),
            pltpu.VMEM((2, cx // 2, 2 * H, cz), f32),
            pltpu.VMEM((2, cx // 2, 2 * H, cz), f32),
            pltpu.VMEM((3, 2 * cz, 2 * cz), jnp.bfloat16),
            pltpu.VMEM((2, 2, 4 * cz, 2 * cz), jnp.bfloat16),
            pltpu.VMEM((cy, cz), f32),
            pltpu.VMEM((2 * (6 * cy + 12 * R) + 8 * cy + 4 * R, cz), f32),
            pltpu.VMEM((spare_rows, cz), f32),
            pltpu.VMEM((cx, cy, cz), f32),
            pltpu.SMEM(weights.shape, f32),
            pltpu.VMEM((summed, 1, cz), f32),
            pltpu.VMEM((ny, 1, cz), f32),
            pltpu.SemaphoreType.DMA((len(FLAT) + 1,)),
            pltpu.SemaphoreType.DMA((2, len(FLAT) + 2)),
            pltpu.SemaphoreType.DMA((stages, most)),
            pltpu.SemaphoreType.DMA((stages, most)),
            pltpu.SemaphoreType.DMA((3,)),
        ],
        compiler_params=pltpu.CompilerParams(collective_id=0, has_side_effects=True,
                                             vmem_limit_bytes=48 * 1024 * 1024),
    )(*[pltpu.with_memory_space_constraint(x, pltpu.HBM) for x in (weights, wave, external)])
    return pl.pallas_call(
        finish,
        out_shape=(jax.ShapeDtypeStruct(wave.shape, f32), jax.ShapeDtypeStruct(wave.shape, f32)),
        in_specs=[vmem, vmem, vmem],
        out_specs=(stay, stay),
        scratch_shapes=[pltpu.VMEM((cx, cy, cz), f32), pltpu.SemaphoreType.DMA((3,))],
    )(*[pltpu.with_memory_space_constraint(x, pltpu.VMEM) for x in (psi, corr, scale)])


def solution(mesh):
    sizes = tuple(mesh.shape[a] for a in AXES)
    spec = P(*AXES)
    return jax.shard_map(
        functools.partial(shards, sizes),
        mesh=mesh,
        in_specs=(spec, spec, P()),
        out_specs=(spec, spec),
        check_vma=False,
    )
```

```python
import functools

import jax
import jax.numpy as jnp
from jax import lax
from jax.experimental import pallas as pl
from jax.experimental.pallas import tpu as pltpu
from jax.sharding import PartitionSpec as P

SUBSTEPS = 3
LAP_COEF = (-205.0 / 72.0, 8.0 / 5.0, -1.0 / 5.0, 8.0 / 315.0, -1.0 / 560.0)
STEP = 0.08
AXES = ("gx", "gy", "gz")
MESH = pl.DeviceIdType.MESH
R = 8
H = 4


def lanes(shape):
    return lax.broadcasted_iota(jnp.int32, shape, len(shape) - 1)


PARTNERS = [(dx, dy, dz) for dx in (-1, 0, 1) for dy in (-1, 0, 1) for dz in (-1, 0, 1) if dx or dy or dz]
PARTNERS.sort(key=lambda d: d.count(0))
FLAT = [(dx, dy) for dx in (-1, 0, 1) for dy in (-1, 0, 1) if dx or dy]
GROUP = 4


def turn(value, shift):
    return value if isinstance(shift, int) and shift == 0 else pltpu.roll(value, shift, 1)


def modulo(a, n):
    return a % n if isinstance(a, int) else lax.rem(a, n)


def kernel(sizes, w_hbm, wave_hbm, ext_hbm, out_ref, corr_ref, scale_ref,
           wb, sb, yb, co, pb, psi, va, part, pack, zin, zb, vx, px, ypack, yin, bands, edges, blanks, spill, spare, ext_ref, w_ref,
           sums, sums2, send, recv, send2, recv2, local):
    nx, ny, nz = sizes
    cx, cy, cz = wave_hbm.shape
    wave_ref = wb.at[pl.ds(R, cx), pl.ds(R, cy)]
    get_wave = pltpu.make_async_copy(wave_hbm, wave_ref, local.at[0])
    get_ext = pltpu.make_async_copy(ext_hbm, ext_ref, local.at[1])
    get_weights = pltpu.make_async_copy(w_hbm, w_ref, local.at[2])
    get_wave.start()
    get_weights.start()
    ix, iy, iz = (lax.axis_index(a) for a in AXES)
    plane = nx * nz
    per = cz // cx
    here = ix * nz + iz

    def plane_id(d):
        t = lax.rem(here + d, plane)
        return t, {"gx": lax.div(t, nz), "gz": lax.rem(t, nz)}

    def line_id(d):
        t = lax.rem(iy + d, ny)
        return t, {"gy": t}

    barrier = pltpu.get_barrier_semaphore()

    def greet(ids):
        def body(d, c):
            pl.semaphore_signal(barrier, inc=1, device_id=ids(d)[1], device_id_type=MESH)
            return c
        return body

    near = nx <= 4 and ny <= 4 and nz <= 2

    def greet_partners(partners):
        count = 0
        for d3 in partners:
            there = None
            target = {}
            for name, d, i, n in zip(AXES, d3, (ix, iy, iz), sizes):
                if d:
                    ok = i < n - 1 if d > 0 else i > 0
                    there = ok if there is None else there & ok
                    target[name] = jnp.clip(i + d, 0, n - 1)
            count += there.astype(jnp.int32)

            @pl.when(there)
            def _(target=target):
                pl.semaphore_signal(barrier, inc=1, device_id=target, device_id_type=MESH)
        return count

    if near:
        guests = greet_partners(PARTNERS)
    else:
        guests = plane - 1 + ny - 1 + greet_partners([d for d in PARTNERS if d[1] and (d[0] or d[2])])
        lax.fori_loop(1, plane, greet(plane_id), 0)
        lax.fori_loop(1, ny, greet(line_id), 0)

    everyone = plane * ny
    order = (ix * ny + iy) * nz + iz
    others = [jnp.where(order + d < everyone, order + d, order + d - everyone) for d in range(1, everyone)] if near else []
    blanks[...] = jnp.zeros(blanks.shape, jnp.float32)
    pool = len(FLAT)
    sent_rows = {}
    spilled = [0]

    def rows_of(ref):
        count = 1
        for n in ref.shape[:-1]:
            count *= n
        return count

    def message(src, dst, dx, dy, dz, group):
        to, back = None, None
        for d, i, n in ((dx, ix, nx), (dy, iy, ny), (dz, iz, nz)):
            if d > 0:
                a, b = i < n - 1, i > 0
            elif d < 0:
                a, b = i > 0, i < n - 1
            else:
                continue
            to = a if to is None else to & a
            back = b if back is None else back & b
        target = {}
        for name, d, i, n in zip(AXES, (dx, dy, dz), (ix, iy, iz), sizes):
            if d:
                target[name] = jnp.clip(i + d, 0, n - 1)
        way = pool if dz else FLAT.index((dx, dy))
        rows, _ = sent_rows.get(way, (0, None))
        sent_rows[way] = rows + rows_of(dst), None if dz else to
        copy = pltpu.make_async_remote_copy(
            src_ref=src, dst_ref=dst, send_sem=send.at[way],
            recv_sem=recv.at[group % 2, pool + group // 2 if dz else way],
            device_id=target, device_id_type=MESH)
        return copy, to, back, dst, dz, group, way

    def start(messages):
        for copy, to, *_ in messages:
            pl.when(to)(copy.start)

    def blank(messages):
        for _, to, back, dst, dz, group, _ in messages:
            if dz:
                some = pl.ds(0, dst.shape[0])
                waste = spill.at[pl.ds(spilled[0], dst.shape[0])]
                spilled[0] += dst.shape[0]
                pl.when(jnp.logical_not(to))(pltpu.make_async_copy(blanks.at[some], waste, send.at[pool]).start)

            @pl.when(jnp.logical_not(back))
            def _(dst=dst, dz=dz, group=group):
                if dz:
                    pltpu.make_async_copy(blanks.at[pl.ds(0, dst.shape[0])], dst, recv.at[group % 2, pool + group // 2]).start()
                else:
                    dst[...] = jnp.zeros(dst.shape, dst.dtype)

    def bytes_of(rows, send_sem, recv_sem):
        some = spare.at[pl.ds(0, rows)]
        return pltpu.make_async_remote_copy(
            src_ref=some, dst_ref=some, send_sem=send_sem, recv_sem=recv_sem,
            device_id={"gx": ix}, device_id_type=MESH)

    def arrive(messages):
        rows, waits = {}, {}
        for _, _, back, dst, dz, group, way in messages:
            rows[way] = rows.get(way, 0) + rows_of(dst)
            waits[way] = None if dz else back, recv.at[group % 2, way + group // 2 if dz else way]
        for way, (back, sem) in waits.items():
            wait = bytes_of(rows[way], send.at[0], sem).wait_recv
            if back is None:
                wait()
            else:
                pl.when(back)(wait)

    at = lanes((cy, cz))
    zero = jnp.zeros((cy, cz), jnp.float32)

    slot_of = lax.div(at, per)

    def pack_one(i, value, packs):
        moved = turn(value, modulo(per * i, cz))
        return jnp.where(slot_of == i, moved, packs[0]), jnp.where(slot_of == (i - 1) % cx, moved, packs[1])

    def pack_out(slot, packs):
        pack[slot, 0] = packs[0]
        pack[slot, 1] = packs[1]

    def z_messages(slot, dxs, dys, group):
        out = []
        for dx in dxs:
            for dy in dys:
                if dy > 0:
                    rows, into = pl.ds(cy - R, R), pl.ds(0, R)
                elif dy < 0:
                    rows, into = pl.ds(0, R), pl.ds(R + cy, R)
                else:
                    rows, into = pl.ds(0, cy), pl.ds(R, cy)
                out.append(message(pack.at[slot, 1, rows], zin.at[slot, 0, 1 - dx, into], dx, dy, 1, group))
                out.append(message(pack.at[slot, 0, rows], zin.at[slot, 1, 1 - dx, into], dx, dy, -1, group))
        return out

    def side_messages(src, dst, moves, group, part=0, parts=1, wide=R):
        out = []
        for dx, dy in moves:
            if dx > 0:
                sx, tx = pl.ds(cx - wide, wide), pl.ds(R - wide, wide)
            elif dx < 0:
                sx, tx = pl.ds(0, wide), pl.ds(R + cx, wide)
            else:
                some = cx // parts
                sx, tx = pl.ds(part * some, some), pl.ds(R + part * some, some)
            if dy > 0:
                sy, ty = pl.ds(cy - R, R), pl.ds(0, R)
            elif dy < 0:
                sy, ty = pl.ds(0, R), pl.ds(R + cy, R)
            else:
                some = cy // parts
                sy, ty = pl.ds(part * some, some), pl.ds(R + part * some, some)
            out.append(message(src.at[sx, sy], dst.at[tx, ty], dx, dy, 0, group))
        return out

    face_x = [(dx, 0) for dx in (1, -1)]
    face_y = [(0, dy) for dy in (1, -1)]
    edge_xy = [(dx, dy) for dx in (1, -1) for dy in (1, -1)]
    src_ref = sb.at[pl.ds(R, cx), pl.ds(R, cy)]
    wave_x1, wave_x2 = (side_messages(wave_hbm, wb, face_x, 0, n, 2) for n in range(2))
    wave_y1, wave_y2 = (side_messages(wave_hbm, wb, face_y, 0, n, 2) for n in range(2))
    src_x, src_y = side_messages(src_ref, sb, face_x, 1), side_messages(src_ref, sb, face_y, 1)
    wave_xy, src_xy = side_messages(wave_hbm, wb, edge_xy, 0), side_messages(src_ref, sb, edge_xy, 1)
    wave_z, src_z = z_messages(0, (-1, 0, 1), (0,), 0), z_messages(1, (-1, 0, 1), (0,), 1)
    wave_e, src_e = z_messages(0, (-1, 0, 1), (-1, 1), 0), z_messages(1, (-1, 0, 1), (-1, 1), 1)

    own_psi = pb.at[pl.ds(R, cx), pl.ds(R, cy)]
    psi_x = side_messages(own_psi, pb, face_x, 2) + [
        message(va.at[pl.ds(cx - H, H)], vx.at[0], 1, 0, 0, 2),
        message(va.at[pl.ds(0, H)], vx.at[1], -1, 0, 0, 2),
    ]
    psi_y = side_messages(own_psi, pb, face_y, 2) + [
        message(ypack.at[1], yin.at[0], 0, 1, 0, 2),
        message(ypack.at[0], yin.at[1], 0, -1, 0, 2),
    ] + side_messages(own_psi, pb, edge_xy, 2, wide=H)
    psi_z = z_messages(2, (-1, 0, 1), (0,), 2) + z_messages(2, (0,), (-1, 1), 2) + z_messages(3, (0,), (0,), 2)
    psi_moves = psi_z + psi_x + psi_y

    pl.semaphore_wait(barrier, guests)
    start(wave_x1 + wave_y1)
    get_wave.wait()
    packs = (zero, zero)
    for i in range(cx):
        packs = pack_one(i, wave_ref[i], packs)
    pack_out(0, packs)
    start(wave_e + wave_z + wave_x2 + wave_y2 + wave_xy)
    wave_x, wave_y = wave_x1 + wave_x2, wave_y1 + wave_y2
    get_ext.start()
    for group in [wave_x, wave_y, wave_xy, wave_z, wave_e, src_x, src_y, src_xy, src_z, src_e, psi_moves]:
        blank(group)
    get_weights.wait()

    def taps_of(dim, flip):
        return [(k, w_ref[dim, R - k if flip else R + k]) for k in range(-R, R + 1)]

    row = lax.broadcasted_iota(jnp.int32, (cz, cz), 0)
    gap = row - lanes((cz, cz))
    gains = [STEP * 0.5 * c for c in LAP_COEF]
    z_taps = [taps_of(2, False), taps_of(2, True), [(k, gains[abs(k)]) for k in range(-H, H + 1) if k]]

    def halves(a):
        high = a.astype(jnp.bfloat16)
        return high, (a - high.astype(jnp.float32)).astype(jnp.bfloat16)

    def keep(ref, index, a):
        high, low = halves(a)
        k = a.shape[0]
        ref[(*index, pl.ds(0, k), pl.ds(0, cz))] = high
        ref[(*index, pl.ds(0, k), pl.ds(cz, cz))] = low
        ref[(*index, pl.ds(k, k), pl.ds(0, cz))] = high
        ref[(*index, pl.ds(k, k), pl.ds(cz, cz))] = jnp.zeros_like(low)

    def dot(a, b):
        both = jnp.dot(jnp.concatenate(halves(a), 1), b, preferred_element_type=jnp.float32)
        return both[:, :cz] + both[:, cz:]

    for slot, taps in enumerate(z_taps):
        inner = jnp.zeros((cz, cz), jnp.float32)
        for k, tap in taps:
            inner = jnp.where(gap == k, tap, inner)
        keep(bands, (slot,), inner)

    tile = (per, cz)
    lane = lanes(tile)
    cell = lax.rem(lane, per)
    apart = lax.broadcasted_iota(jnp.int32, tile, 0) - cell
    group_of = lax.div(lane, per)
    owner = [group_of, lax.rem(group_of + 1, cx)]
    none = jnp.zeros(tile, jnp.float32)

    def corner(side, taps):
        shift = per if side == 0 else -per
        made = none
        for k, tap in taps:
            made = jnp.where(apart == k + shift, tap, made)
        return made

    for flip in range(2):
        taps = dict(taps_of(0, bool(flip)))
        for side in range(2):
            by_z = corner(side, [(k, tap) for k, tap in z_taps[flip] if (k < 0) == (side == 0) and k])
            is_owner = [owner[side] == q for q in range(cx)]
            rows = []
            for t in range(2 * cx):
                at_plane = (t + 1 - side) % cx
                if t >= cx:
                    at_plane += cx if at_plane < cx // 2 else -cx
                by_x = none
                for q in range(cx):
                    if at_plane - q in taps:
                        by_x = jnp.where(is_owner[q], taps[at_plane - q], by_x)
                rows.append(by_x * by_z)
            keep(edges, (flip, side), jnp.concatenate(rows, 0))
    def rim_pair(sides):
        even = lax.rem(lax.div(lanes(sides[0].shape), per), 2) == 0
        return jnp.where(even, sides[0], sides[1]), jnp.where(even, sides[1], sides[0])

    def from_rim(pair, i, width):
        spot = lanes(pair[0].shape)
        moved = turn(pair[i % 2], modulo(cz - per * i, cz))
        return jnp.where((spot < width) | (spot >= cz - width), moved, jnp.zeros_like(moved))

    def planes(buf, first, count, rows):
        return buf[pl.ds(first, count), rows].reshape(count * rows.size, cz)

    def smear(src, slot, square, flip, faces, packs_in, late):
        taps_x, taps_y = taps_of(0, flip), taps_of(1, flip)

        def load(k, first):
            v = src[k, pl.ds(R + first, 8)]
            return v * v if square else v

        def along_x(first, own, other, init):
            ins = {k: load(k, first) for k in range(cx + 2 * R) if (own if R <= k < R + cx else other)}
            for i in range(cx):
                total = yb[i, pl.ds(R + first, 8)] if init else None
                for k, tap in taps_x:
                    if i + R + k in ins:
                        part_ = ins[i + R + k] * tap
                        total = part_ if total is None else total + part_
                if total is not None:
                    yb[i, pl.ds(R + first, 8)] = total

        for first in range(0, cy, 8):
            along_x(first, True, False, False)
        arrive(faces)
        for first in range(0, cy, 8):
            along_x(first, False, True, True)
        own = pl.ds(R, cy)
        for g in range(0, cx, cx // 2):
            yb[pl.ds(g, cx // 2), own] = dot(planes(yb, g, cx // 2, own), bands[int(flip)]).reshape(cx // 2, cy, cz)
        for i in range(cx):
            low = mid = high = None
            for k, tap in taps_y:
                a = yb[i, pl.ds(R + 8 + k, cy - 16)] * tap
                mid = a if mid is None else mid + a
                if k >= 0:
                    a = yb[i, pl.ds(R + k, 8)] * tap
                    low = a if low is None else low + a
                if k <= 0:
                    a = yb[i, pl.ds(R + cy - 8 + k, 8)] * tap
                    high = a if high is None else high + a
            co[i] = jnp.concatenate([low, mid, high], 0)
        arrive(packs_in)
        wide_slot = lax.div(lanes((cy + 2 * R, cz)), per)
        for side in range(2):
            wide = lax.rem(wide_slot + 1 - side, cx) < cx // 2
            mine = zin[slot, side, 1]
            other = jnp.where(wide, zin[slot, side, 2], zin[slot, side, 0])
            if square:
                mine, other = mine * mine, other * other
            zb[side] = dot(jnp.concatenate([mine, other], 1), edges[int(flip), side])
        pair = []
        for side in range(2):
            total = zero
            for k, tap in taps_y:
                total = total + zb[side, pl.ds(R + k, cy)] * tap
            pair.append(total)
        pair = rim_pair(pair)
        arrive(late)
        for first in (-8, cy):
            along_x(first, True, True, False)
            rows = pl.ds(R + first, 8)
            yb[:, rows] = dot(planes(yb, 0, cx, rows), bands[int(flip)]).reshape(cx, 8, cz)

        def result(i):
            total = co[i] + from_rim(pair, i, R)
            low, high = total[:8], total[cy - 8:]
            for k, tap in taps_y:
                if k < 0:
                    low = low + yb[i, pl.ds(R + k, 8)] * tap
                if k > 0:
                    high = high + yb[i, pl.ds(R + cy - 8 + k, 8)] * tap
            return jnp.concatenate([low, total[8:cy - 8], high], 0)

        return result

    smeared = smear(wb, 0, True, False, wave_x, wave_z + wave_e, wave_y + wave_xy)
    packs = (zero, zero)
    for i in range(cx):
        coarse = smeared(i)
        value = wave_ref[i]
        dens = value * value
        both = coarse * coarse
        source = 0.5 * dens * both - dens * coarse
        corr_ref[i] = (0.5 / 3.0) * both * coarse - 0.5 * both
        sb[R + i, pl.ds(R, cy)] = source
        packs = pack_one(i, source, packs)
    pack_out(1, packs)
    start(src_e + src_z + src_x + src_y + src_xy)

    def z_rim_of(low, high):
        cell_of = lax.rem(lanes(low.shape), per)
        made = [jnp.zeros_like(low), jnp.zeros_like(low)]
        for k in range(1, H + 1):
            made[0] = made[0] + gains[k] * jnp.where(cell_of < k, turn(low, k), 0.0)
            made[1] = made[1] + gains[k] * jnp.where(cell_of >= per - k, turn(high, cz - k), 0.0)
        return rim_pair(made)

    def z_rim(slot, place=1, rows=pl.ds(R, cy)):
        return z_rim_of(*[zin[slot, side, place, rows] for side in range(2)])

    def y_own(buf, p):
        up = down = None
        for k in range(1, H + 1):
            a = gains[k] * buf[p, pl.ds(R + k, cy - 8)]
            b = gains[k] * buf[p, pl.ds(R + 8 - k, cy - 8)]
            up, down = (a, b) if up is None else (up + a, down + b)
        return jnp.concatenate([up[:8], up[8:] + down[:cy - 16], down[cy - 16:]], 0)

    def y_halo(buf, p, total):
        low, high = total[:8], total[cy - 8:]
        for k in range(1, H + 1):
            low = low + gains[k] * buf[p, pl.ds(R - k, 8)]
            high = high + gains[k] * buf[p, pl.ds(R + cy - 8 + k, 8)]
        return jnp.concatenate([low, total[8:cy - 8], high], 0)

    def advance(buf, reach, weight, pair, put):
        own = pl.ds(R, cy)
        step = 2 * GROUP
        for g in range(0, cx, step):
            along = dot(planes(buf, reach + g, step, own), bands[2])
            for i in range(g, g + step):
                total = buf[reach + i, own] * weight(i) + along[(i - g) * cy:(i - g + 1) * cy]
                for k in range(1, H + 1):
                    pairs = [buf[reach + j, own] for j in (i - k, i + k) if pair is not None or 0 <= j < cx]
                    if pair is not None:
                        pairs += [buf[reach + i, pl.ds(R + j, cy)] for j in (-k, k)]
                    both = pairs[0]
                    for p in pairs[1:]:
                        both = both + p
                    total = total + gains[k] * both
                put(i, total + (y_own(buf, reach + i) if pair is None else from_rim(pair, i, H)))

    def keep_part(i, value):
        part[i] = value

    middle = 1.0 + STEP * 0.5 * 3.0 * LAP_COEF[0]
    advance(wb, R, lambda i: middle, z_rim(0), keep_part)
    smeared = smear(sb, 1, False, True, src_x, src_z + src_e, src_y + src_xy)
    get_ext.wait()
    psi_packs = va_packs = (zero, zero)
    for i in range(cx):
        corr = corr_ref[i] + smeared(i)
        corr_ref[i] = corr
        felt = STEP * (corr + ext_ref[i])
        weight = middle - felt
        va[i] = weight
        value = part[i] - felt * wave_ref[i]
        pb[R + i, pl.ds(R, cy)] = value
        psi_packs = pack_one(i, value, psi_packs)
        va_packs = pack_one(i, weight, va_packs)
        half = pl.ds(H * (i % 2), H)
        ypack[0, i // 2, half] = weight[:H]
        ypack[1, i // 2, half] = weight[cy - H:]
    pack_out(2, psi_packs)
    pack_out(3, va_packs)
    start(psi_moves)
    advance(pb, R, lambda i: va[i], None, keep_part)
    own = pl.ds(R, cy)
    inside = {(0, 0): ix > 0, (0, 1): ix < nx - 1, (1, 0): iy > 0, (1, 1): iy < ny - 1, (2, 0): iz > 0, (2, 1): iz < nz - 1}

    def kept(dim, side, value):
        return jnp.where(inside[dim, side], value, 0.0)

    def star(p, first, rows):
        total = None
        for k in range(1, H + 1):
            pairs = pb[R + p - k, pl.ds(first, rows)] + pb[R + p + k, pl.ds(first, rows)]
            pairs += pb[R + p, pl.ds(first - k, rows)] + pb[R + p, pl.ds(first + k, rows)]
            total = gains[k] * pairs if total is None else total + gains[k] * pairs
        return total

    arrive(psi_z)
    rim = []
    cell = lax.rem(at, per)
    for side in range(2):
        far = zin[2, side, 1, own]
        plane_at = lax.rem(slot_of + 1 - side, cx)
        mine = turn(pack[2, side], per if side else cz - per)
        total = far * zin[3, side, 1, own]
        for k in range(1, H + 1):
            ahead = turn(jnp.where(plane_at < k, zin[2, side, 2, own], far), cz - per * k)
            behind = turn(jnp.where(plane_at >= cx - k, zin[2, side, 0, own], far), per * k)
            up, down = turn(far, cz - k), turn(far, k)
            if side:
                down = jnp.where(cell >= k, down, turn(mine, cz - per + k))
            else:
                up = jnp.where(cell < per - k, up, turn(mine, per - k))
            pairs = ahead + behind + up + down
            pairs += zin[2, side, 1, pl.ds(R - k, cy)] + zin[2, side, 1, pl.ds(R + k, cy)]
            total = total + gains[k] * pairs
        rim.append(kept(2, side, total))
    arrive(psi_x)
    pair = z_rim(2)
    for i in range(cx):
        total = part[i] + from_rim(pair, i, H)
        for k in range(1, H + 1):
            for j in (i - k, i + k):
                if not 0 <= j < cx:
                    total = total + gains[k] * pb[R + j, own]
        part[i] = total
    for side in range(2):
        pair = z_rim(2, 2 * side)
        begin = cx if side else -H
        along = dot(planes(pb, R + begin, H, own), bands[2])
        for n in range(H):
            p = begin + n
            total = pb[R + p, own] * vx[side, n] + along[n * cy:(n + 1) * cy]
            for k in range(1, H + 1):
                total = total + gains[k] * (pb[R + p - k, own] + pb[R + p + k, own])
            px[side, n] = total + y_own(pb, R + p) + from_rim(pair, p % cx, H)
    arrive(psi_y)
    for side in range(2):
        first = R + cy - H if side else R - H
        pair = z_rim(2, 1, pl.ds(first, 2 * H))
        centers = [pb[R + i, pl.ds(first, 2 * H)] for i in range(cx)]
        along = dot(jnp.concatenate(centers, 0), bands[2])
        for i in range(cx):
            weight = yin[side, i // 2]
            if i % 2 != side:
                weight = pltpu.roll(weight, H, 0)
            total = centers[i] * weight + along[i * 2 * H:(i + 1) * 2 * H] + star(i, first, 2 * H)
            total = kept(1, side, total + from_rim(pair, i, H))
            if side:
                psi[H + i, pl.ds(R + cy, H)] = total[H:]
            else:
                psi[H + i, pl.ds(R - H, H)] = total[:H]
    for side in range(2):
        begin = cx if side else -H
        for n in range(H):
            psi[H + begin + n, own] = kept(0, side, y_halo(pb, R + begin + n, px[side, n]))
    for i in range(cx):
        psi[H + i, own] = y_halo(pb, R + i, part[i])
    totals = [zero]

    def finish_cell(i, value):
        out_ref[i] = value
        totals[0] = totals[0] + value * value

    advance(psi, H, lambda i: va[i], z_rim_of(*rim), finish_cell)
    total = totals[0]
    partial = jnp.sum(total, axis=0, keepdims=True)
    def all_sum(value, slots, ssem, rsem, me, n, ids):
        if n == 1:
            return value
        slots[me] = value

        def copy_of(d, slot):
            return pltpu.make_async_remote_copy(
                src_ref=slots.at[me], dst_ref=slots.at[slot], send_sem=ssem.at[d], recv_sem=rsem.at[slot],
                device_id=ids(d)[1], device_id_type=MESH)

        def go(d, c):
            copy_of(d, me).start()
            return c

        def come(d, c):
            copy_of(d, ids(d)[0]).wait_recv()
            return c

        def left(d, c):
            copy_of(d, me).wait_send()
            return c

        lax.fori_loop(1, n, go, 0)
        lax.fori_loop(1, n, come, 0)
        total = jnp.sum(slots[...], axis=0)
        lax.fori_loop(1, n, left, 0)
        return total

    if near:
        sums[0] = partial
        for d in range(1, everyone):
            pltpu.make_async_remote_copy(
                src_ref=sums.at[0], dst_ref=sums.at[d], send_sem=send2.at[0, 0], recv_sem=recv2.at[0, 0],
                device_id=others[d - 1], device_id_type=pl.DeviceIdType.LOGICAL).start()
        rest = sums.at[pl.ds(1, everyone - 1)]
        whole = pltpu.make_async_remote_copy(
            src_ref=rest, dst_ref=rest, send_sem=send2.at[0, 0], recv_sem=recv2.at[0, 0],
            device_id=others[0], device_id_type=pl.DeviceIdType.LOGICAL)
        whole.wait_recv()
        partial = jnp.sum(sums[...], axis=0)
    else:
        partial = all_sum(partial, sums, send2.at[0], recv2.at[0], here, plane, plane_id)
        partial = all_sum(partial, sums2, send2.at[1], recv2.at[1], iy, ny, line_id)
    cells = float(cx * cy * cz * nx * ny * nz)
    scale_ref[...] = lax.rsqrt(jnp.broadcast_to(jnp.sum(partial, axis=1, keepdims=True), scale_ref.shape) / cells + 1e-06)
    for way, (rows, to) in sent_rows.items():
        left = bytes_of(rows, send.at[way], recv.at[0, 0]).wait_send
        if to is None:
            left()
        else:
            pl.when(to)(left)
    if near:
        whole.wait_send()


def finish(psi_ref, corr_ref, scale_ref, out_hbm, corr_hbm, scaled, sems):
    copies = [pltpu.make_async_copy(corr_ref, corr_hbm, sems.at[0])]
    copies[0].start()
    cx, cy, cz = psi_ref.shape
    scale = scale_ref[0:1]
    steps = 2 if cx % 2 == 0 else 1
    for n in range(steps):
        some = pl.ds(n * (cx // steps), cx // steps)
        scaled[some] = psi_ref[some] * scale.reshape(1, 1, cz)
        copies.append(pltpu.make_async_copy(scaled.at[some], out_hbm.at[some], sems.at[1 + n]))
        copies[-1].start()
    for copy in copies:
        copy.wait()


def shards(sizes, wave, external, weights):
    cx, cy, cz = wave.shape
    nx, ny, nz = sizes
    f32 = jnp.float32
    near = nx <= 4 and ny <= 4 and nz <= 2
    spare_rows = max(2 * (R + H) * cy, 2 * cx * (R + H), 2 * cx * R + 4 * R * R, 6 * cy + 12 * R, 2 * (6 * cy + 12 * R) + 8 * cy + 4 * R, (3 * R + H) * cy, 3 * cx * R + cx * H)
    summed = nx * ny * nz if near else nx * nz
    stages, most = (1, 1) if near else (2, max(summed, ny))
    vmem = pl.BlockSpec(memory_space=pltpu.VMEM)
    stay = pl.BlockSpec(memory_space=pltpu.HBM)
    psi, corr, scale = pl.pallas_call(
        functools.partial(kernel, sizes),
        out_shape=(jax.ShapeDtypeStruct(wave.shape, f32), jax.ShapeDtypeStruct(wave.shape, f32),
                   jax.ShapeDtypeStruct((8, cz), f32)),
        in_specs=[stay, stay, stay],
        out_specs=(vmem, vmem, vmem),
        scratch_shapes=[
            pltpu.VMEM((cx + 2 * R, cy + 2 * R, cz), f32),
            pltpu.VMEM((cx + 2 * R, cy + 2 * R, cz), f32),
            pltpu.VMEM((cx, cy + 2 * R, cz), f32),
            pltpu.VMEM((cx, cy, cz), f32),
            pltpu.VMEM((cx + 2 * R, cy + 2 * R, cz), f32),
            pltpu.VMEM((cx + 2 * H, cy + 2 * R, cz), f32),
            pltpu.VMEM((cx, cy, cz), f32),
            pltpu.VMEM((cx, cy, cz), f32),
            pltpu.VMEM((4, 2, cy, cz), f32),
            pltpu.VMEM((4, 2, 3, cy + 2 * R, cz), f32),
            pltpu.VMEM((2, cy + 2 * R, cz), f32),
            pltpu.VMEM((2, H, cy, cz), f32),
            pltpu.VMEM((2, H, cy, cz), f32),
            pltpu.VMEM((2, cx // 2, 2 * H, cz), f32),
            pltpu.VMEM((2, cx // 2, 2 * H, cz), f32),
            pltpu.VMEM((3, 2 * cz, 2 * cz), jnp.bfloat16),
            pltpu.VMEM((2, 2, 4 * cz, 2 * cz), jnp.bfloat16),
            pltpu.VMEM((cy, cz), f32),
            pltpu.VMEM((2 * (6 * cy + 12 * R) + 8 * cy + 4 * R, cz), f32),
            pltpu.VMEM((spare_rows, cz), f32),
            pltpu.VMEM((cx, cy, cz), f32),
            pltpu.SMEM(weights.shape, f32),
            pltpu.VMEM((summed, 1, cz), f32),
            pltpu.VMEM((ny, 1, cz), f32),
            pltpu.SemaphoreType.DMA((len(FLAT) + 1,)),
            pltpu.SemaphoreType.DMA((2, len(FLAT) + 2)),
            pltpu.SemaphoreType.DMA((stages, most)),
            pltpu.SemaphoreType.DMA((stages, most)),
            pltpu.SemaphoreType.DMA((3,)),
        ],
        compiler_params=pltpu.CompilerParams(collective_id=0, has_side_effects=True,
                                             vmem_limit_bytes=48 * 1024 * 1024),
    )(*[pltpu.with_memory_space_constraint(x, pltpu.HBM) for x in (weights, wave, external)])
    return pl.pallas_call(
        finish,
        out_shape=(jax.ShapeDtypeStruct(wave.shape, f32), jax.ShapeDtypeStruct(wave.shape, f32)),
        in_specs=[vmem, vmem, vmem],
        out_specs=(stay, stay),
        scratch_shapes=[pltpu.VMEM((cx, cy, cz), f32), pltpu.SemaphoreType.DMA((3,))],
    )(*[pltpu.with_memory_space_constraint(x, pltpu.VMEM) for x in (psi, corr, scale)])


def solution(mesh):
    sizes = tuple(mesh.shape[a] for a in AXES)
    spec = P(*AXES)
    return jax.shard_map(
        functools.partial(shards, sizes),
        mesh=mesh,
        in_specs=(spec, spec, P()),
        out_specs=(spec, spec),
        check_vma=False,
    )
```

```python
import functools

import jax
import jax.numpy as jnp
from jax import lax
from jax.experimental import pallas as pl
from jax.experimental.pallas import tpu as pltpu
from jax.sharding import PartitionSpec as P

SUBSTEPS = 3
LAP_COEF = (-205.0 / 72.0, 8.0 / 5.0, -1.0 / 5.0, 8.0 / 315.0, -1.0 / 560.0)
STEP = 0.08
AXES = ("gx", "gy", "gz")
MESH = pl.DeviceIdType.MESH
R = 8
H = 4


def lanes(shape):
    return lax.broadcasted_iota(jnp.int32, shape, len(shape) - 1)


PARTNERS = [(dx, dy, dz) for dx in (-1, 0, 1) for dy in (-1, 0, 1) for dz in (-1, 0, 1) if dx or dy or dz]
PARTNERS.sort(key=lambda d: d.count(0))
FLAT = [(dx, dy) for dx in (-1, 0, 1) for dy in (-1, 0, 1) if dx or dy]
GROUP = 4


def turn(value, shift):
    return value if isinstance(shift, int) and shift == 0 else pltpu.roll(value, shift, 1)


def modulo(a, n):
    return a % n if isinstance(a, int) else lax.rem(a, n)


def kernel(sizes, w_hbm, wave_hbm, ext_hbm, out_ref, corr_ref, scale_ref,
           wb, sb, yb, co, pb, psi, va, part, pack, zin, zb, vx, px, ypack, yin, bands, edges, blanks, spill, spare, ext_ref, w_ref,
           sums, sums2, send, recv, send2, recv2, local):
    nx, ny, nz = sizes
    cx, cy, cz = wave_hbm.shape
    wave_ref = wb.at[pl.ds(R, cx), pl.ds(R, cy)]
    get_wave = pltpu.make_async_copy(wave_hbm, wave_ref, local.at[0])
    get_ext = pltpu.make_async_copy(ext_hbm, ext_ref, local.at[1])
    get_weights = pltpu.make_async_copy(w_hbm, w_ref, local.at[2])
    get_wave.start()
    get_weights.start()
    ix, iy, iz = (lax.axis_index(a) for a in AXES)
    plane = nx * nz
    per = cz // cx
    here = ix * nz + iz

    def plane_id(d):
        t = lax.rem(here + d, plane)
        return t, {"gx": lax.div(t, nz), "gz": lax.rem(t, nz)}

    def line_id(d):
        t = lax.rem(iy + d, ny)
        return t, {"gy": t}

    barrier = pltpu.get_barrier_semaphore()

    def greet(ids):
        def body(d, c):
            pl.semaphore_signal(barrier, inc=1, device_id=ids(d)[1], device_id_type=MESH)
            return c
        return body

    near = nx <= 4 and ny <= 4 and nz <= 2

    def greet_partners(partners):
        count = 0
        for d3 in partners:
            there = None
            target = {}
            for name, d, i, n in zip(AXES, d3, (ix, iy, iz), sizes):
                if d:
                    ok = i < n - 1 if d > 0 else i > 0
                    there = ok if there is None else there & ok
                    target[name] = jnp.clip(i + d, 0, n - 1)
            count += there.astype(jnp.int32)

            @pl.when(there)
            def _(target=target):
                pl.semaphore_signal(barrier, inc=1, device_id=target, device_id_type=MESH)
        return count

    if near:
        guests = greet_partners(PARTNERS)
    else:
        guests = plane - 1 + ny - 1 + greet_partners([d for d in PARTNERS if d[1] and (d[0] or d[2])])
        lax.fori_loop(1, plane, greet(plane_id), 0)
        lax.fori_loop(1, ny, greet(line_id), 0)

    everyone = plane * ny
    order = (ix * ny + iy) * nz + iz
    others = [jnp.where(order + d < everyone, order + d, order + d - everyone) for d in range(1, everyone)] if near else []
    blanks[...] = jnp.zeros(blanks.shape, jnp.float32)
    pool = len(FLAT)
    sent_rows = {}
    spilled = [0]

    def rows_of(ref):
        count = 1
        for n in ref.shape[:-1]:
            count *= n
        return count

    def message(src, dst, dx, dy, dz, group):
        to, back = None, None
        for d, i, n in ((dx, ix, nx), (dy, iy, ny), (dz, iz, nz)):
            if d > 0:
                a, b = i < n - 1, i > 0
            elif d < 0:
                a, b = i > 0, i < n - 1
            else:
                continue
            to = a if to is None else to & a
            back = b if back is None else back & b
        target = {}
        for name, d, i, n in zip(AXES, (dx, dy, dz), (ix, iy, iz), sizes):
            if d:
                target[name] = jnp.clip(i + d, 0, n - 1)
        way = pool if dz else FLAT.index((dx, dy))
        rows, _ = sent_rows.get(way, (0, None))
        sent_rows[way] = rows + rows_of(dst), None if dz else to
        copy = pltpu.make_async_remote_copy(
            src_ref=src, dst_ref=dst, send_sem=send.at[way],
            recv_sem=recv.at[group % 2, pool + group // 2 if dz else way],
            device_id=target, device_id_type=MESH)
        return copy, to, back, dst, dz, group, way

    def start(messages):
        for copy, to, *_ in messages:
            pl.when(to)(copy.start)

    def blank(messages):
        for _, to, back, dst, dz, group, _ in messages:
            if dz:
                some = pl.ds(0, dst.shape[0])
                waste = spill.at[pl.ds(spilled[0], dst.shape[0])]
                spilled[0] += dst.shape[0]
                pl.when(jnp.logical_not(to))(pltpu.make_async_copy(blanks.at[some], waste, send.at[pool]).start)

            @pl.when(jnp.logical_not(back))
            def _(dst=dst, dz=dz, group=group):
                if dz:
                    pltpu.make_async_copy(blanks.at[pl.ds(0, dst.shape[0])], dst, recv.at[group % 2, pool + group // 2]).start()
                else:
                    dst[...] = jnp.zeros(dst.shape, dst.dtype)

    def bytes_of(rows, send_sem, recv_sem):
        some = spare.at[pl.ds(0, rows)]
        return pltpu.make_async_remote_copy(
            src_ref=some, dst_ref=some, send_sem=send_sem, recv_sem=recv_sem,
            device_id={"gx": ix}, device_id_type=MESH)

    def arrive(messages):
        rows, waits = {}, {}
        for _, _, back, dst, dz, group, way in messages:
            rows[way] = rows.get(way, 0) + rows_of(dst)
            waits[way] = None if dz else back, recv.at[group % 2, way + group // 2 if dz else way]
        for way, (back, sem) in waits.items():
            wait = bytes_of(rows[way], send.at[0], sem).wait_recv
            if back is None:
                wait()
            else:
                pl.when(back)(wait)

    at = lanes((cy, cz))
    zero = jnp.zeros((cy, cz), jnp.float32)

    slot_of = lax.div(at, per)

    def pack_one(i, value, packs):
        moved = turn(value, modulo(per * i, cz))
        return jnp.where(slot_of == i, moved, packs[0]), jnp.where(slot_of == (i - 1) % cx, moved, packs[1])

    def pack_out(slot, packs):
        pack[slot, 0] = packs[0]
        pack[slot, 1] = packs[1]

    def z_messages(slot, dxs, dys, group):
        out = []
        for dx in dxs:
            for dy in dys:
                if dy > 0:
                    rows, into = pl.ds(cy - R, R), pl.ds(0, R)
                elif dy < 0:
                    rows, into = pl.ds(0, R), pl.ds(R + cy, R)
                else:
                    rows, into = pl.ds(0, cy), pl.ds(R, cy)
                out.append(message(pack.at[slot, 1, rows], zin.at[slot, 0, 1 - dx, into], dx, dy, 1, group))
                out.append(message(pack.at[slot, 0, rows], zin.at[slot, 1, 1 - dx, into], dx, dy, -1, group))
        return out

    def side_messages(src, dst, moves, group, part=0, parts=1, wide=R, tall=R):
        out = []
        for dx, dy in moves:
            if dx > 0:
                sx, tx = pl.ds(cx - wide, wide), pl.ds(R - wide, wide)
            elif dx < 0:
                sx, tx = pl.ds(0, wide), pl.ds(R + cx, wide)
            else:
                some = cx // parts
                sx, tx = pl.ds(part * some, some), pl.ds(R + part * some, some)
            if dy > 0:
                sy, ty = pl.ds(cy - tall, tall), pl.ds(R - tall, tall)
            elif dy < 0:
                sy, ty = pl.ds(0, tall), pl.ds(R + cy, tall)
            else:
                some = cy // parts
                sy, ty = pl.ds(part * some, some), pl.ds(R + part * some, some)
            out.append(message(src.at[sx, sy], dst.at[tx, ty], dx, dy, 0, group))
        return out

    face_x = [(dx, 0) for dx in (1, -1)]
    face_y = [(0, dy) for dy in (1, -1)]
    edge_xy = [(dx, dy) for dx in (1, -1) for dy in (1, -1)]
    src_ref = sb.at[pl.ds(R, cx), pl.ds(R, cy)]
    wave_x1, wave_x2 = (side_messages(wave_hbm, wb, face_x, 0, n, 2) for n in range(2))
    wave_y1, wave_y2 = (side_messages(wave_hbm, wb, face_y, 0, n, 2) for n in range(2))
    src_x, src_y = side_messages(src_ref, sb, face_x, 1), side_messages(src_ref, sb, face_y, 1)
    wave_xy, src_xy = side_messages(wave_hbm, wb, edge_xy, 0), side_messages(src_ref, sb, edge_xy, 1)
    wave_z, src_z = z_messages(0, (-1, 0, 1), (0,), 0), z_messages(1, (-1, 0, 1), (0,), 1)
    wave_e, src_e = z_messages(0, (-1, 0, 1), (-1, 1), 0), z_messages(1, (-1, 0, 1), (-1, 1), 1)

    own_psi = pb.at[pl.ds(R, cx), pl.ds(R, cy)]
    psi_x = side_messages(own_psi, pb, face_x, 2) + [
        message(va.at[pl.ds(cx - H, H)], vx.at[0], 1, 0, 0, 2),
        message(va.at[pl.ds(0, H)], vx.at[1], -1, 0, 0, 2),
    ]
    psi_y = side_messages(own_psi, pb, face_y, 2) + [
        message(ypack.at[1], yin.at[0], 0, 1, 0, 2),
        message(ypack.at[0], yin.at[1], 0, -1, 0, 2),
    ] + side_messages(own_psi, pb, edge_xy, 2, wide=H, tall=H)
    psi_z = z_messages(2, (-1, 0, 1), (0,), 2) + z_messages(2, (0,), (-1, 1), 2) + z_messages(3, (0,), (0,), 2)
    psi_moves = psi_z + psi_x + psi_y

    pl.semaphore_wait(barrier, guests)
    start(wave_x1 + wave_y1)
    get_wave.wait()
    packs = (zero, zero)
    for i in range(cx):
        packs = pack_one(i, wave_ref[i], packs)
    pack_out(0, packs)
    start(wave_e + wave_z + wave_x2 + wave_y2 + wave_xy)
    wave_x, wave_y = wave_x1 + wave_x2, wave_y1 + wave_y2
    get_ext.start()
    for group in [wave_x, wave_y, wave_xy, wave_z, wave_e, src_x, src_y, src_xy, src_z, src_e, psi_moves]:
        blank(group)
    get_weights.wait()

    def taps_of(dim, flip):
        return [(k, w_ref[dim, R - k if flip else R + k]) for k in range(-R, R + 1)]

    row = lax.broadcasted_iota(jnp.int32, (cz, cz), 0)
    gap = row - lanes((cz, cz))
    gains = [STEP * 0.5 * c for c in LAP_COEF]
    z_taps = [taps_of(2, False), taps_of(2, True), [(k, gains[abs(k)]) for k in range(-H, H + 1) if k]]

    def halves(a):
        high = a.astype(jnp.bfloat16)
        return high, (a - high.astype(jnp.float32)).astype(jnp.bfloat16)

    def keep(ref, index, a):
        high, low = halves(a)
        k = a.shape[0]
        ref[(*index, pl.ds(0, k), pl.ds(0, cz))] = high
        ref[(*index, pl.ds(0, k), pl.ds(cz, cz))] = low
        ref[(*index, pl.ds(k, k), pl.ds(0, cz))] = high
        ref[(*index, pl.ds(k, k), pl.ds(cz, cz))] = jnp.zeros_like(low)

    def dot(a, b):
        both = jnp.dot(jnp.concatenate(halves(a), 1), b, preferred_element_type=jnp.float32)
        return both[:, :cz] + both[:, cz:]

    for slot, taps in enumerate(z_taps):
        inner = jnp.zeros((cz, cz), jnp.float32)
        for k, tap in taps:
            inner = jnp.where(gap == k, tap, inner)
        keep(bands, (slot,), inner)

    tile = (per, cz)
    lane = lanes(tile)
    cell = lax.rem(lane, per)
    apart = lax.broadcasted_iota(jnp.int32, tile, 0) - cell
    group_of = lax.div(lane, per)
    owner = [group_of, lax.rem(group_of + 1, cx)]
    none = jnp.zeros(tile, jnp.float32)

    def corner(side, taps):
        shift = per if side == 0 else -per
        made = none
        for k, tap in taps:
            made = jnp.where(apart == k + shift, tap, made)
        return made

    for flip in range(2):
        taps = dict(taps_of(0, bool(flip)))
        for side in range(2):
            by_z = corner(side, [(k, tap) for k, tap in z_taps[flip] if (k < 0) == (side == 0) and k])
            is_owner = [owner[side] == q for q in range(cx)]
            rows = []
            for t in range(2 * cx):
                at_plane = (t + 1 - side) % cx
                if t >= cx:
                    at_plane += cx if at_plane < cx // 2 else -cx
                by_x = none
                for q in range(cx):
                    if at_plane - q in taps:
                        by_x = jnp.where(is_owner[q], taps[at_plane - q], by_x)
                rows.append(by_x * by_z)
            keep(edges, (flip, side), jnp.concatenate(rows, 0))
    def rim_pair(sides):
        even = lax.rem(lax.div(lanes(sides[0].shape), per), 2) == 0
        return jnp.where(even, sides[0], sides[1]), jnp.where(even, sides[1], sides[0])

    def from_rim(pair, i, width):
        spot = lanes(pair[0].shape)
        moved = turn(pair[i % 2], modulo(cz - per * i, cz))
        return jnp.where((spot < width) | (spot >= cz - width), moved, jnp.zeros_like(moved))

    def planes(buf, first, count, rows):
        return buf[pl.ds(first, count), rows].reshape(count * rows.size, cz)

    def smear(src, slot, square, flip, faces, packs_in, late):
        taps_x, taps_y = taps_of(0, flip), taps_of(1, flip)

        def load(k, first):
            v = src[k, pl.ds(R + first, 8)]
            return v * v if square else v

        def along_x(first, own, other, init):
            ins = {k: load(k, first) for k in range(cx + 2 * R) if (own if R <= k < R + cx else other)}
            for i in range(cx):
                total = yb[i, pl.ds(R + first, 8)] if init else None
                for k, tap in taps_x:
                    if i + R + k in ins:
                        part_ = ins[i + R + k] * tap
                        total = part_ if total is None else total + part_
                if total is not None:
                    yb[i, pl.ds(R + first, 8)] = total

        for first in range(0, cy, 8):
            along_x(first, True, False, False)
        arrive(faces)
        for first in range(0, cy, 8):
            along_x(first, False, True, True)
        own = pl.ds(R, cy)
        for g in range(0, cx, cx // 2):
            yb[pl.ds(g, cx // 2), own] = dot(planes(yb, g, cx // 2, own), bands[int(flip)]).reshape(cx // 2, cy, cz)
        for i in range(cx):
            low = mid = high = None
            for k, tap in taps_y:
                a = yb[i, pl.ds(R + 8 + k, cy - 16)] * tap
                mid = a if mid is None else mid + a
                if k >= 0:
                    a = yb[i, pl.ds(R + k, 8)] * tap
                    low = a if low is None else low + a
                if k <= 0:
                    a = yb[i, pl.ds(R + cy - 8 + k, 8)] * tap
                    high = a if high is None else high + a
            co[i] = jnp.concatenate([low, mid, high], 0)
        arrive(packs_in)
        wide_slot = lax.div(lanes((cy + 2 * R, cz)), per)
        for side in range(2):
            wide = lax.rem(wide_slot + 1 - side, cx) < cx // 2
            mine = zin[slot, side, 1]
            other = jnp.where(wide, zin[slot, side, 2], zin[slot, side, 0])
            if square:
                mine, other = mine * mine, other * other
            zb[side] = dot(jnp.concatenate([mine, other], 1), edges[int(flip), side])
        pair = []
        for side in range(2):
            total = zero
            for k, tap in taps_y:
                total = total + zb[side, pl.ds(R + k, cy)] * tap
            pair.append(total)
        pair = rim_pair(pair)
        arrive(late)
        for first in (-8, cy):
            along_x(first, True, True, False)
            rows = pl.ds(R + first, 8)
            yb[:, rows] = dot(planes(yb, 0, cx, rows), bands[int(flip)]).reshape(cx, 8, cz)

        def result(i):
            total = co[i] + from_rim(pair, i, R)
            low, high = total[:8], total[cy - 8:]
            for k, tap in taps_y:
                if k < 0:
                    low = low + yb[i, pl.ds(R + k, 8)] * tap
                if k > 0:
                    high = high + yb[i, pl.ds(R + cy - 8 + k, 8)] * tap
            return jnp.concatenate([low, total[8:cy - 8], high], 0)

        return result

    smeared = smear(wb, 0, True, False, wave_x, wave_z + wave_e, wave_y + wave_xy)
    packs = (zero, zero)
    for i in range(cx):
        coarse = smeared(i)
        value = wave_ref[i]
        dens = value * value
        both = coarse * coarse
        source = 0.5 * dens * both - dens * coarse
        corr_ref[i] = (0.5 / 3.0) * both * coarse - 0.5 * both
        sb[R + i, pl.ds(R, cy)] = source
        packs = pack_one(i, source, packs)
    pack_out(1, packs)
    start(src_e + src_z + src_x + src_y + src_xy)

    def z_rim_of(low, high):
        cell_of = lax.rem(lanes(low.shape), per)
        made = [jnp.zeros_like(low), jnp.zeros_like(low)]
        for k in range(1, H + 1):
            made[0] = made[0] + gains[k] * jnp.where(cell_of < k, turn(low, k), 0.0)
            made[1] = made[1] + gains[k] * jnp.where(cell_of >= per - k, turn(high, cz - k), 0.0)
        return rim_pair(made)

    def z_rim(slot, place=1, rows=pl.ds(R, cy)):
        return z_rim_of(*[zin[slot, side, place, rows] for side in range(2)])

    def y_own(buf, p):
        up = down = None
        for k in range(1, H + 1):
            a = gains[k] * buf[p, pl.ds(R + k, cy - 8)]
            b = gains[k] * buf[p, pl.ds(R + 8 - k, cy - 8)]
            up, down = (a, b) if up is None else (up + a, down + b)
        return jnp.concatenate([up[:8], up[8:] + down[:cy - 16], down[cy - 16:]], 0)

    def y_halo(buf, p, total):
        low, high = total[:8], total[cy - 8:]
        for k in range(1, H + 1):
            low = low + gains[k] * buf[p, pl.ds(R - k, 8)]
            high = high + gains[k] * buf[p, pl.ds(R + cy - 8 + k, 8)]
        return jnp.concatenate([low, total[8:cy - 8], high], 0)

    def advance(buf, reach, weight, pair, put):
        own = pl.ds(R, cy)
        step = 2 * GROUP
        for g in range(0, cx, step):
            along = dot(planes(buf, reach + g, step, own), bands[2])
            for i in range(g, g + step):
                total = buf[reach + i, own] * weight(i) + along[(i - g) * cy:(i - g + 1) * cy]
                for k in range(1, H + 1):
                    pairs = [buf[reach + j, own] for j in (i - k, i + k) if pair is not None or 0 <= j < cx]
                    if pair is not None:
                        pairs += [buf[reach + i, pl.ds(R + j, cy)] for j in (-k, k)]
                    both = pairs[0]
                    for p in pairs[1:]:
                        both = both + p
                    total = total + gains[k] * both
                put(i, total + (y_own(buf, reach + i) if pair is None else from_rim(pair, i, H)))

    def keep_part(i, value):
        part[i] = value

    middle = 1.0 + STEP * 0.5 * 3.0 * LAP_COEF[0]
    advance(wb, R, lambda i: middle, z_rim(0), keep_part)
    smeared = smear(sb, 1, False, True, src_x, src_z + src_e, src_y + src_xy)
    get_ext.wait()
    psi_packs = va_packs = (zero, zero)
    for i in range(cx):
        corr = corr_ref[i] + smeared(i)
        corr_ref[i] = corr
        felt = STEP * (corr + ext_ref[i])
        weight = middle - felt
        va[i] = weight
        value = part[i] - felt * wave_ref[i]
        pb[R + i, pl.ds(R, cy)] = value
        psi_packs = pack_one(i, value, psi_packs)
        va_packs = pack_one(i, weight, va_packs)
        half = pl.ds(H * (i % 2), H)
        ypack[0, i // 2, half] = weight[:H]
        ypack[1, i // 2, half] = weight[cy - H:]
    pack_out(2, psi_packs)
    pack_out(3, va_packs)
    start(psi_moves)
    advance(pb, R, lambda i: va[i], None, keep_part)
    own = pl.ds(R, cy)
    inside = {(0, 0): ix > 0, (0, 1): ix < nx - 1, (1, 0): iy > 0, (1, 1): iy < ny - 1, (2, 0): iz > 0, (2, 1): iz < nz - 1}

    def kept(dim, side, value):
        return jnp.where(inside[dim, side], value, 0.0)

    def star(p, first, rows):
        total = None
        for k in range(1, H + 1):
            pairs = pb[R + p - k, pl.ds(first, rows)] + pb[R + p + k, pl.ds(first, rows)]
            pairs += pb[R + p, pl.ds(first - k, rows)] + pb[R + p, pl.ds(first + k, rows)]
            total = gains[k] * pairs if total is None else total + gains[k] * pairs
        return total

    arrive(psi_z)
    rim = []
    cell = lax.rem(at, per)
    for side in range(2):
        far = zin[2, side, 1, own]
        plane_at = lax.rem(slot_of + 1 - side, cx)
        mine = turn(pack[2, side], per if side else cz - per)
        total = far * zin[3, side, 1, own]
        for k in range(1, H + 1):
            ahead = turn(jnp.where(plane_at < k, zin[2, side, 2, own], far), cz - per * k)
            behind = turn(jnp.where(plane_at >= cx - k, zin[2, side, 0, own], far), per * k)
            up, down = turn(far, cz - k), turn(far, k)
            if side:
                down = jnp.where(cell >= k, down, turn(mine, cz - per + k))
            else:
                up = jnp.where(cell < per - k, up, turn(mine, per - k))
            pairs = ahead + behind + up + down
            pairs += zin[2, side, 1, pl.ds(R - k, cy)] + zin[2, side, 1, pl.ds(R + k, cy)]
            total = total + gains[k] * pairs
        rim.append(kept(2, side, total))
    arrive(psi_x)
    pair = z_rim(2)
    for i in range(cx):
        total = part[i] + from_rim(pair, i, H)
        for k in range(1, H + 1):
            for j in (i - k, i + k):
                if not 0 <= j < cx:
                    total = total + gains[k] * pb[R + j, own]
        part[i] = total
    for side in range(2):
        pair = z_rim(2, 2 * side)
        begin = cx if side else -H
        along = dot(planes(pb, R + begin, H, own), bands[2])
        for n in range(H):
            p = begin + n
            total = pb[R + p, own] * vx[side, n] + along[n * cy:(n + 1) * cy]
            for k in range(1, H + 1):
                total = total + gains[k] * (pb[R + p - k, own] + pb[R + p + k, own])
            px[side, n] = total + y_own(pb, R + p) + from_rim(pair, p % cx, H)
    arrive(psi_y)
    for side in range(2):
        first = R + cy - H if side else R - H
        pair = z_rim(2, 1, pl.ds(first, 2 * H))
        centers = [pb[R + i, pl.ds(first, 2 * H)] for i in range(cx)]
        along = dot(jnp.concatenate(centers, 0), bands[2])
        for i in range(cx):
            weight = yin[side, i // 2]
            if i % 2 != side:
                weight = pltpu.roll(weight, H, 0)
            total = centers[i] * weight + along[i * 2 * H:(i + 1) * 2 * H] + star(i, first, 2 * H)
            total = kept(1, side, total + from_rim(pair, i, H))
            if side:
                psi[H + i, pl.ds(R + cy, H)] = total[H:]
            else:
                psi[H + i, pl.ds(R - H, H)] = total[:H]
    for side in range(2):
        begin = cx if side else -H
        for n in range(H):
            psi[H + begin + n, own] = kept(0, side, y_halo(pb, R + begin + n, px[side, n]))
    for i in range(cx):
        psi[H + i, own] = y_halo(pb, R + i, part[i])
    totals = [zero]

    def finish_cell(i, value):
        out_ref[i] = value
        totals[0] = totals[0] + value * value

    advance(psi, H, lambda i: va[i], z_rim_of(*rim), finish_cell)
    total = totals[0]
    partial = jnp.sum(total, axis=0, keepdims=True)
    def all_sum(value, slots, ssem, rsem, me, n, ids):
        if n == 1:
            return value
        slots[me] = value

        def copy_of(d, slot):
            return pltpu.make_async_remote_copy(
                src_ref=slots.at[me], dst_ref=slots.at[slot], send_sem=ssem.at[d], recv_sem=rsem.at[slot],
                device_id=ids(d)[1], device_id_type=MESH)

        def go(d, c):
            copy_of(d, me).start()
            return c

        def come(d, c):
            copy_of(d, ids(d)[0]).wait_recv()
            return c

        def left(d, c):
            copy_of(d, me).wait_send()
            return c

        lax.fori_loop(1, n, go, 0)
        lax.fori_loop(1, n, come, 0)
        total = jnp.sum(slots[...], axis=0)
        lax.fori_loop(1, n, left, 0)
        return total

    if near:
        sums[0] = partial
        for d in range(1, everyone):
            pltpu.make_async_remote_copy(
                src_ref=sums.at[0], dst_ref=sums.at[d], send_sem=send2.at[0, 0], recv_sem=recv2.at[0, 0],
                device_id=others[d - 1], device_id_type=pl.DeviceIdType.LOGICAL).start()
        rest = sums.at[pl.ds(1, everyone - 1)]
        whole = pltpu.make_async_remote_copy(
            src_ref=rest, dst_ref=rest, send_sem=send2.at[0, 0], recv_sem=recv2.at[0, 0],
            device_id=others[0], device_id_type=pl.DeviceIdType.LOGICAL)
        whole.wait_recv()
        partial = jnp.sum(sums[...], axis=0)
    else:
        partial = all_sum(partial, sums, send2.at[0], recv2.at[0], here, plane, plane_id)
        partial = all_sum(partial, sums2, send2.at[1], recv2.at[1], iy, ny, line_id)
    cells = float(cx * cy * cz * nx * ny * nz)
    scale_ref[...] = lax.rsqrt(jnp.broadcast_to(jnp.sum(partial, axis=1, keepdims=True), scale_ref.shape) / cells + 1e-06)
    for way, (rows, to) in sent_rows.items():
        left = bytes_of(rows, send.at[way], recv.at[0, 0]).wait_send
        if to is None:
            left()
        else:
            pl.when(to)(left)
    if near:
        whole.wait_send()


def finish(psi_ref, corr_ref, scale_ref, out_hbm, corr_hbm, scaled, sems):
    copies = [pltpu.make_async_copy(corr_ref, corr_hbm, sems.at[0])]
    copies[0].start()
    cx, cy, cz = psi_ref.shape
    scale = scale_ref[0:1]
    steps = 2 if cx % 2 == 0 else 1
    for n in range(steps):
        some = pl.ds(n * (cx // steps), cx // steps)
        scaled[some] = psi_ref[some] * scale.reshape(1, 1, cz)
        copies.append(pltpu.make_async_copy(scaled.at[some], out_hbm.at[some], sems.at[1 + n]))
        copies[-1].start()
    for copy in copies:
        copy.wait()


def shards(sizes, wave, external, weights):
    cx, cy, cz = wave.shape
    nx, ny, nz = sizes
    f32 = jnp.float32
    near = nx <= 4 and ny <= 4 and nz <= 2
    spare_rows = max(2 * (R + H) * cy, 2 * cx * (R + H), 2 * cx * R + 4 * R * R, 6 * cy + 12 * R, 2 * (6 * cy + 12 * R) + 8 * cy + 4 * R, (3 * R + H) * cy, 3 * cx * R + cx * H)
    summed = nx * ny * nz if near else nx * nz
    stages, most = (1, 1) if near else (2, max(summed, ny))
    vmem = pl.BlockSpec(memory_space=pltpu.VMEM)
    stay = pl.BlockSpec(memory_space=pltpu.HBM)
    psi, corr, scale = pl.pallas_call(
        functools.partial(kernel, sizes),
        out_shape=(jax.ShapeDtypeStruct(wave.shape, f32), jax.ShapeDtypeStruct(wave.shape, f32),
                   jax.ShapeDtypeStruct((8, cz), f32)),
        in_specs=[stay, stay, stay],
        out_specs=(vmem, vmem, vmem),
        scratch_shapes=[
            pltpu.VMEM((cx + 2 * R, cy + 2 * R, cz), f32),
            pltpu.VMEM((cx + 2 * R, cy + 2 * R, cz), f32),
            pltpu.VMEM((cx, cy + 2 * R, cz), f32),
            pltpu.VMEM((cx, cy, cz), f32),
            pltpu.VMEM((cx + 2 * R, cy + 2 * R, cz), f32),
            pltpu.VMEM((cx + 2 * H, cy + 2 * R, cz), f32),
            pltpu.VMEM((cx, cy, cz), f32),
            pltpu.VMEM((cx, cy, cz), f32),
            pltpu.VMEM((4, 2, cy, cz), f32),
            pltpu.VMEM((4, 2, 3, cy + 2 * R, cz), f32),
            pltpu.VMEM((2, cy + 2 * R, cz), f32),
            pltpu.VMEM((2, H, cy, cz), f32),
            pltpu.VMEM((2, H, cy, cz), f32),
            pltpu.VMEM((2, cx // 2, 2 * H, cz), f32),
            pltpu.VMEM((2, cx // 2, 2 * H, cz), f32),
            pltpu.VMEM((3, 2 * cz, 2 * cz), jnp.bfloat16),
            pltpu.VMEM((2, 2, 4 * cz, 2 * cz), jnp.bfloat16),
            pltpu.VMEM((cy, cz), f32),
            pltpu.VMEM((2 * (6 * cy + 12 * R) + 8 * cy + 4 * R, cz), f32),
            pltpu.VMEM((spare_rows, cz), f32),
            pltpu.VMEM((cx, cy, cz), f32),
            pltpu.SMEM(weights.shape, f32),
            pltpu.VMEM((summed, 1, cz), f32),
            pltpu.VMEM((ny, 1, cz), f32),
            pltpu.SemaphoreType.DMA((len(FLAT) + 1,)),
            pltpu.SemaphoreType.DMA((2, len(FLAT) + 2)),
            pltpu.SemaphoreType.DMA((stages, most)),
            pltpu.SemaphoreType.DMA((stages, most)),
            pltpu.SemaphoreType.DMA((3,)),
        ],
        compiler_params=pltpu.CompilerParams(collective_id=0, has_side_effects=True,
                                             vmem_limit_bytes=48 * 1024 * 1024),
    )(*[pltpu.with_memory_space_constraint(x, pltpu.HBM) for x in (weights, wave, external)])
    return pl.pallas_call(
        finish,
        out_shape=(jax.ShapeDtypeStruct(wave.shape, f32), jax.ShapeDtypeStruct(wave.shape, f32)),
        in_specs=[vmem, vmem, vmem],
        out_specs=(stay, stay),
        scratch_shapes=[pltpu.VMEM((cx, cy, cz), f32), pltpu.SemaphoreType.DMA((3,))],
    )(*[pltpu.with_memory_space_constraint(x, pltpu.VMEM) for x in (psi, corr, scale)])


def solution(mesh):
    sizes = tuple(mesh.shape[a] for a in AXES)
    spec = P(*AXES)
    return jax.shard_map(
        functools.partial(shards, sizes),
        mesh=mesh,
        in_specs=(spec, spec, P()),
        out_specs=(spec, spec),
        check_vma=False,
    )
```
